32 devices in a mesh: dp: 16 (over z, y, x), fsdp: 2 (over core).
Axes of the slice: x: 2, y: 2, z: 4, core: 2. Of those that a mesh axis runs over, the one named last changes fastest.
Arguments:
- tokens: bfloat16 [16384, 768], P(('dp', 'fsdp')), may hold values from -6 to 6
- segments: int32 [16384], P(('dp', 'fsdp')), may hold values from -1 to 15, as said below
- mask_flags: int32 [16384], P(('dp', 'fsdp')), may hold values from 0 to 1, as said below
- targets: int32 [16384], P(('dp', 'fsdp')), may hold values from 0 to 50175
- cotangent: bfloat16 [16384, 768], P(('dp', 'fsdp')), may hold values from -6 to 6
- qkv_weight: bfloat16 [768, 2304], P(('dp', 'fsdp')), may hold values from -0.21875 to 0.21875
- attn_bias: bfloat16 [1536], P(('dp', 'fsdp')), may hold values from -4 to 4
- out_weight: bfloat16 [768, 768], P(('dp', 'fsdp')), may hold values from -0.875 to 0.875
- out_bias: bfloat16 [768], P(('dp', 'fsdp')), may hold values from -4 to 4
- attn_gain: bfloat16 [768], P(('dp', 'fsdp')), may hold values from 0.25 to 1.75
- attn_shift: bfloat16 [768], P(('dp', 'fsdp')), may hold values from -4 to 4
- up_weight: bfloat16 [768, 3072], P(('dp', 'fsdp')), may hold values from -0.21875 to 0.21875
- up_bias: bfloat16 [3072], P(('dp', 'fsdp')), may hold values from -4 to 4
- down_weight: bfloat16 [3072, 768], P(('dp', 'fsdp')), may hold values from -0.15625 to 0.15625
- down_bias: bfloat16 [768], P(('dp', 'fsdp')), may hold values from -4 to 4
- ffn_gain: bfloat16 [768], P(('dp', 'fsdp')), may hold values from 0.25 to 1.75
- ffn_shift: bfloat16 [768], P(('dp', 'fsdp')), may hold values from -4 to 4
- dense_weight: bfloat16 [768, 768], P(('dp', 'fsdp')), may hold values from -0.21875 to 0.21875
- dense_bias: bfloat16 [768], P(('dp', 'fsdp')), may hold values from -4 to 4
- head_gain: bfloat16 [768], P(('dp', 'fsdp')), may hold values from 0.25 to 1.75
- head_shift: bfloat16 [768], P(('dp', 'fsdp')), may hold values from -4 to 4
- decoder: bfloat16 [50176, 768], P(('dp', 'fsdp')), may hold values from -0.4375 to 0.4375
- vocab_bias: bfloat16 [50176], P(('dp', 'fsdp')), may hold values from 0.5 to 2.5
Outputs:
- output: bfloat16 [16384, 768], P(('dp', 'fsdp'))
- mean_loss: float32 [], replicated
- tokens_grad: float32 [16384, 768], P(('dp', 'fsdp'))
- qkv_weight_grad: float32 [768, 2304], P(('dp', 'fsdp'))
- attn_bias_grad: float32 [1536], P(('dp', 'fsdp'))
- out_weight_grad: float32 [768, 768], P(('dp', 'fsdp'))
- out_bias_grad: float32 [768], P(('dp', 'fsdp'))
- attn_gain_grad: float32 [768], P(('dp', 'fsdp'))
- attn_shift_grad: float32 [768], P(('dp', 'fsdp'))
- up_weight_grad: float32 [768, 3072], P(('dp', 'fsdp'))
- up_bias_grad: float32 [3072], P(('dp', 'fsdp'))
- down_weight_grad: float32 [3072, 768], P(('dp', 'fsdp'))
- down_bias_grad: float32 [768], P(('dp', 'fsdp'))
- ffn_gain_grad: float32 [768], P(('dp', 'fsdp'))
- ffn_shift_grad: float32 [768], P(('dp', 'fsdp'))
- dense_weight_grad: float32 [768, 768], P(('dp', 'fsdp'))
- dense_bias_grad: float32 [768], P(('dp', 'fsdp'))
- head_gain_grad: float32 [768], P(('dp', 'fsdp'))
- head_shift_grad: float32 [768], P(('dp', 'fsdp'))
- decoder_grad: float32 [50176, 768], P(('dp', 'fsdp'))
- vocab_bias_grad: float32 [50176], P(('dp', 'fsdp'))
The draws below stay inside these ranges and needn't reach their ends.
Inputs may be any that keep to these rules, and one draw needn't show every extreme that they name: `segments`: the rows of one device are one pack of 512 positions. Within a pack ids start at 0 and rise by one at each new sequence; every sequence has 32 to 512 positions; positions after the pack's last sequence, fewer than 32, hold -1. The first pack is one sequence of 512 positions; the second pack is 16 sequences of 32 positions. `mask_flags`: flags fall only on positions whose segment is not -1. The devices that share one fsdp index hold exactly 1024 flags together; each device holds at most 128, and in every draw a device of each fsdp index holds exactly 128.
All inputs are finite; a program needn't handle non-finite values.
Results may differ from the reference program's by a relative error of at most 0.014.
Values may be sent and summed in bfloat16 or wider, within the bound.
No kernel may reach another device: no remote copies, remote signals or barrier semaphores. Data moves between devices by JAX's collectives and lax.ppermute only.
A program may use at most 576 MiB of HBM per device.

```python
import jax
import jax.numpy as jnp
from jax import lax

D = 768
HEADS = 12
HEAD_DIM = 64
FF = 3072
VOCAB = 50176
TOK_DEV = 512
MIN_LEN = 32
MASK_DEV = 64
MAXM = 128
TOKENS = 16384
N_FSDP = 2


def pack_layout(key):
    block_count = TOKENS // TOK_DEV
    candidates = TOK_DEV // MIN_LEN
    levels = candidates.bit_length() - 1
    base_key = jax.random.fold_in(key, 11)
    first_key, second_key, third_key = jax.random.split(base_key, 3)
    grid_shape = (block_count, candidates)
    octave = jnp.minimum(jax.random.randint(first_key, grid_shape, 0, levels + 1), jax.random.randint(second_key, grid_shape, 0, levels + 1))
    base_length = jnp.left_shift(jnp.full(grid_shape, MIN_LEN, jnp.int32), octave)
    jitter = jax.random.randint(third_key, grid_shape, 0, 1 << 30) % base_length
    length = jnp.minimum(base_length + jitter, TOK_DEV)
    length = length.at[0, 0].set(TOK_DEV)
    length = length.at[1, :].set(MIN_LEN)
    seq_ends = jnp.cumsum(length, axis=1)
    seq_starts = seq_ends - length
    usable = seq_starts <= TOK_DEV - MIN_LEN
    live_end = jnp.max(jnp.where(usable, jnp.minimum(seq_ends, TOK_DEV), 0), axis=1)
    position = jnp.arange(TOK_DEV, dtype=jnp.int32)
    earlier = jnp.sum((seq_ends[:, None, :] <= position[None, :, None]).astype(jnp.int32), axis=2)
    return jnp.where(position[None, :] < live_end[:, None], earlier, -1).astype(jnp.int32)


def draw_segments(key, part):
    return pack_layout(key).reshape(TOKENS)


def draw_mask_flags(key, part):
    segment_table = pack_layout(key)
    block_count = TOKENS // TOK_DEV
    lane_count = N_FSDP
    groups = block_count // lane_count
    counts = jnp.full((lane_count, groups), MASK_DEV, jnp.int32)
    counts = counts.at[:, 0].add(MAXM - MASK_DEV).at[:, 1].add(MASK_DEV - MAXM)
    lane_index = jnp.arange(lane_count)[:, None]
    pair_count = (groups - 1) // 2
    move_key = jax.random.fold_in(key, 23)
    for round_index in range(3):
        order_key, step_key, move_key = jax.random.split(move_key, 3)
        shuffled = jax.vmap(lambda one_key: jax.random.permutation(one_key, groups - 1))(jax.random.split(order_key, lane_count)) + 1
        givers = shuffled[:, :pair_count]
        takers = shuffled[:, pair_count:2 * pair_count]
        giver_count = jnp.take_along_axis(counts, givers, axis=1)
        taker_count = jnp.take_along_axis(counts, takers, axis=1)
        lowest = jnp.maximum(-giver_count, taker_count - MAXM)
        highest = jnp.minimum(MAXM - giver_count, taker_count)
        moved = lowest + jax.random.randint(step_key, lowest.shape, 0, 1 << 30) % (highest - lowest + 1)
        counts = counts.at[lane_index, givers].add(moved).at[lane_index, takers].add(-moved)
    per_block = counts.T.reshape(block_count)
    position = jnp.arange(TOK_DEV, dtype=jnp.int32)
    noise = jax.random.randint(jax.random.fold_in(key, 29), (block_count, TOK_DEV), 0, 1 << 20)
    priority = jnp.where(segment_table >= 0, noise * TOK_DEV + position[None, :], (1 << 30) + position[None, :])
    ranking = jnp.argsort(jnp.argsort(priority, axis=1), axis=1)
    return (ranking < per_block[:, None]).astype(jnp.int32).reshape(TOKENS)


def touch_ends(entries, stream_key, low, largest):
    longest = entries.shape.index(max(entries.shape))
    spots = []
    for shift in (0, 1):
        where = [jax.random.randint(jax.random.fold_in(stream_key, axis), (), 0, length) for axis, length in enumerate(entries.shape)]
        where[longest] = (where[longest] + shift) % entries.shape[longest]
        spots.append(tuple(where))
    return entries.at[spots[0]].set(low).at[spots[1]].set(largest)


def block_levels(rng, extent, cuts, low, top_value):
    loudness = 1.0
    for dim, blocks in cuts:
        heights = jax.random.uniform(jax.random.fold_in(jax.random.fold_in(rng, 6), dim), (blocks,), jnp.float32, low / len(cuts), top_value / len(cuts))
        loudness = loudness * jnp.repeat(jnp.exp(heights), extent[dim] // blocks).reshape((-1,) + (1,) * (len(extent) - 1 - dim))
    return loudness


def normal_values(own_key, extent, scale, bound, cuts=(), kind=jnp.bfloat16):
    array = scale * jax.random.normal(own_key, extent, jnp.float32)
    if cuts:
        array = array * block_levels(own_key, extent, cuts, -0.22, 0.18)
    return jnp.clip(array, -bound, bound).astype(kind)


def setup_inputs(seed: int = 0) -> dict:
    keys = jax.random.split(jax.random.key(seed), 24)
    return {
        "tokens": normal_values(keys[0], (TOKENS, D), 1.0, 6.0, ((0, 32),)),
        "segments": draw_segments(jax.random.fold_in(keys[23], 71), 0),
        "mask_flags": draw_mask_flags(jax.random.fold_in(keys[23], 71), 0),
        "targets": touch_ends(jax.random.randint(keys[3], (TOKENS,), 0, VOCAB), jax.random.fold_in(keys[3], 1), 0, VOCAB - 1).astype(jnp.int32),
        "cotangent": normal_values(keys[4], (TOKENS, D), 1.0, 6.0, ((0, 32),)),
        "qkv_weight": normal_values(keys[5], (D, 3 * D), D ** -0.5, 0.21875, ((0, 32),)),
        "attn_bias": normal_values(keys[6], (2 * D,), 0.3, 4.0, ((0, 32),)),
        "out_weight": normal_values(keys[7], (D, D), (D // 16) ** -0.5, 0.875, ((0, 32),)),
        "out_bias": normal_values(keys[8], (D,), 0.3, 4.0, ((0, 32),)),
        "attn_gain": jnp.clip(1.0 + 0.15 * jax.random.normal(keys[9], (D,), jnp.float32), 0.25, 1.75).astype(jnp.bfloat16),
        "attn_shift": normal_values(keys[10], (D,), 0.3, 4.0, ((0, 32),)),
        "up_weight": normal_values(keys[11], (D, FF), D ** -0.5, 0.21875, ((0, 32),)),
        "up_bias": normal_values(keys[12], (FF,), 0.3, 4.0, ((0, 32),)),
        "down_weight": normal_values(keys[13], (FF, D), (FF // 2) ** -0.5, 0.15625, ((0, 32),)),
        "down_bias": normal_values(keys[14], (D,), 0.3, 4.0, ((0, 32),)),
        "ffn_gain": jnp.clip(1.0 + 0.15 * jax.random.normal(keys[15], (D,), jnp.float32), 0.25, 1.75).astype(jnp.bfloat16),
        "ffn_shift": normal_values(keys[16], (D,), 0.3, 4.0, ((0, 32),)),
        "dense_weight": normal_values(keys[17], (D, D), D ** -0.5, 0.21875, ((0, 32),)),
        "dense_bias": normal_values(keys[18], (D,), 0.3, 4.0, ((0, 32),)),
        "head_gain": jnp.clip(1.0 + 0.15 * jax.random.normal(keys[19], (D,), jnp.float32), 0.25, 1.75).astype(jnp.bfloat16),
        "head_shift": normal_values(keys[20], (D,), 0.3, 4.0, ((0, 32),)),
        "decoder": normal_values(keys[21], (VOCAB, D), (D // 4) ** -0.5, 0.4375, ((0, 32),)),
        "vocab_bias": jnp.clip(0.5 + 2.0 * jax.random.uniform(keys[22], (VOCAB,), jnp.float32) ** block_levels(keys[22], (VOCAB,), ((0, 32),), -0.2, 0.2), 0.5, 2.5).astype(jnp.bfloat16),
    }


@jax.custom_vjp
def low(v):
    return lax.optimization_barrier(v.astype(jnp.bfloat16)).astype(jnp.float32)

@jax.custom_vjp
def low_back(v):
    return v

def low_keep(v):
    return (low(v), None)

def low_pass(kept, grad):
    return (grad,)

def back_keep(v):
    return (v, None)

def back_low(kept, grad):
    return (low(grad),)
low.defvjp(low_keep, low_pass)
low_back.defvjp(back_keep, back_low)
EPSILON = 1e-05
HIGHEST = lax.Precision.HIGHEST

def matmul(left_side, right_side):
    return jnp.dot(left_side, right_side, precision=HIGHEST, preferred_element_type=jnp.float32)

def layer_norm(values, gain_vector, shift_vector):
    center = values - lax.optimization_barrier(jnp.mean(values, axis=-1, keepdims=True))
    spread = lax.optimization_barrier(jnp.mean(center * center, axis=-1, keepdims=True))
    return center * lax.rsqrt(spread + EPSILON) * gain_vector + shift_vector

def gelu_exact(values):
    return jax.nn.gelu(values, approximate=False)

def attend_pack(pieces):
    queries, keys_in, values_in, segment_row = pieces
    scores = jnp.einsum('qhd,khd->hqk', queries, keys_in, precision=HIGHEST) * HEAD_DIM ** (-0.5)
    scores = low_back(scores)
    same_doc = segment_row[:, None] == segment_row[None, :]
    scores = jnp.where(same_doc[None], scores, -1e+30)
    softmax = low(jax.nn.softmax(scores, axis=-1))
    return jnp.einsum('hqk,khd->qhd', softmax, values_in, precision=HIGHEST)

def reference(tokens, segments, mask_flags, targets, cotangent, qkv_weight, attn_bias, out_weight, out_bias, attn_gain, attn_shift, up_weight, up_bias, down_weight, down_bias, ffn_gain, ffn_shift, dense_weight, dense_bias, head_gain, head_shift, decoder, vocab_bias):
    pack_count = TOKENS // TOK_DEV
    picked_count = MASK_DEV * pack_count
    positions = jnp.nonzero(mask_flags, size=picked_count)[0].astype(jnp.int32)
    labels = targets[positions].astype(jnp.int32)
    floats = tuple((item.astype(jnp.float32) for item in (tokens, qkv_weight, attn_bias, out_weight, out_bias, attn_gain, attn_shift, up_weight, up_bias, down_weight, down_bias, ffn_gain, ffn_shift, dense_weight, dense_bias, head_gain, head_shift, decoder, vocab_bias)))

    def forward(tokens, qkv_weight, attn_bias, out_weight, out_bias, attn_gain, attn_shift, up_weight, up_bias, down_weight, down_bias, ffn_gain, ffn_shift, dense_weight, dense_bias, head_gain, head_shift, decoder, vocab_bias):
        projected = matmul(tokens, qkv_weight)
        queries = low(low_back(projected[:, :D] + attn_bias[:D]))
        keys_in = low(low_back(projected[:, D:2 * D]))
        values_in = low(low_back(projected[:, 2 * D:] + attn_bias[D:]))
        shaped = (pack_count, TOK_DEV, HEADS, HEAD_DIM)
        context = lax.map(jax.checkpoint(attend_pack), (queries.reshape(shaped), keys_in.reshape(shaped), values_in.reshape(shaped), segments.reshape(pack_count, TOK_DEV)))
        context = low(low_back(context.reshape(TOKENS, D)))
        attn_branch = low_back(matmul(context, out_weight) + out_bias)
        hidden = low(layer_norm(tokens + attn_branch, attn_gain, attn_shift))
        pre_act = low_back(matmul(hidden, up_weight) + up_bias)
        active = low(gelu_exact(pre_act))
        ffn_branch = low_back(matmul(active, down_weight) + down_bias)
        output = low(layer_norm(hidden + ffn_branch, ffn_gain, ffn_shift))
        picked = low_back(output[positions])

        def head_block(pieces):
            rows_block, labels_block = pieces
            dense = low_back(matmul(rows_block, dense_weight) + dense_bias)
            normed = low(layer_norm(gelu_exact(dense), head_gain, head_shift))
            logits = lax.dot_general(normed, decoder, (((1,), (1,)), ((), ())), precision=HIGHEST, preferred_element_type=jnp.float32)
            logits = low_back(logits + vocab_bias)
            totals = jax.scipy.special.logsumexp(logits, axis=1)
            chosen = jnp.take_along_axis(logits, labels_block[:, None], axis=1)[:, 0]
            return jnp.sum(totals - chosen)
        block_sums = lax.map(jax.checkpoint(head_block), (picked.reshape(pack_count, MASK_DEV, D), labels.reshape(pack_count, MASK_DEV)))
        return (output, jnp.sum(block_sums))
    (output, loss_sum), pullback = jax.vjp(forward, *floats)
    grads = pullback((cotangent.astype(jnp.float32), jnp.ones_like(loss_sum)))
    return (output.astype(jnp.bfloat16), loss_sum / picked_count, grads[0], grads[1], grads[2], grads[3], grads[4], grads[5], grads[6], grads[7], grads[8], grads[9], grads[10], grads[11], grads[12], grads[13], grads[14], grads[15], grads[16], grads[17], grads[18])
```

```python
import jax
import jax.numpy as jnp
from jax import lax
from jax.sharding import PartitionSpec as P

HEADS = 12
HEAD_DIM = 64
MASK_DEV = 64
MAXM = 128

EPSILON = 1e-05
NEGATIVE = -1e30
AXES = ("dp", "fsdp")


def to_low(values):
    return values.astype(jnp.bfloat16)


def to_full(values):
    return values.astype(jnp.float32)


def layer_norm(values, gain_vector, shift_vector):
    center = values - jnp.mean(values, axis=-1, keepdims=True)
    spread = jnp.mean(center * center, axis=-1, keepdims=True)
    return center * lax.rsqrt(spread + EPSILON) * gain_vector + shift_vector


def gelu_exact(values):
    return jax.nn.gelu(values, approximate=False)


def head_tail(dense_out, gain_vector, shift_vector):
    return layer_norm(gelu_exact(dense_out), gain_vector, shift_vector)


def matmul(left_side, right_side):
    return jnp.dot(left_side, right_side, preferred_element_type=jnp.float32)


def matmul_tn(left_side, right_side):
    return lax.dot_general(
        left_side, right_side, (((0,), (0,)), ((), ())), preferred_element_type=jnp.float32
    )


def matmul_nt(left_side, right_side):
    return lax.dot_general(
        left_side, right_side, (((1,), (1,)), ((), ())), preferred_element_type=jnp.float32
    )


def attention_forward(tokens, segments, params):
    qkv_weight, attn_bias, out_weight, out_bias, attn_gain, attn_shift = params
    row_count, model_width = tokens.shape
    shaped = (row_count, HEADS, HEAD_DIM)
    score_scale = HEAD_DIM ** (-0.5)
    bias_full = to_full(attn_bias)
    queries = to_low(matmul(tokens, qkv_weight[0]) + bias_full[:model_width]).reshape(shaped)
    keys_low = to_low(matmul(tokens, qkv_weight[1])).reshape(shaped)
    values_low = to_low(matmul(tokens, qkv_weight[2]) + bias_full[model_width:]).reshape(shaped)
    scores = (
        jnp.einsum("qhd,khd->hqk", queries, keys_low, preferred_element_type=jnp.float32)
        * score_scale
    )
    same_doc = segments[:, None] == segments[None, :]
    scores = jnp.where(same_doc[None], scores, NEGATIVE)
    row_peak = jnp.max(scores, axis=-1, keepdims=True)
    exponent = jnp.exp(scores - row_peak)
    softmax = exponent / jnp.sum(exponent, axis=-1, keepdims=True)
    softmax_low = to_low(softmax)
    context = to_low(
        jnp.einsum(
            "hqk,khd->qhd", softmax_low, values_low, preferred_element_type=jnp.float32
        ).reshape(row_count, model_width)
    )
    summed = to_full(tokens) + matmul(context, out_weight) + to_full(out_bias)
    hidden = to_low(layer_norm(summed, to_full(attn_gain), to_full(attn_shift)))
    return (hidden, (queries, keys_low, values_low, softmax, softmax_low, context, summed))


def attention_backward(tokens, params, saved, hidden_grad):
    qkv_weight, attn_bias, out_weight, out_bias, attn_gain, attn_shift = params
    row_count, model_width = tokens.shape
    shaped = (row_count, HEADS, HEAD_DIM)
    score_scale = HEAD_DIM ** (-0.5)
    queries, keys_low, values_low, softmax, softmax_low, context, summed = saved
    _, norm_back = jax.vjp(layer_norm, summed, to_full(attn_gain), to_full(attn_shift))
    summed_grad, gain_grad, shift_grad = norm_back(hidden_grad)
    branch_grad = to_low(summed_grad)
    out_bias_grad = jnp.sum(to_full(branch_grad), axis=0)
    out_weight_grad = matmul_tn(context, branch_grad)
    context_grad = to_low(matmul_nt(branch_grad, out_weight)).reshape(shaped)
    softmax_grad = jnp.einsum(
        "qhd,khd->hqk", context_grad, values_low, preferred_element_type=jnp.float32
    )
    value_grad = jnp.einsum(
        "hqk,qhd->khd", softmax_low, context_grad, preferred_element_type=jnp.float32
    )
    score_grad = to_low(
        softmax * (softmax_grad - jnp.sum(softmax * softmax_grad, axis=-1, keepdims=True))
    )
    query_grad = (
        jnp.einsum("hqk,khd->qhd", score_grad, keys_low, preferred_element_type=jnp.float32)
        * score_scale
    )
    key_grad = (
        jnp.einsum("hqk,qhd->khd", score_grad, queries, preferred_element_type=jnp.float32)
        * score_scale
    )
    parts = [
        to_low(part.reshape(row_count, model_width)) for part in (query_grad, key_grad, value_grad)
    ]
    qkv_grad = [matmul_tn(tokens, part) for part in parts]
    bias_grad = jnp.concatenate(
        [jnp.sum(to_full(parts[0]), axis=0), jnp.sum(to_full(parts[2]), axis=0)]
    )
    tokens_grad = summed_grad
    for part, weight in zip(parts, qkv_weight):
        tokens_grad = tokens_grad + matmul_nt(part, weight)
    return (
        tokens_grad,
        (qkv_grad, bias_grad, out_weight_grad, out_bias_grad, gain_grad, shift_grad),
    )


def ffn_forward(hidden, params):
    up_weight, up_bias, down_weight, down_bias, ffn_gain, ffn_shift = params
    pre_act = matmul(hidden, up_weight) + to_full(up_bias)
    active = to_low(gelu_exact(pre_act))
    summed = to_full(hidden) + matmul(active, down_weight) + to_full(down_bias)
    result = to_low(layer_norm(summed, to_full(ffn_gain), to_full(ffn_shift)))
    return (result, (pre_act, active, summed))


def ffn_backward(hidden, params, saved, result_grad):
    up_weight, up_bias, down_weight, down_bias, ffn_gain, ffn_shift = params
    pre_act, active, summed = saved
    _, norm_back = jax.vjp(layer_norm, summed, to_full(ffn_gain), to_full(ffn_shift))
    summed_grad, gain_grad, shift_grad = norm_back(result_grad)
    branch_grad = to_low(summed_grad)
    down_bias_grad = jnp.sum(to_full(branch_grad), axis=0)
    down_weight_grad = matmul_tn(active, branch_grad)
    active_grad = matmul_nt(branch_grad, down_weight)
    _, gelu_back = jax.vjp(gelu_exact, pre_act)
    pre_grad = to_low(gelu_back(active_grad)[0])
    up_bias_grad = jnp.sum(to_full(pre_grad), axis=0)
    up_weight_grad = matmul_tn(hidden, pre_grad)
    hidden_grad = summed_grad + matmul_nt(pre_grad, up_weight)
    return (
        hidden_grad,
        (up_weight_grad, up_bias_grad, down_weight_grad, down_bias_grad, gain_grad, shift_grad),
    )


def column_blocks(matrix, width):
    return [matrix[:, k : k + width] for k in range(0, matrix.shape[1], width)]


def butterfly(value, join, count):
    index = 1
    while index < count:
        pairs = [(device, device ^ index) for device in range(count)]
        value = join(value, lax.ppermute(value, AXES, pairs))
        index *= 2
    return value


def pack_small(parts, count, width):
    flat = jnp.concatenate([part.reshape(count, -1) for part in parts], axis=1)
    flat = jnp.pad(flat, ((0, 0), (0, width - flat.shape[1])))
    return jnp.pad(flat[:, None, :], ((0, 0), (0, 7), (0, 0)))


def per_device(
    tokens,
    segments,
    mask_flags,
    targets,
    cotangent,
    qkv_weight,
    attn_bias,
    out_weight,
    out_bias,
    attn_gain,
    attn_shift,
    up_weight,
    up_bias,
    down_weight,
    down_bias,
    ffn_gain,
    ffn_shift,
    dense_weight,
    dense_bias,
    head_gain,
    head_shift,
    decoder,
    vocab_bias,
):
    count = lax.axis_size(AXES)
    width = tokens.shape[1]
    small = (
        attn_bias,
        out_bias,
        attn_gain,
        attn_shift,
        up_bias,
        down_bias,
        ffn_gain,
        ffn_shift,
        dense_bias,
        head_gain,
        head_shift,
    )
    qkv_blocks = column_blocks(qkv_weight, width)
    up_blocks = column_blocks(up_weight, width)
    matrices = [*qkv_blocks, out_weight, *up_blocks, down_weight, dense_weight]
    packed = jnp.concatenate([*matrices, pack_small(small, 1, width)[0]], axis=0)
    gathered = lax.all_gather(packed, AXES, axis=0)
    full = []
    offset = 0
    for matrix in matrices:
        rows = matrix.shape[0]
        full.append(gathered[:, offset : offset + rows].reshape(count * rows, width))
        offset += rows
    small_full = []
    start = 0
    for vector in small:
        share = vector.shape[0]
        small_full.append(gathered[:, offset, start : start + share].reshape(count * share))
        start += share
    blocks = len(qkv_blocks)
    qkv_full = full[:blocks]
    out_full = full[blocks]
    up_full = jnp.concatenate(full[blocks + 1 : blocks + 1 + len(up_blocks)], axis=1)
    down_full, dense_full = full[-2:]
    attn_params = (qkv_full, small_full[0], out_full, *small_full[1:4])
    ffn_params = (up_full, small_full[4], down_full, *small_full[5:8])
    dense_bias_full, head_gain_full, head_shift_full = small_full[8:]

    hidden, attn_saved = attention_forward(tokens, segments, attn_params)
    output, ffn_saved = ffn_forward(hidden, ffn_params)
    flagged = mask_flags > 0
    mask_rank = jnp.cumsum(mask_flags) - 1
    slot_place = jnp.where(flagged, mask_rank, -1)
    picker = jnp.arange(MAXM)[:, None] == slot_place[None, :]
    picker_low = picker.astype(jnp.bfloat16)
    own_rows = to_low(matmul(picker_low, output))
    own_labels = jnp.where(
        jnp.any(picker, axis=1), jnp.sum(jnp.where(picker, targets[None, :], 0), axis=1), -1
    )
    dense = matmul(own_rows, dense_full) + to_full(dense_bias_full)
    normed, tail_back = jax.vjp(head_tail, dense, to_full(head_gain_full), to_full(head_shift_full))
    normed_low = to_low(normed)
    shifted = own_labels + 1
    label_rows = jnp.stack([shifted // 256, shifted % 256]).astype(jnp.bfloat16)
    label_rows = jnp.pad(label_rows, ((0, 6), (0, width - MAXM)))
    rows_gathered = lax.all_gather(jnp.concatenate([normed_low, label_rows]), AXES, axis=0)
    all_rows = rows_gathered[:, :MAXM].reshape(count * MAXM, width)
    label_parts = rows_gathered[:, MAXM : MAXM + 2, :MAXM].astype(jnp.int32)
    all_labels = (label_parts[:, 0] * 256 + label_parts[:, 1] - 1).reshape(count * MAXM)
    slice_index = lax.axis_index(AXES)
    vocab_rows = decoder.shape[0]
    logits = matmul_nt(all_rows, decoder) + to_full(vocab_bias)
    row_peak = jnp.max(logits, axis=1)
    exp_sums = jnp.sum(jnp.exp(logits - row_peak[:, None]), axis=1)
    local_label = all_labels - slice_index * vocab_rows
    row_valid = all_labels >= 0
    label_hit = (jnp.arange(vocab_rows)[None, :] == local_label[:, None]) & row_valid[:, None]
    label_sum = jnp.sum(jnp.where(label_hit, logits, 0.0))
    local_total = (row_peak + jnp.log(exp_sums)).reshape(count, MAXM)
    stats = jnp.concatenate(
        [local_total, jnp.pad(label_sum[None, None], ((0, 7), (0, MAXM - 1)))], axis=0
    )

    def join(first, second):
        merged = jnp.maximum(first, second) + jnp.log1p(jnp.exp(-jnp.abs(first - second)))
        is_total = jnp.arange(first.shape[0])[:, None] < count
        return jnp.where(is_total, merged, first + second)

    stats = butterfly(stats, join, count)
    log_total = stats[:count].reshape(count * MAXM)
    row_weight = row_valid.astype(jnp.float32)
    mean_loss = (jnp.sum(row_weight * log_total) - stats[count, 0]) / (MASK_DEV * count)
    logit_grad = to_low(
        row_weight[:, None] * (jnp.exp(logits - log_total[:, None]) - label_hit.astype(jnp.float32))
    )
    rows_part = to_low(matmul(logit_grad, decoder))
    normed_grad = to_full(lax.psum_scatter(rows_part, AXES, scatter_dimension=0, tiled=True))
    decoder_grad = matmul_tn(logit_grad, all_rows)
    vocab_bias_grad = jnp.sum(to_full(logit_grad), axis=0)
    dense_grad, head_gain_grad, head_shift_grad = tail_back(normed_grad)
    dense_grad_low = to_low(dense_grad)
    dense_weight_grad = matmul_tn(own_rows, dense_grad_low)
    dense_bias_grad = jnp.sum(to_full(dense_grad_low), axis=0)
    picked_grad = to_low(matmul_nt(dense_grad_low, dense_full))
    token_grad = matmul_tn(picker_low, picked_grad)
    output_grad = to_full(cotangent) + token_grad
    hidden_grad, ffn_terms = ffn_backward(hidden, ffn_params, ffn_saved, output_grad)
    tokens_grad, attn_terms = attention_backward(tokens, attn_params, attn_saved, hidden_grad)

    small_grads = (
        *(attn_terms[k] for k in (1, 3, 4, 5)),
        *(ffn_terms[k] for k in (1, 3, 4, 5)),
        dense_bias_grad,
        head_gain_grad,
        head_shift_grad,
    )
    grad_matrices = [
        *attn_terms[0],
        attn_terms[2],
        *column_blocks(ffn_terms[0], width),
        ffn_terms[2],
        dense_weight_grad,
    ]
    grads_packed = jnp.concatenate(
        [to_low(matrix).reshape(count, -1, width) for matrix in grad_matrices]
        + [to_low(pack_small(small_grads, count, width))],
        axis=1,
    )
    grads = to_full(lax.psum_scatter(grads_packed, AXES, scatter_dimension=0, tiled=True)[0])
    pieces = []
    offset = 0
    for matrix in matrices:
        pieces.append(grads[offset : offset + matrix.shape[0]])
        offset += matrix.shape[0]
    small_pieces = []
    start = 0
    for vector in small:
        small_pieces.append(grads[offset, start : start + vector.shape[0]])
        start += vector.shape[0]
    return (
        output,
        mean_loss,
        tokens_grad,
        jnp.concatenate(pieces[:blocks], axis=1),
        small_pieces[0],
        pieces[blocks],
        *small_pieces[1:4],
        jnp.concatenate(pieces[blocks + 1 : blocks + 1 + len(up_blocks)], axis=1),
        small_pieces[4],
        pieces[-2],
        *small_pieces[5:8],
        pieces[-1],
        *small_pieces[8:],
        decoder_grad,
        vocab_bias_grad,
    )


def solution(mesh):
    matrix_spec = P(AXES, None)
    vector_spec = P(AXES)
    m, v = matrix_spec, vector_spec
    return jax.shard_map(
        per_device,
        mesh=mesh,
        in_specs=(m, v, v, v, m, m, v, m, v, v, v, m, v, m, v, v, v, m, v, v, v, m, v),
        out_specs=(m, P(), m, m, v, m, v, v, v, m, v, m, v, v, v, m, v, v, v, m, v),
        check_vma=False,
    )
```

```python
import functools

import jax
import jax.numpy as jnp
from jax import lax
from jax.experimental import pallas as pl
from jax.experimental.pallas import tpu as pltpu
from jax.sharding import PartitionSpec as P

HEADS = 12
HEAD_DIM = 64
MASK_DEV = 64
MAXM = 128

EPSILON = 1e-05
NEGATIVE = -1e30
AXES = ("dp", "fsdp")


def to_low(values):
    return values.astype(jnp.bfloat16)


def to_full(values):
    return values.astype(jnp.float32)


def layer_norm(values, gain_vector, shift_vector):
    center = values - jnp.mean(values, axis=-1, keepdims=True)
    spread = jnp.mean(center * center, axis=-1, keepdims=True)
    return center * lax.rsqrt(spread + EPSILON) * gain_vector + shift_vector


def gelu_exact(values):
    return jax.nn.gelu(values, approximate=False)


def head_tail(dense_out, gain_vector, shift_vector):
    return layer_norm(gelu_exact(dense_out), gain_vector, shift_vector)


def matmul(left_side, right_side):
    return jnp.dot(left_side, right_side, preferred_element_type=jnp.float32)


def matmul_tn(left_side, right_side):
    return lax.dot_general(
        left_side, right_side, (((0,), (0,)), ((), ())), preferred_element_type=jnp.float32
    )


def matmul_nt(left_side, right_side):
    return lax.dot_general(
        left_side, right_side, (((1,), (1,)), ((), ())), preferred_element_type=jnp.float32
    )


def attention_forward(tokens, segments, params):
    qkv_weight, attn_bias, out_weight, out_bias, attn_gain, attn_shift = params
    row_count, model_width = tokens.shape
    shaped = (row_count, HEADS, HEAD_DIM)
    score_scale = HEAD_DIM ** (-0.5)
    bias_full = to_full(attn_bias)
    queries = to_low(matmul(tokens, qkv_weight[0]) + bias_full[:model_width]).reshape(shaped)
    keys_low = to_low(matmul(tokens, qkv_weight[1])).reshape(shaped)
    values_low = to_low(matmul(tokens, qkv_weight[2]) + bias_full[model_width:]).reshape(shaped)
    scores = (
        jnp.einsum("qhd,khd->hqk", queries, keys_low, preferred_element_type=jnp.float32)
        * score_scale
    )
    same_doc = segments[:, None] == segments[None, :]
    scores = jnp.where(same_doc[None], scores, NEGATIVE)
    row_peak = jnp.max(scores, axis=-1, keepdims=True)
    exponent = jnp.exp(scores - row_peak)
    softmax = exponent / jnp.sum(exponent, axis=-1, keepdims=True)
    softmax_low = to_low(softmax)
    context = to_low(
        jnp.einsum(
            "hqk,khd->qhd", softmax_low, values_low, preferred_element_type=jnp.float32
        ).reshape(row_count, model_width)
    )
    summed = to_full(tokens) + matmul(context, out_weight) + to_full(out_bias)
    hidden = to_low(layer_norm(summed, to_full(attn_gain), to_full(attn_shift)))
    return (hidden, (queries, keys_low, values_low, softmax, softmax_low, context, summed))


def ffn_forward(hidden, params):
    up_weight, up_bias, down_weight, down_bias, ffn_gain, ffn_shift = params
    pre_act = matmul(hidden, up_weight) + to_full(up_bias)
    active = to_low(gelu_exact(pre_act))
    summed = to_full(hidden) + matmul(active, down_weight) + to_full(down_bias)
    result = to_low(layer_norm(summed, to_full(ffn_gain), to_full(ffn_shift)))
    return (result, (pre_act, active, summed))


def column_blocks(matrix, width):
    return [matrix[:, k : k + width] for k in range(0, matrix.shape[1], width)]


def take(value, axis, index):
    return lax.dynamic_index_in_dim(value, index, axis, keepdims=False)


def add_low(first, second):
    return to_low(to_full(first) + to_full(second))


def halve(value, axis, stride):
    chips = lax.axis_size("dp")
    bit = (lax.axis_index("dp") // stride) % 2
    pairs = [(chip, chip ^ stride) for chip in range(chips)]
    arrived = lax.ppermute(take(value, axis, 1 - bit), "dp", pairs)
    return add_low(take(value, axis, bit), arrived)


def core_halves(value, chips):
    split = value.reshape(chips, 2, -1, value.shape[-1])
    core = lax.axis_index("fsdp")
    return take(split, 1, 1 - core), take(split, 1, core)


def core_stage(matrices):
    chips = lax.axis_size("dp")
    halves = [core_halves(matrix, chips) for matrix in matrices]
    away = jnp.concatenate([half[0] for half in halves], axis=1)
    kept = jnp.concatenate([half[1] for half in halves], axis=1)
    return core_swap(away, kept)


def core_swap(away, kept):
    return add_low(kept, lax.ppermute(away, "fsdp", [(0, 1), (1, 0)]))


def first_plane_stage(value):
    rows, width = value.shape[1:]
    value = value.reshape(-1, 2, 2, rows, width)
    return halve(value[..., : width // 2], 2, 1), halve(value[..., width // 2 :], 1, 2)


def second_plane_stage(value):
    left, right = value
    return jnp.concatenate([halve(left, 1, 2), halve(right, 1, 1)], axis=-1)


def level_stage(value):
    levels, rows, width = value.shape
    return halve(value.reshape(2, levels // 2, rows, width), 0, 2 * levels)


def level_stages(value):
    while value.shape[0] > 1:
        value = level_stage(value)
    return to_full(value[0])


def level_exchange(value):
    levels = value.shape[0]
    groups = [[place + 4 * level for level in range(levels)] for place in range(4)]
    value = lax.all_to_all(value, "dp", 0, 0, axis_index_groups=groups, tiled=True)
    return jnp.sum(to_full(value), axis=0)


def tie(value, *others):
    return lax.optimization_barrier((value, *others))


def window_base(start, total, window):
    return pl.multiple_of(jnp.minimum((start // 16) * 16, total - window), 16)


def compact_kernel(places, counts, gathered_ref, out_ref, picked_ref, *, window, slots):
    step = pl.program_id(0)

    @pl.when(step == 0)
    def _():
        out_ref[...] = jnp.zeros_like(out_ref)
        picked_ref[...] = jnp.zeros_like(picked_ref)

    batch = gathered_ref.shape[0]
    total = out_ref.shape[0]
    for lane in range(batch):
        source = step * batch + lane
        start = places[source]
        base = window_base(start, total, window)
        row = lax.broadcasted_iota(jnp.int32, (window, slots), 0) + (base - start)
        column = lax.broadcasted_iota(jnp.int32, (window, slots), 1)
        chosen = jnp.where((row == column) & (column < counts[source]), 1.0, 0.0)
        chosen = chosen.astype(jnp.bfloat16)
        span = pl.ds(base, window)
        moved = jnp.dot(chosen, gathered_ref[lane, :slots, :], preferred_element_type=jnp.float32)
        out_ref[span, :] += moved.astype(jnp.bfloat16)
        picked_ref[span, :] += lax.dot_general(
            chosen,
            gathered_ref[lane, slots:, :slots],
            (((1,), (1,)), ((), ())),
            preferred_element_type=jnp.float32,
        )


def compact(places, counts, gathered, slots, total):
    sources, depth, width = gathered.shape
    batch = 4
    return pl.pallas_call(
        functools.partial(compact_kernel, window=slots + 16, slots=slots),
        grid_spec=pltpu.PrefetchScalarGridSpec(
            num_scalar_prefetch=2,
            grid=(sources // batch,),
            in_specs=[pl.BlockSpec((batch, depth, width), lambda i, p, c: (i, 0, 0))],
            out_specs=[
                pl.BlockSpec((total, width), lambda i, p, c: (0, 0)),
                pl.BlockSpec((total, depth - slots), lambda i, p, c: (0, 0)),
            ],
        ),
        out_shape=[
            jax.ShapeDtypeStruct((total, width), jnp.bfloat16),
            jax.ShapeDtypeStruct((total, depth - slots), jnp.float32),
        ],
        compiler_params=pltpu.CompilerParams(dimension_semantics=("arbitrary",)),
        name="compact_rows",
    )(places, counts, gathered)


def spread_kernel(places, counts, rows_ref, *out_refs, window):
    step = pl.program_id(0)
    total = rows_ref.shape[0]
    batch, slots = out_refs[0].shape[:2]
    for side, out_ref in enumerate(out_refs):
        for lane in range(batch):
            chip = step * batch + lane
            start = places[side, chip]
            base = window_base(start, total, window)
            row = lax.broadcasted_iota(jnp.int32, (slots, window), 0)
            column = lax.broadcasted_iota(jnp.int32, (slots, window), 1) + (base - start)
            chosen = jnp.where((row == column) & (row < counts[side, chip]), 1.0, 0.0)
            chosen = chosen.astype(jnp.bfloat16)
            moved = jnp.dot(
                chosen, rows_ref[pl.ds(base, window), :], preferred_element_type=jnp.float32
            )
            out_ref[lane] = moved.astype(jnp.bfloat16)


def spread(places, counts, rows, slots):
    sides, chips = places.shape
    total, width = rows.shape
    batch = 2
    block = pl.BlockSpec((batch, slots, width), lambda i, p, c: (i, 0, 0))
    return pl.pallas_call(
        functools.partial(spread_kernel, window=slots + 16),
        grid_spec=pltpu.PrefetchScalarGridSpec(
            num_scalar_prefetch=2,
            grid=(chips // batch,),
            in_specs=[
                pl.BlockSpec(
                    (total, width), lambda i, p, c: (0, 0), pipeline_mode=pl.Buffered(1)
                )
            ],
            out_specs=[block] * sides,
        ),
        out_shape=[jax.ShapeDtypeStruct((chips, slots, width), jnp.bfloat16)] * sides,
        compiler_params=pltpu.CompilerParams(dimension_semantics=("arbitrary",)),
        name="spread_rows",
    )(places, counts, rows)


def butterfly(value, join, count):
    index = 1
    while index < count:
        pairs = [(device, device ^ index) for device in range(count)]
        value = join(value, lax.ppermute(value, AXES, pairs))
        index *= 2
    return value


def pack_small(parts, count, width):
    flat = jnp.concatenate([part.reshape(count, -1) for part in parts], axis=1)
    flat = jnp.pad(flat, ((0, 0), (0, width - flat.shape[1])))
    return jnp.pad(flat[:, None, :], ((0, 0), (0, 7), (0, 0)))


def per_device(
    tokens,
    segments,
    mask_flags,
    targets,
    cotangent,
    qkv_weight,
    attn_bias,
    out_weight,
    out_bias,
    attn_gain,
    attn_shift,
    up_weight,
    up_bias,
    down_weight,
    down_bias,
    ffn_gain,
    ffn_shift,
    dense_weight,
    dense_bias,
    head_gain,
    head_shift,
    decoder,
    vocab_bias,
):
    count = lax.axis_size(AXES)
    width = tokens.shape[1]
    small = (
        attn_bias,
        out_bias,
        attn_gain,
        attn_shift,
        up_bias,
        down_bias,
        ffn_gain,
        ffn_shift,
        dense_bias,
        head_gain,
        head_shift,
    )
    qkv_blocks = column_blocks(qkv_weight, width)
    up_blocks = column_blocks(up_weight, width)
    matrices = [*qkv_blocks, out_weight, *up_blocks, down_weight, dense_weight]
    packed = jnp.concatenate([*matrices, pack_small(small, 1, width)[0]], axis=0)
    gathered = lax.all_gather(packed, AXES, axis=0)
    full = []
    offset = 0
    for matrix in matrices:
        rows = matrix.shape[0]
        full.append(gathered[:, offset : offset + rows].reshape(count * rows, width))
        offset += rows
    small_full = []
    start = 0
    for vector in small:
        share = vector.shape[0]
        small_full.append(gathered[:, offset, start : start + share].reshape(count * share))
        start += share
    blocks = len(qkv_blocks)
    qkv_full = full[:blocks]
    out_full = full[blocks]
    up_full = jnp.concatenate(full[blocks + 1 : blocks + 1 + len(up_blocks)], axis=1)
    down_full, dense_full = full[-2:]
    attn_params = (qkv_full, small_full[0], out_full, *small_full[1:4])
    ffn_params = (up_full, small_full[4], down_full, *small_full[5:8])
    dense_bias_full, head_gain_full, head_shift_full = small_full[8:]

    hidden, attn_saved = attention_forward(tokens, segments, attn_params)
    output, ffn_saved = ffn_forward(hidden, ffn_params)
    flagged = mask_flags > 0
    mask_rank = jnp.cumsum(mask_flags) - 1
    slot_place = jnp.where(flagged, mask_rank, -1)
    picker = jnp.arange(MAXM)[:, None] == slot_place[None, :]
    picker_low = picker.astype(jnp.bfloat16)
    own_rows = to_low(matmul(picker_low, output))
    own_labels = jnp.where(
        jnp.any(picker, axis=1), jnp.sum(jnp.where(picker, targets[None, :], 0), axis=1), -1
    )
    dense = matmul(own_rows, dense_full) + to_full(dense_bias_full)
    normed, tail_back = jax.vjp(head_tail, dense, to_full(head_gain_full), to_full(head_shift_full))
    normed_low = to_low(normed)
    shifted = own_labels + 1
    label_rows = jnp.stack([shifted // 256, shifted % 256]).astype(jnp.bfloat16)
    label_rows = jnp.pad(label_rows, ((0, 6), (0, width - MAXM)))
    rows_gathered = lax.all_gather(jnp.concatenate([normed_low, label_rows]), AXES, axis=0)
    chips = count // 2
    label_parts = rows_gathered[:, MAXM : MAXM + 2, :MAXM].astype(jnp.float32)
    counts = jnp.sum((label_parts[:, 0] + label_parts[:, 1] > 0).astype(jnp.int32), axis=1)
    by_core = counts.reshape(chips, 2)
    group = MASK_DEV * chips
    places = jnp.cumsum(by_core, axis=0) - by_core + jnp.arange(2)[None, :] * group
    total = 2 * group
    all_rows, picked_labels = compact(places.reshape(count), counts, rows_gathered, MAXM, total)
    parts = picked_labels[:, :2].astype(jnp.int32)
    all_labels = parts[:, 0] * 256 + parts[:, 1] - 1
    slice_index = lax.axis_index(AXES)
    vocab_rows = decoder.shape[0]
    logits = matmul_nt(all_rows, decoder) + to_full(vocab_bias)
    row_peak = jnp.max(logits, axis=1)
    exp_sums = jnp.sum(jnp.exp(logits - row_peak[:, None]), axis=1)
    local_label = all_labels - slice_index * vocab_rows
    label_hit = jnp.arange(vocab_rows)[None, :] == local_label[:, None]
    label_sum = jnp.sum(jnp.where(label_hit, logits, 0.0))
    local_total = (row_peak + jnp.log(exp_sums)).reshape(-1, 128)
    lines = local_total.shape[0]
    stats = jnp.concatenate(
        [local_total, jnp.pad(label_sum[None, None], ((0, 7), (0, 127)))], axis=0
    )

    def join(first, second):
        merged = jnp.maximum(first, second) + jnp.log1p(jnp.exp(-jnp.abs(first - second)))
        is_total = jnp.arange(first.shape[0])[:, None] < lines
        return jnp.where(is_total, merged, first + second)

    stats = butterfly(stats, join, count)
    log_total = stats[:lines].reshape(total)
    mean_loss = (jnp.sum(log_total) - stats[lines, 0]) / total
    logit_grad = to_low(
        jnp.exp(logits - log_total[:, None]) - label_hit.astype(jnp.float32)
    )
    rows_part = to_low(matmul(logit_grad, decoder))
    core = lax.axis_index("fsdp")
    sides = jnp.stack([1 - core, core])
    away, kept = spread(places.T[sides], by_core.T[sides], rows_part, MAXM)
    value = first_plane_stage(core_swap(away, kept))
    normed_grad = level_exchange(second_plane_stage(value))
    vocab_bias_grad = jnp.sum(to_full(logit_grad), axis=0)
    dense_grad, head_gain_grad, head_shift_grad = tail_back(normed_grad)
    dense_grad_low = to_low(dense_grad)
    dense_weight_grad = matmul_tn(own_rows, dense_grad_low)
    dense_bias_grad = jnp.sum(to_full(dense_grad_low), axis=0)
    picked_grad = to_low(matmul_nt(dense_grad_low, dense_full))
    token_grad = matmul_tn(picker_low, picked_grad)
    output_grad = to_full(cotangent) + token_grad
    pre_act, active, summed2 = ffn_saved
    up_full, up_bias_full, down_full, _, ffn_gain_full, ffn_shift_full = ffn_params
    _, norm_back = jax.vjp(layer_norm, summed2, to_full(ffn_gain_full), to_full(ffn_shift_full))
    summed2_grad, ffn_gain_grad, ffn_shift_grad = norm_back(output_grad)
    branch2_grad = to_low(summed2_grad)
    down_bias_grad = jnp.sum(to_full(branch2_grad), axis=0)
    down_grad = to_low(matmul_tn(active, branch2_grad))
    first = core_stage([down_grad, to_low(dense_weight_grad)])
    active_grad = matmul_nt(branch2_grad, down_full)
    _, gelu_back = jax.vjp(gelu_exact, pre_act)
    pre_grad = to_low(gelu_back(active_grad)[0])
    up_bias_grad = jnp.sum(to_full(pre_grad), axis=0)
    up_grad = to_low(matmul_tn(hidden, pre_grad))
    hidden_grad = summed2_grad + matmul_nt(pre_grad, up_full)
    hidden_grad, up_grad, first = tie(hidden_grad, up_grad, first)

    queries, keys_low, values_low, softmax, softmax_low, context, summed1 = attn_saved
    row_count = tokens.shape[0]
    shaped = (row_count, HEADS, HEAD_DIM)
    score_scale = HEAD_DIM ** (-0.5)
    _, norm_back = jax.vjp(
        layer_norm, summed1, to_full(attn_params[4]), to_full(attn_params[5])
    )
    summed1_grad, attn_gain_grad, attn_shift_grad = norm_back(hidden_grad)
    branch1_grad = to_low(summed1_grad)
    out_bias_grad = jnp.sum(to_full(branch1_grad), axis=0)
    out_grad = to_low(matmul_tn(context, branch1_grad))
    context_grad = to_low(matmul_nt(branch1_grad, out_full))
    first = first_plane_stage(first)
    second = core_stage([*column_blocks(up_grad, width), out_grad])
    context_grad = context_grad.reshape(shaped)
    softmax_grad = jnp.einsum(
        "qhd,khd->hqk", context_grad, values_low, preferred_element_type=jnp.float32
    )
    row_dot = jnp.sum(softmax * softmax_grad, axis=-1, keepdims=True)
    row_dot, second, *first = tie(row_dot, second, *first)
    score_grad = to_low(softmax * (softmax_grad - row_dot))
    first = second_plane_stage(first)
    second = first_plane_stage(second)
    value_grad = jnp.einsum(
        "hqk,qhd->khd", softmax_low, context_grad, preferred_element_type=jnp.float32
    )
    score_grad, first = tie(score_grad, first)
    query_grad = (
        jnp.einsum("hqk,khd->qhd", score_grad, keys_low, preferred_element_type=jnp.float32)
        * score_scale
    )
    key_grad = (
        jnp.einsum("hqk,qhd->khd", score_grad, queries, preferred_element_type=jnp.float32)
        * score_scale
    )
    mixed = [to_low(part.reshape(row_count, width)) for part in (query_grad, key_grad, value_grad)]
    bias_grad = jnp.concatenate(
        [jnp.sum(to_full(mixed[0]), axis=0), jnp.sum(to_full(mixed[2]), axis=0)]
    )
    qkv_grads = [to_low(matmul_tn(tokens, part)) for part in mixed]
    small_grads = (
        bias_grad,
        out_bias_grad,
        attn_gain_grad,
        attn_shift_grad,
        up_bias_grad,
        down_bias_grad,
        ffn_gain_grad,
        ffn_shift_grad,
        dense_bias_grad,
        head_gain_grad,
        head_shift_grad,
    )
    first = level_stage(first) if first.shape[0] > 1 else first
    third = core_stage([*qkv_grads, to_low(pack_small(small_grads, count, width)).reshape(-1, width)])
    second = second_plane_stage(second)
    mixed[0], second, third = tie(mixed[0], second, third)
    tokens_grad = summed1_grad
    for part, weight in zip(mixed, qkv_full):
        tokens_grad = tokens_grad + matmul_nt(part, weight)
    third = first_plane_stage(third)
    logit_grad, first = tie(logit_grad, first)
    decoder_grad = matmul_tn(logit_grad, all_rows)
    first = level_stages(first)
    third = second_plane_stage(third)
    second = level_stages(second)
    third = level_exchange(third)

    def own_pieces(summed, matrices):
        ends = []
        offset = 0
        for matrix in matrices:
            share = matrix.shape[0] // count
            ends.append(summed[offset : offset + share])
            offset += share
        return ends

    down_piece, dense_piece = own_pieces(first, [down_grad, dense_weight_grad])
    *up_pieces, out_piece = own_pieces(second, [*column_blocks(up_grad, width), out_grad])
    *qkv_pieces, small_grad = own_pieces(third, [*qkv_grads, jnp.zeros((count * 8, 1))])
    small_pieces = []
    start = 0
    for vector in small:
        small_pieces.append(small_grad[0, start : start + vector.shape[0]])
        start += vector.shape[0]
    return (
        output,
        mean_loss,
        tokens_grad,
        jnp.concatenate(qkv_pieces, axis=1),
        small_pieces[0],
        out_piece,
        *small_pieces[1:4],
        jnp.concatenate(up_pieces, axis=1),
        small_pieces[4],
        down_piece,
        *small_pieces[5:8],
        dense_piece,
        *small_pieces[8:],
        decoder_grad,
        vocab_bias_grad,
    )


def solution(mesh):
    matrix_spec = P(AXES, None)
    vector_spec = P(AXES)
    m, v = matrix_spec, vector_spec
    return jax.shard_map(
        per_device,
        mesh=mesh,
        in_specs=(m, v, v, v, m, m, v, m, v, v, v, m, v, m, v, v, v, m, v, v, v, m, v),
        out_specs=(m, P(), m, m, v, m, v, v, v, m, v, m, v, v, v, m, v, v, v, m, v),
        check_vma=False,
    )
```

```python
import functools

import jax
import jax.numpy as jnp
from jax import lax
from jax.experimental import pallas as pl
from jax.experimental.pallas import tpu as pltpu
from jax.sharding import PartitionSpec as P

HEADS = 12
HEAD_DIM = 64
MASK_DEV = 64
MAXM = 128

EPSILON = 1e-05
NEGATIVE = -1e30
AXES = ("dp", "fsdp")


def to_low(values):
    return values.astype(jnp.bfloat16)


def to_full(values):
    return values.astype(jnp.float32)


def layer_norm(values, gain_vector, shift_vector):
    center = values - jnp.mean(values, axis=-1, keepdims=True)
    spread = jnp.mean(center * center, axis=-1, keepdims=True)
    return center * lax.rsqrt(spread + EPSILON) * gain_vector + shift_vector


def gelu_exact(values):
    return jax.nn.gelu(values, approximate=False)


def head_tail(dense_out, gain_vector, shift_vector):
    return layer_norm(gelu_exact(dense_out), gain_vector, shift_vector)


def matmul(left_side, right_side):
    return jnp.dot(left_side, right_side, preferred_element_type=jnp.float32)


def matmul_tn(left_side, right_side):
    return lax.dot_general(
        left_side, right_side, (((0,), (0,)), ((), ())), preferred_element_type=jnp.float32
    )


def matmul_nt(left_side, right_side):
    return lax.dot_general(
        left_side, right_side, (((1,), (1,)), ((), ())), preferred_element_type=jnp.float32
    )


def column_blocks(matrix, width):
    return [matrix[:, k : k + width] for k in range(0, matrix.shape[1], width)]


def gelu_parts(values):
    size = jnp.abs(values) * 0.7071067811865476
    ratio = 1.0 / (1.0 + 0.3275911 * size)
    bell = jnp.exp(-0.5 * values * values)
    series = 1.421413741 + ratio * (-1.453152027 + ratio * 1.061405429)
    series = ratio * (0.254829592 + ratio * (-0.284496736 + ratio * series))
    tail = 0.5 * series * bell
    below = jnp.where(values < 0, tail, 1.0 - tail)
    return values * below, below + values * bell * 0.3989422804014327


def flat_rows(value):
    return value.reshape(-1, value.shape[-1])


def whole(array):
    return pl.BlockSpec(array.shape, lambda *_: (0,) * array.ndim)


class Weights:
    def __init__(self, arrays, shares):
        self.arrays = arrays
        self.starts = [sum(shares[:k]) for k in range(len(shares))]
        self.shares = shares

    def natural(self, index, core):
        span = slice(self.starts[index], self.starts[index] + self.shares[index])
        pieces = [array[:, span] for array in self.arrays]
        if len(pieces) == 2:
            pieces = [jnp.stack(in_order(*pieces, core), axis=1)]
        return flat_rows(pieces[0].reshape(-1, *pieces[0].shape[-2:]))

    def operands(self, index, core, columns, column_map, parts=1, part_map=lambda *_: 0):
        share, start = self.shares[index], self.starts[index]
        if share % 8 or start % share:
            array = self.natural(index, core)
            rows = array.shape[0] // parts
            spec = pl.BlockSpec((rows, columns), lambda *i: (part_map(*i), column_map(*i)))
            return [array], [spec]
        place = start // share
        specs = [
            pl.BlockSpec(
                (array.shape[0] // parts, share, columns),
                lambda *i: (part_map(*i), place, column_map(*i)),
            )
            for array in self.arrays
        ]
        return list(self.arrays), specs


def up_operands_of(weights, steps):
    share = weights.shares[0]
    width = weights.arrays[0].shape[-1]
    if share % 8:
        array = jnp.concatenate([weights.natural(k, None) for k in range(steps)], axis=1)
        return [array], [pl.BlockSpec((array.shape[0], width), lambda s, *_: (0, s))]
    array = weights.arrays[0]
    return [array], [pl.BlockSpec((array.shape[0], share, width), lambda s, *_: (0, s, 0))]


def in_order(mine, other, core):
    return jnp.where(core == 0, mine, other), jnp.where(core == 0, other, mine)


def read_weight(refs, core):
    if len(refs) == 1:
        return flat_rows(refs[0][...])
    return flat_rows(jnp.stack(in_order(refs[0][...], refs[1][...], core), axis=1))


def pack_kernel(*refs, layout):
    *sources, out_ref = refs
    for source, (column, row, rows, columns) in zip(sources, layout):
        for k in range(column):
            out_ref[row[k] : row[k] + rows, :] = source[:, k * columns : (k + 1) * columns]


def pack_rows(pieces):
    width = pieces[0][0].shape[1] // len(pieces[0][1])
    total = max(row + m.shape[0] for m, rows in pieces for row in rows)
    if any(row % 8 for _, rows in pieces for row in rows):
        placed = sorted(
            (row, m[:, k * width : (k + 1) * width])
            for m, rows in pieces
            for k, row in enumerate(rows)
        )
        return jnp.concatenate([block for _, block in placed], axis=0)
    matrices = [m for m, _ in pieces]
    layout = [(len(rows), tuple(rows), m.shape[0], width) for m, rows in pieces]
    return pl.pallas_call(
        functools.partial(pack_kernel, layout=layout),
        grid=(1,),
        in_specs=[whole(m) for m in matrices],
        out_specs=pl.BlockSpec((total, width), lambda i: (0, 0)),
        out_shape=jax.ShapeDtypeStruct((total, width), matrices[0].dtype),
        name="pack_rows",
    )(*matrices)


def pack_later_kernel(flags_ref, targets_ref, *refs, layout, label_place):
    *sources, out_ref = refs
    pack_kernel(*sources, out_ref, layout=layout)
    count = flags_ref.shape[1]
    flags = jnp.broadcast_to(flags_ref[...], (8, count))
    row = lax.broadcasted_iota(jnp.int32, (count, count), 0)
    column = lax.broadcasted_iota(jnp.int32, (count, count), 1)
    until = to_low(jnp.where(row <= column, 1.0, 0.0))
    rank = matmul(to_low(flags.astype(jnp.float32)), until)[:1] - 1.0
    slot = lax.broadcasted_iota(jnp.int32, (MAXM, count), 0).astype(jnp.float32)
    picker = to_low(jnp.where((slot == rank) & (flags_ref[...] > 0), 1.0, 0.0))
    shifted = targets_ref[...] + 1
    high = lax.shift_right_logical(shifted, 8)
    level = lax.broadcasted_iota(jnp.int32, (8, count), 0)
    halves = jnp.where(level == 0, high, jnp.where(level == 1, shifted - high * 256, 0))
    labels = matmul_nt(to_low(halves.astype(jnp.float32)), picker)
    empty = jnp.zeros((8, out_ref.shape[1] - MAXM), jnp.float32)
    out_ref[label_place : label_place + 8, :] = to_low(jnp.concatenate([labels, empty], axis=1))


def pack_later(pieces, mask_flags, targets):
    width = pieces[0][0].shape[1] // len(pieces[0][1])
    label_place = max(row + m.shape[0] for m, rows in pieces for row in rows)
    if any(row % 8 for _, rows in pieces for row in rows) or label_place % 8:
        rank = jnp.cumsum(mask_flags) - 1
        picker = (jnp.arange(MAXM)[:, None] == rank[None, :]) & (mask_flags > 0)[None, :]
        shifted = jnp.sum(jnp.where(picker, targets[None, :] + 1, 0), axis=1)
        labels = jnp.stack([shifted // 256, shifted % 256]).astype(jnp.bfloat16)
        labels = jnp.pad(labels, ((0, 6), (0, width - MAXM)))
        return pack_rows([*pieces, (labels, [label_place])])
    matrices = [m for m, _ in pieces]
    layout = [(len(rows), tuple(rows), m.shape[0], width) for m, rows in pieces]
    operands = [mask_flags[None], targets[None], *matrices]
    return pl.pallas_call(
        functools.partial(pack_later_kernel, layout=layout, label_place=label_place),
        grid=(1,),
        in_specs=[whole(operand) for operand in operands],
        out_specs=pl.BlockSpec((label_place + 8, width), lambda i: (0, 0)),
        out_shape=jax.ShapeDtypeStruct((label_place + 8, width), matrices[0].dtype),
        name="pack_later",
    )(*operands)


def place_kernel(index, line_ref, out_ref, *, plan):
    rows, width = out_ref.shape
    device = index[0]
    line = jnp.broadcast_to(line_ref[...], (8, width))
    lane = lax.broadcasted_iota(jnp.int32, (rows, width), 1)
    level = lax.broadcasted_iota(jnp.int32, (rows, width), 0)
    out = jnp.zeros((rows, width), jnp.float32)
    for first_row, start, share in plan:
        spot = device * share
        row, place = first_row + spot // width, spot % width
        moved = pltpu.roll(line, lax.rem(place - start + width, width), 1)
        here = (level == row) & (lane >= place) & (lane < place + share)
        out = jnp.where(here, jnp.broadcast_to(moved[:1], (rows, width)), out)
    out_ref[...] = out.astype(out_ref.dtype)


def place_shares(device, vectors, first_rows, rows, width):
    plan = []
    line = 0.0
    start = 0
    for vector, first_row in zip(vectors, first_rows):
        end = start + vector.shape[0]
        plan.append((first_row, start, vector.shape[0]))
        line = line + jnp.pad(to_full(vector), (start, width - end))
        start = end
    line = line[None, :]
    return pl.pallas_call(
        functools.partial(place_kernel, plan=plan),
        grid_spec=pltpu.PrefetchScalarGridSpec(
            num_scalar_prefetch=1,
            grid=(1,),
            in_specs=[whole(line)],
            out_specs=pl.BlockSpec((rows, width), lambda i, d: (0, 0)),
        ),
        out_shape=jax.ShapeDtypeStruct((rows, width), jnp.bfloat16),
        name="place_shares",
    )(device.reshape(1), line)


def double(value, stride, axis):
    chips = lax.axis_size("dp")
    bit = (lax.axis_index("dp") // stride) % 2
    arrived = lax.ppermute(value, "dp", [(chip, chip ^ stride) for chip in range(chips)])
    low, high = in_order(value, arrived, bit)
    return jnp.stack([low, high], axis=axis)


def gather_pair(value, split):
    chips = lax.axis_size("dp")
    stride = 4
    value = value[None]
    while stride < chips:
        value = double(value, stride, 0)
        value = value.reshape(-1, *value.shape[2:])
        stride *= 2
    upper, lower = value[:, :split], value[:, split:]
    upper, lower = double(upper, 1, 1), double(lower, 2, 1)
    upper, lower = double(upper, 2, 1), double(lower, 1, 2)
    upper, lower = (part.reshape(chips, *part.shape[-2:]) for part in (upper, lower))
    swap = [(0, 1), (1, 0)]
    return (upper, lax.ppermute(upper, "fsdp", swap)), (lower, lax.ppermute(lower, "fsdp", swap))


def attention_kernel(core, *refs, sizes):
    ends = [0]
    for size in sizes:
        ends.append(ends[-1] + size)
    weights = [refs[ends[k] : ends[k + 1]] for k in range(len(sizes))]
    (tokens_ref, bias_ref, vector_ref, down_ref, across_ref) = refs[ends[-1] : ends[-1] + 5]
    (q_ref, k_ref, v_ref, context_ref, total_ref, summed_ref, hidden_ref) = refs[ends[-1] + 5 : -2]
    mask_ref, all_ref = refs[-2:]
    step = pl.program_id(0)

    @pl.when(step == 0)
    def _():
        mask_ref[...] = jnp.where(down_ref[...] == across_ref[...], 0.0, NEGATIVE)

    tokens = tokens_ref[...]
    queries = to_low(matmul(tokens, read_weight(weights[0], core[0])) + bias_ref[0:1, :])
    keys = to_low(matmul(tokens, read_weight(weights[1], core[0])))
    values = to_low(matmul(tokens, read_weight(weights[2], core[0])) + bias_ref[1:2, :])
    q_ref[...], k_ref[...], v_ref[...] = queries, keys, values
    heads = queries.shape[1] // HEAD_DIM
    pair_width = 2 * HEAD_DIM
    lane = lax.broadcasted_iota(jnp.int32, (1, pair_width), 1)
    for pair in range(heads // 2):
        span = slice(pair_width * pair, pair_width * (pair + 1))
        scaled = to_full(queries[:, span]) * HEAD_DIM ** (-0.5)
        sides = []
        for side in range(2):
            mine = to_low(jnp.where((lane < HEAD_DIM) == (side == 0), scaled, 0.0))
            scores = matmul_nt(keys[:, span], mine) + mask_ref[...]
            peak = jnp.max(scores, axis=0, keepdims=True)
            exponent = jnp.exp(scores - peak)
            total = jnp.sum(exponent, axis=0, keepdims=True)
            total_ref[pl.ds(step * heads + 2 * pair + side, 1), :] = peak + jnp.log(total)
            softmax_low = to_low(exponent * (1.0 / total))
            mixed = matmul_tn(values[:, span], softmax_low)
            sides.append(mixed[HEAD_DIM * side : HEAD_DIM * (side + 1)])
        context = to_low(jnp.concatenate(sides, axis=0).T)
        context_ref[:, span] = context
        all_ref[step * (heads // 2) + pair] = context

    @pl.when(step == pl.num_programs(0) - 1)
    def _():
        pairs = all_ref.shape[0]
        context = jnp.concatenate([all_ref[k] for k in range(pairs)], axis=1)
        product = matmul(context, read_weight(weights[3], core[0]))
        summed = to_full(tokens_ref[...]) + product + vector_ref[2:3, :]
        summed_ref[...] = summed
        hidden_ref[...] = to_low(layer_norm(summed, vector_ref[3:4, :], vector_ref[4:5, :]))


def attention_forward(core, tokens, segments, weights, vectors):
    rows, width = tokens.shape
    columns = 256
    arrays, specs, sizes = [], [], []
    for k, (group, index) in enumerate(weights):
        size, place = (columns, lambda s, c: s) if k < 3 else (width, lambda s, c: 0)
        some, their = group.operands(index, core, size, place)
        arrays, specs, sizes = arrays + some, specs + their, sizes + [len(some)]
    down, across = segments[:, None], segments[None, :]
    block = pl.BlockSpec((rows, columns), lambda s, c: (0, s))
    head_rows = 16
    return pl.pallas_call(
        functools.partial(attention_kernel, sizes=sizes),
        grid_spec=pltpu.PrefetchScalarGridSpec(
            num_scalar_prefetch=1,
            grid=(width // columns,),
            in_specs=[
                *specs,
                whole(tokens),
                pl.BlockSpec((8, columns), lambda s, c: (0, s)),
                whole(vectors),
                whole(down),
                whole(across),
            ],
            out_specs=[
                block,
                block,
                block,
                block,
                pl.BlockSpec((head_rows, rows), lambda s, c: (0, 0)),
                whole(tokens),
                whole(tokens),
            ],
            scratch_shapes=[
                pltpu.VMEM((rows, rows), jnp.float32),
                pltpu.VMEM((width // (2 * HEAD_DIM), rows, 2 * HEAD_DIM), jnp.bfloat16),
            ],
        ),
        out_shape=[
            *[jax.ShapeDtypeStruct((rows, width), jnp.bfloat16)] * 4,
            jax.ShapeDtypeStruct((head_rows, rows), jnp.float32),
            jax.ShapeDtypeStruct((rows, width), jnp.float32),
            jax.ShapeDtypeStruct((rows, width), jnp.bfloat16),
        ],
        compiler_params=pltpu.CompilerParams(dimension_semantics=("arbitrary",)),
        name="attention_forward",
    )(core.reshape(1), *arrays, tokens, vectors, vectors, down, across)


def ffn_kernel(*refs, sizes):
    up_refs, down_refs = refs[: sizes[0]], refs[sizes[0] : sum(sizes)]
    hidden_ref, bias_ref, vector_ref = refs[sum(sizes) : sum(sizes) + 3]
    active_ref, slope_ref, summed_ref, output_ref, total_ref = refs[sum(sizes) + 3 :]
    step = pl.program_id(0)
    up, down = read_weight(up_refs, None), read_weight(down_refs, None)
    pre_act = matmul(hidden_ref[...], up) + bias_ref[pl.ds(step, 1), :]
    active, slope = gelu_parts(pre_act)
    active = to_low(active)
    active_ref[...] = active
    slope_ref[...] = slope
    part = matmul(active, down)

    @pl.when(step == 0)
    def _():
        total_ref[...] = part

    @pl.when(step > 0)
    def _():
        total_ref[...] += part

    @pl.when(step == pl.num_programs(0) - 1)
    def _():
        summed = to_full(hidden_ref[...]) + total_ref[...] + vector_ref[5:6, :]
        summed_ref[...] = summed
        output_ref[...] = to_low(layer_norm(summed, vector_ref[6:7, :], vector_ref[7:8, :]))


def ffn_forward(hidden, weights, up_bias, vectors):
    rows, width = hidden.shape
    steps = len(weights.shares) - 2
    first, first_specs = up_operands_of(weights, steps)
    second, second_specs = weights.operands(steps, None, width, lambda s: 0, steps, lambda s: s)
    block = pl.BlockSpec((rows, width), lambda s: (0, s))
    return pl.pallas_call(
        functools.partial(ffn_kernel, sizes=[len(first), len(second)]),
        grid=(steps,),
        in_specs=[*first_specs, *second_specs, whole(hidden), whole(up_bias), whole(vectors)],
        out_specs=[block, block, whole(hidden), whole(hidden)],
        out_shape=[
            jax.ShapeDtypeStruct((rows, steps * width), jnp.bfloat16),
            jax.ShapeDtypeStruct((rows, steps * width), jnp.float32),
            jax.ShapeDtypeStruct((rows, width), jnp.float32),
            jax.ShapeDtypeStruct((rows, width), jnp.bfloat16),
        ],
        scratch_shapes=[pltpu.VMEM((rows, width), jnp.float32)],
        compiler_params=pltpu.CompilerParams(dimension_semantics=("arbitrary",)),
        name="ffn_forward",
    )(*first, *second, hidden, up_bias, vectors)


def head_kernel(*refs, size):
    weight_refs = refs[:size]
    picker_ref, output_ref, vector_ref, own_ref, dense_ref, normed_ref = refs[size:]
    own = to_low(matmul(picker_ref[...], output_ref[...]))
    own_ref[...] = own
    dense = matmul(own, read_weight(weight_refs, None)) + vector_ref[4:5, :]
    dense_ref[...] = dense
    active = gelu_parts(dense)[0]
    normed_ref[...] = to_low(layer_norm(active, vector_ref[5:6, :], vector_ref[6:7, :]))


def head_forward(picker, output, group, index, vectors):
    slots, width = picker.shape[0], output.shape[1]
    arrays, specs = group.operands(index, None, width, lambda s: 0)
    operands = [picker, output, vectors]
    out_shape = [
        jax.ShapeDtypeStruct((slots, width), kind)
        for kind in (jnp.bfloat16, jnp.float32, jnp.bfloat16)
    ]
    return pl.pallas_call(
        functools.partial(head_kernel, size=len(arrays)),
        grid=(1,),
        in_specs=[*specs, *[whole(operand) for operand in operands]],
        out_specs=[whole(shape) for shape in out_shape],
        out_shape=out_shape,
        name="head_forward",
    )(*arrays, *operands)


def norm_backward(summed, gain_row, grad):
    center = summed - jnp.mean(summed, axis=-1, keepdims=True)
    scale = lax.rsqrt(jnp.mean(center * center, axis=-1, keepdims=True) + EPSILON)
    unit = center * scale
    inner = grad * gain_row
    mean = jnp.mean(inner, axis=-1, keepdims=True)
    along = jnp.mean(inner * unit, axis=-1, keepdims=True)
    gain_grad = jnp.sum(grad * unit, axis=0, keepdims=True)
    shift_grad = jnp.sum(grad, axis=0, keepdims=True)
    return scale * (inner - mean - unit * along), gain_grad, shift_grad


def feed_back_kernel(place, *refs, sizes, share, down_share):
    up_refs, down_refs = refs[: sizes[0]], refs[sizes[0] : sum(sizes)]
    (cotangent_ref, picker_ref, picked_ref, summed_ref, vector_ref, own_ref, dense_ref) = refs[
        sum(sizes) : sum(sizes) + 7
    ]
    hidden_ref, active_ref, slope_ref, total_ref, sums_ref, *outs = refs[sum(sizes) + 7 : -2]
    low_ref, turned_ref = refs[-2:]
    step = pl.program_id(0)
    width = vector_ref.shape[1]

    @pl.when(step == 0)
    def _():
        grad = to_full(cotangent_ref[...]) + matmul_tn(picker_ref[...], picked_ref[...])
        summed_grad, gain_grad, shift_grad = norm_backward(
            summed_ref[...], vector_ref[6:7, :], grad
        )
        total_ref[...] = summed_grad
        low = to_low(summed_grad)
        low_ref[...] = low
        turned_ref[...] = hidden_ref[...].T
        sums_ref[...] = jnp.zeros_like(sums_ref)
        sums_ref[0:1, :] = jnp.sum(to_full(low), axis=0, keepdims=True)
        sums_ref[1:2, :] = gain_grad
        sums_ref[2:3, :] = shift_grad
        dense_grad = to_low(matmul_tn(own_ref[...], dense_ref[...]))
        if down_share:
            store_blocks(outs, dense_grad, place, share, slice(2 * down_share, None))
        else:
            outs[2][...] = dense_grad

    low = low_ref[...]
    up, down = read_weight(up_refs, None), read_weight(down_refs, None)
    down_grad = to_low(matmul_tn(active_ref[...], low))
    pre_grad = to_low(matmul_nt(low, down) * slope_ref[...])
    total_ref[...] += matmul_nt(pre_grad, up)
    sums_ref[pl.ds(3 + step, 1), :] = jnp.sum(to_full(pre_grad), axis=0, keepdims=True)
    up_grad = to_low(matmul(turned_ref[...], pre_grad))
    if down_share:
        chips = width // (2 * down_share)
        rows = slice(down_share, 2 * down_share)
        store_blocks(outs, down_grad, place, down_share, rows, step * chips)
        rows = pl.ds(pl.multiple_of(step * share, share), share)
        store_blocks(outs, up_grad, place, share, rows)
    else:
        outs[0][...] = up_grad
        outs[1][...] = down_grad


def feed_backward(place, count, cotangent, picker, picked_grad, summed, vectors, own, dense, hidden, active, slope, weights):
    rows, width = cotangent.shape
    steps = active.shape[1] // width
    share, down_share, chips = width // count, active.shape[1] // count, count // 2
    aligned = share % 8 == 0
    first, first_specs = up_operands_of(weights, steps)
    second, second_specs = weights.operands(steps, None, width, lambda s, c: 0, steps, lambda s, c: s)
    operands = [cotangent, picker, picked_grad, summed, vectors, own, dense, hidden]
    block = pl.BlockSpec((rows, width), lambda s, c: (0, s))
    low = jnp.bfloat16
    if aligned:
        shape = jax.ShapeDtypeStruct((chips, 2 * down_share + share, width // 2), low)
        out_shape, out_specs = [shape] * 4, [whole(shape)] * 4
    else:
        out_shape = [
            jax.ShapeDtypeStruct((width, steps * width), low),
            jax.ShapeDtypeStruct((steps * width, width), low),
            jax.ShapeDtypeStruct((width, width), low),
        ]
        out_specs = [
            pl.BlockSpec((width, width), lambda s, c: (0, s)),
            pl.BlockSpec((width, width), lambda s, c: (s, 0)),
            whole(out_shape[2]),
        ]
    common = [
        jax.ShapeDtypeStruct((rows, width), jnp.float32),
        jax.ShapeDtypeStruct((8, width), jnp.float32),
    ]
    kernel = functools.partial(
        feed_back_kernel,
        sizes=[len(first), len(second)],
        share=share,
        down_share=down_share if aligned else 0,
    )
    hidden_grad, sums, *outs = pl.pallas_call(
        kernel,
        grid_spec=pltpu.PrefetchScalarGridSpec(
            num_scalar_prefetch=1,
            grid=(steps,),
            in_specs=[
                *first_specs,
                *second_specs,
                *[whole(operand) for operand in operands],
                block,
                block,
            ],
            out_specs=[*[whole(shape) for shape in common], *out_specs],
            scratch_shapes=[pltpu.VMEM((rows, width), low), pltpu.VMEM((width, rows), low)],
        ),
        out_shape=[*common, *out_shape],
        compiler_params=pltpu.CompilerParams(dimension_semantics=("arbitrary",)),
        name="feed_backward",
    )(place, *first, *second, *operands, active, slope)
    if not aligned:
        away, kept = arranged([*column_blocks(outs[0], width), *outs[1:]], place)
    else:
        away, kept = outs[:2], outs[2:]
    return hidden_grad, sums, away, kept


def out_back_kernel(core, *refs, size):
    weight_refs = refs[:size]
    grad_ref, summed_ref, vector_ref, total_ref, low_ref, back_ref, sums_ref = refs[size:]
    width = vector_ref.shape[1]
    summed_grad, gain_grad, shift_grad = norm_backward(
        summed_ref[...], vector_ref[3:4, :], grad_ref[...]
    )
    total_ref[...] = summed_grad
    low = to_low(summed_grad)
    low_ref[...] = low
    bias_grad = jnp.sum(to_full(low), axis=0, keepdims=True)
    zero = jnp.zeros((5, width), jnp.float32)
    sums_ref[...] = jnp.concatenate([bias_grad, gain_grad, shift_grad, zero], axis=0)
    back_ref[...] = to_low(matmul_nt(low, read_weight(weight_refs, core[0])))


def out_backward(core, hidden_grad, summed, vectors, group, index):
    rows, width = hidden_grad.shape
    arrays, specs = group.operands(index, core, width, lambda s, c: 0)
    operands = [hidden_grad, summed, vectors]
    out_shape = [
        jax.ShapeDtypeStruct((rows, width), jnp.float32),
        jax.ShapeDtypeStruct((rows, width), jnp.bfloat16),
        jax.ShapeDtypeStruct((rows, width), jnp.bfloat16),
        jax.ShapeDtypeStruct((8, width), jnp.float32),
    ]
    return pl.pallas_call(
        functools.partial(out_back_kernel, size=len(arrays)),
        grid_spec=pltpu.PrefetchScalarGridSpec(
            num_scalar_prefetch=1,
            grid=(1,),
            in_specs=[*specs, *[whole(operand) for operand in operands]],
            out_specs=[whole(shape) for shape in out_shape],
        ),
        out_shape=out_shape,
        name="out_backward",
    )(core.reshape(1), *arrays, *operands)


def attention_back_kernel(*refs, first_head):
    (grad_ref, q_ref, k_ref, v_ref, total_ref, down_ref, across_ref) = refs[:7]
    dq_ref, dk_ref, dv_ref, sums_ref, mask_ref = refs[7:]
    step = pl.program_id(0)

    @pl.when(step == 0)
    def _():
        mask_ref[...] = jnp.where(down_ref[...] == across_ref[...], 0.0, NEGATIVE)

    pair_width = 2 * HEAD_DIM
    scale = HEAD_DIM ** (-0.5)
    lane = lax.broadcasted_iota(jnp.int32, (1, pair_width), 1)
    columns = q_ref.shape[1]
    heads = columns // HEAD_DIM
    for pair in range(heads // 2):
        span = slice(pair_width * pair, pair_width * (pair + 1))
        queries, keys, values = q_ref[:, span], k_ref[:, span], v_ref[:, span]
        grads = grad_ref[:, span]
        scaled = to_full(queries) * scale
        sides = []
        for side in range(2):
            here = (lane < HEAD_DIM) == (side == 0)
            mine = to_low(jnp.where(here, scaled, 0.0))
            my_grads = jnp.where(here, grads, jnp.zeros_like(grads))
            head = first_head + step * heads + 2 * pair + side
            scores = matmul_nt(keys, mine) + mask_ref[...]
            softmax = jnp.exp(scores - total_ref[pl.ds(head, 1), :])
            softmax_grad = matmul_nt(values, my_grads)
            inner = jnp.sum(softmax * softmax_grad, axis=0, keepdims=True)
            score_grad = to_low(softmax * (softmax_grad - inner))
            query_grad = matmul_tn(keys, score_grad)[HEAD_DIM * side : HEAD_DIM * (side + 1)]
            sides.append((query_grad, matmul(score_grad, mine), matmul(to_low(softmax), my_grads)))
        query_grad = to_low(jnp.concatenate([sides[0][0], sides[1][0]], axis=0).T * scale)
        value_grad = to_low(sides[0][2] + sides[1][2])
        dq_ref[:, span] = query_grad
        dk_ref[:, span] = to_low(sides[0][1] + sides[1][1])
        dv_ref[:, span] = value_grad
        sums_ref[0:1, span] = jnp.sum(to_full(query_grad), axis=0, keepdims=True)
        sums_ref[1:2, span] = jnp.sum(to_full(value_grad), axis=0, keepdims=True)


def attention_backward(context_grad, queries, keys, values, score_total, segments, start, columns):
    rows = context_grad.shape[0]
    size = 2 * HEAD_DIM
    down, across = segments[:, None], segments[None, :]
    block = pl.BlockSpec((rows, size), lambda s: (0, start // size + s))
    out_block = pl.BlockSpec((rows, size), lambda s: (0, s))
    return pl.pallas_call(
        functools.partial(attention_back_kernel, first_head=start // HEAD_DIM),
        grid=(columns // size,),
        in_specs=[*[block] * 4, whole(score_total), whole(down), whole(across)],
        out_specs=[*[out_block] * 3, pl.BlockSpec((8, size), lambda s: (0, s))],
        out_shape=[
            *[jax.ShapeDtypeStruct((rows, columns), jnp.bfloat16)] * 3,
            jax.ShapeDtypeStruct((8, columns), jnp.float32),
        ],
        scratch_shapes=[pltpu.VMEM((rows, rows), jnp.float32)],
        compiler_params=pltpu.CompilerParams(dimension_semantics=("arbitrary",)),
        name="attention_backward",
    )(context_grad, queries, keys, values, score_total, down, across)


def joined_sums(bias_sums, out_sums, feed_sums, head_sums, steps):
    return jnp.concatenate(
        [
            jnp.concatenate([part[:2] for part in bias_sums], axis=1),
            out_sums[:3],
            feed_sums[: 3 + steps],
            head_sums[: 8 - steps],
        ],
        axis=0,
    )


def last_grads_kernel(place, *refs, parts, share, steps):
    tokens_ref, context_ref, branch_ref, out_sums_ref, feed_sums_ref, head_sums_ref, *rest = refs
    mixed_refs, rest = rest[: 3 * parts], rest[3 * parts :]
    bias_refs, outs = rest[:parts], rest[parts:]
    turned = tokens_ref[...].T
    for which in range(3):
        for part in range(parts):
            mixed = mixed_refs[3 * part + which][...]
            columns = mixed.shape[1]
            grad = to_low(matmul(turned, mixed))
            if share:
                rows = slice(share * which, share * (which + 1))
                store_blocks(outs, grad, place, share, rows, column=columns * part)
            else:
                outs[which][:, columns * part : columns * (part + 1)] = grad
    grad = to_low(matmul_tn(context_ref[...], branch_ref[...]))
    if share:
        store_blocks(outs, grad, place, share, slice(3 * share, 4 * share))
        small = to_low(
            joined_sums(
                [ref[...] for ref in bias_refs],
                out_sums_ref[...],
                feed_sums_ref[...],
                head_sums_ref[...],
                steps,
            )
        )
        half = small.shape[1] // 2
        for index, out_ref in enumerate(outs):
            part = small[:, half * (index % 2) : half * (index % 2 + 1)]
            out_ref[:, 4 * share :, :] = jnp.broadcast_to(
                part[None], (out_ref.shape[0], *part.shape)
            )
    else:
        outs[3][...] = grad


def last_grads(place, count, tokens, context, branch_grad, sums, steps, mixed):
    width = tokens.shape[1]
    share, chips = width // count, count // 2
    aligned = share % 8 == 0
    parts = len(mixed)
    biases = [part[3] for part in mixed]
    mixed = [part[:3] for part in mixed]
    operands = [tokens, context, branch_grad, *sums, *[m for part in mixed for m in part], *biases]
    small = joined_sums(biases, *sums, steps)
    if aligned:
        rows = 4 * share + small.shape[0]
        out_shape = [jax.ShapeDtypeStruct((chips, rows, width // 2), jnp.bfloat16)] * 4
    else:
        out_shape = [jax.ShapeDtypeStruct((width, width), jnp.bfloat16)] * 4
    outs = pl.pallas_call(
        functools.partial(
            last_grads_kernel, parts=parts, share=share if aligned else 0, steps=steps
        ),
        grid_spec=pltpu.PrefetchScalarGridSpec(
            num_scalar_prefetch=1,
            grid=(1,),
            in_specs=[whole(operand) for operand in operands],
            out_specs=[whole(shape) for shape in out_shape],
        ),
        out_shape=out_shape,
        name="last_grads",
    )(place, *operands)
    if not aligned:
        both = jnp.broadcast_to(to_low(small)[None], (count, *small.shape))
        return arranged([*outs, both.reshape(-1, width)], place)
    return outs[:2], outs[2:]


def tokens_back_kernel(core, *refs, sizes, parts):
    ends = [sum(sizes[:k]) for k in range(4)]
    weights = [refs[ends[k] : ends[k + 1]] for k in range(3)]
    summed_ref, *mixed_refs, out_ref = refs[ends[3] :]
    total = summed_ref[...]
    for which in range(3):
        weight = read_weight(weights[which], core[0])
        for part in range(parts):
            mixed = mixed_refs[3 * part + which][...]
            columns = mixed.shape[1]
            total += matmul_nt(mixed, weight[:, columns * part : columns * (part + 1)])
    out_ref[...] = total


def tokens_backward(core, summed_grad, mixed, weights):
    width = summed_grad.shape[1]
    arrays, specs, sizes = [], [], []
    for group, index in weights:
        some, their = group.operands(index, core, width, lambda s, c: 0)
        arrays, specs, sizes = arrays + some, specs + their, sizes + [len(some)]
    operands = [summed_grad, *[matrix for part in mixed for matrix in part]]
    return pl.pallas_call(
        functools.partial(tokens_back_kernel, sizes=sizes, parts=len(mixed)),
        grid_spec=pltpu.PrefetchScalarGridSpec(
            num_scalar_prefetch=1,
            grid=(1,),
            in_specs=[*specs, *[whole(operand) for operand in operands]],
            out_specs=whole(summed_grad),
        ),
        out_shape=jax.ShapeDtypeStruct(summed_grad.shape, jnp.float32),
        name="tokens_backward",
    )(core.reshape(1), *arrays, *operands)


def take_kernel(index, whole_ref, *out_refs, plan):
    width = whole_ref.shape[1]
    for out_ref, (first_row, share) in zip(out_refs, plan):
        spot = index[0] * share
        row, place = first_row + spot // width, spot % width
        line = jnp.broadcast_to(whole_ref[pl.ds(row, 1), :], (8, width))
        moved = pltpu.roll(line, lax.rem(width - place, width), 1)
        out_ref[...] = moved[:1, :share]


def take_shares(device, values, first_rows, shares):
    shapes = [jax.ShapeDtypeStruct((1, share), jnp.float32) for share in shares]
    lines = pl.pallas_call(
        functools.partial(take_kernel, plan=list(zip(first_rows, shares))),
        grid_spec=pltpu.PrefetchScalarGridSpec(
            num_scalar_prefetch=1,
            grid=(1,),
            in_specs=[whole(values)],
            out_specs=[whole(shape) for shape in shapes],
        ),
        out_shape=shapes,
        name="take_shares",
    )(device.reshape(1), values)
    return [line[0] for line in lines]


def take(value, axis, index):
    return lax.dynamic_index_in_dim(value, index, axis, keepdims=False)


def add_low(first, second):
    return to_low(to_full(first) + to_full(second))


def halve(value, axis, stride):
    chips = lax.axis_size("dp")
    bit = (lax.axis_index("dp") // stride) % 2
    pairs = [(chip, chip ^ stride) for chip in range(chips)]
    arrived = lax.ppermute(take(value, axis, 1 - bit), "dp", pairs)
    return add_low(take(value, axis, bit), arrived)


def core_swap(away):
    return lax.ppermute(away, "fsdp", [(0, 1), (1, 0)])


def along(sent, stride):
    chips = lax.axis_size("dp")
    return lax.ppermute(sent, "dp", [(chip, chip ^ stride) for chip in range(chips)])


def total_of(addends):
    total = to_full(addends[0])
    for addend in addends[1:]:
        total = total + to_full(addend)
    return total


def my_place():
    chip = lax.axis_index("dp")
    return jnp.stack([lax.axis_index("fsdp"), chip % 2, (chip // 2) % 2, chip // 4])


def chip_at(index, place, levels, first_axis):
    outer, level = index // levels, index % levels
    bits = (outer // 2, outer % 2) if first_axis == 0 else (outer % 2, outer // 2)
    return ((place[3] ^ level) * 2 + (place[2] ^ bits[1])) * 2 + (place[1] ^ bits[0])


def index_of(chip, place, levels, first_axis):
    bits = ((chip % 2) ^ place[1], ((chip // 2) % 2) ^ place[2])
    outer = 2 * bits[first_axis] + bits[1 - first_axis]
    return outer * levels + ((chip // 4) ^ place[3])


class ChipSum:
    def __init__(self, away, kept):
        self.sides = [[part] for part in kept]
        self.strides = [[1, 2], [2, 1]]
        self.arrived = [core_swap(part) for part in away]

    def add(self, arrived):
        for side, part in zip(self.sides, arrived):
            side.append(part)

    def sends(self):
        sent = [to_low(total_of([a[a.shape[0] // 2 :] for a in side])) for side in self.sides]
        self.sides = [[a[: a.shape[0] // 2] for a in side] for side in self.sides]
        return sent

    def start(self, sent):
        self.arrived = [along(part, strides.pop(0)) for part, strides in zip(sent, self.strides)]

    def level_block(self, level):
        return jnp.concatenate(
            [total_of([a[level] for a in side]) for side in self.sides], axis=-1
        )

    def level_sends(self):
        while self.sides[0][0].shape[0] > 4:
            stride = 4 * (self.sides[0][0].shape[0] // 2)
            sent = self.sends()
            self.add([along(part, stride) for part in sent])
        levels = self.sides[0][0].shape[0]
        return [to_low(self.level_block(level)) for level in range(1, levels)]

    def start_levels(self, sent):
        self.arrived = [along(part, 4 * (level + 1)) for level, part in enumerate(sent)]

    def result(self, arrived):
        return total_of([self.level_block(0), *arrived])


def arranged(matrices, place):
    chips = lax.axis_size("dp")
    value = jnp.concatenate(
        [matrix.reshape(chips, 2, -1, matrix.shape[-1]) for matrix in matrices], axis=2
    )
    half = value.shape[-1] // 2
    sides = []
    for core in (1 - place[0], place[0]):
        mine = take(value, 1, core)
        sides.append(
            [
                jnp.take(
                    mine[..., axis * half : (axis + 1) * half],
                    chip_at(jnp.arange(chips), place, chips // 4, axis),
                    axis=0,
                )
                for axis in range(2)
            ]
        )
    return sides


def store_blocks(outs, value, place, share, rows, first_chip=0, column=0):
    columns = value.shape[-1]
    split = value.reshape(-1, 2, share, columns)
    kept, away = in_order(split[:, 0], split[:, 1], place[0])
    levels = outs[0].shape[0] // 4
    width = outs[0].shape[-1]
    for chip in range(split.shape[0]):
        for which, half in enumerate((away, kept)):
            for axis in range(2):
                low, high = max(column, axis * width), min(column + columns, (axis + 1) * width)
                if low >= high:
                    continue
                spot = index_of(first_chip + chip, place, levels, axis)
                outs[2 * which + axis][
                    pl.ds(spot, 1), rows, low - axis * width : high - axis * width
                ] = half[chip : chip + 1, :, low - column : high - column]


def tie(value, *others):
    return lax.optimization_barrier((value, *others))


def window_base(start, total, window):
    return pl.multiple_of(jnp.minimum((start // 16) * 16, total - window), 16)


def compact_kernel(place, places, counts, mine_ref, other_ref, out_ref, *, window):
    step = pl.program_id(0)

    @pl.when(step == 0)
    def _():
        out_ref[...] = jnp.zeros_like(out_ref)

    _, batch, slots, half = mine_ref.shape
    levels = pl.num_programs(0) * batch // 4
    total = out_ref.shape[0]
    for which, ref in enumerate((mine_ref, other_ref)):
        core = place[0] if which == 0 else 1 - place[0]
        for axis in range(2):
            for lane in range(batch):
                source = 2 * chip_at(step * batch + lane, place, levels, axis) + core
                start = places[source]
                base = window_base(start, total, window)
                row = lax.broadcasted_iota(jnp.int32, (window, slots), 0) + (base - start)
                column = lax.broadcasted_iota(jnp.int32, (window, slots), 1)
                chosen = jnp.where((row == column) & (column < counts[source]), 1.0, 0.0)
                moved = matmul(to_low(chosen), ref[axis, lane])
                out_ref[pl.ds(base, window), half * axis : half * (axis + 1)] += to_low(moved)


def compact(place, places, counts, mine, other, total):
    _, chips, slots, half = mine.shape
    batch = 4
    block = pl.BlockSpec((2, batch, slots, half), lambda i, *_: (0, i, 0, 0))
    return pl.pallas_call(
        functools.partial(compact_kernel, window=slots + 16),
        grid_spec=pltpu.PrefetchScalarGridSpec(
            num_scalar_prefetch=3,
            grid=(chips // batch,),
            in_specs=[block, block],
            out_specs=pl.BlockSpec((total, 2 * half), lambda i, *_: (0, 0)),
        ),
        out_shape=jax.ShapeDtypeStruct((total, 2 * half), jnp.bfloat16),
        compiler_params=pltpu.CompilerParams(dimension_semantics=("arbitrary",)),
        name="compact_rows",
    )(place, places, counts, mine, other)


def compact_labels_kernel(places, counts, lines_ref, out_ref):
    out_ref[...] = jnp.zeros_like(out_ref)
    sources, slots = lines_ref.shape
    total = out_ref.shape[1]
    wide = 2 * slots
    lane = lax.broadcasted_iota(jnp.int32, (8, wide), 1)

    def place_one(source, carry):
        start = places[source]
        base = pl.multiple_of(jnp.minimum(start // slots * slots, total - wide), slots)
        shift = start - base
        line = jnp.broadcast_to(to_full(lines_ref[pl.ds(source, 1), :]), (8, slots))
        line = jnp.concatenate([line, jnp.zeros_like(line)], axis=1)
        moved = pltpu.roll(line, lax.rem(shift, wide), 1)
        here = (lane >= shift) & (lane < shift + counts[source])
        span = pl.ds(base, wide)
        out_ref[:, span] = jnp.where(here, moved, out_ref[:, span])
        return carry

    lax.fori_loop(0, sources, place_one, 0)


def compact_labels(places, counts, lines, total):
    out = pl.pallas_call(
        compact_labels_kernel,
        grid_spec=pltpu.PrefetchScalarGridSpec(
            num_scalar_prefetch=2,
            grid=(1,),
            in_specs=[whole(lines)],
            out_specs=pl.BlockSpec((8, total), lambda *_: (0, 0)),
        ),
        out_shape=jax.ShapeDtypeStruct((8, total), jnp.float32),
        name="compact_labels",
    )(places, counts, lines)
    return out[0].astype(jnp.int32)


def gather_blocks(value, beside, given):
    chips = lax.axis_size("dp")
    levels = chips // 4
    half = value.shape[-1] // 2
    if levels <= 4:
        others = jnp.stack([along(value, 4 * level) for level in range(1, levels)])
    else:
        others = value[None]
        while others.shape[0] < levels:
            others = jnp.concatenate([others, along(others, 4 * others.shape[0])])
        others = others[1:]
    own = [value[:, :half], value[:, half:]]
    strides = [(1, 2), (2, 1)]
    near = [along(part, first) for part, (first, _) in zip(own, strides)]
    far_sent = [jnp.stack([part, got]) for part, got in zip(own, near)]
    others = tie(others, *far_sent)[0]
    far = [along(sent, second) for sent, (_, second) in zip(far_sent, strides)]
    rest = [others[..., :half], others[..., half:]]
    near_rest = [along(part, first) for part, (first, _) in zip(rest, strides)]
    given, *near_rest = tie(given, *near_rest)
    far_rest = [
        along(jnp.concatenate([part, got]), second)
        for part, got, (_, second) in zip(rest, near_rest, strides)
    ]
    result, *far_rest = tie(beside(given), *far_rest)
    count = levels - 1
    mine = jnp.stack(
        [
            jnp.concatenate(
                [
                    own[k][None],
                    rest[k],
                    far[k][:1],
                    far_rest[k][:count],
                    near[k][None],
                    near_rest[k],
                    far[k][1:],
                    far_rest[k][count:],
                ]
            )
            for k in range(2)
        ]
    )
    return mine, core_swap(mine), result


def spread_kernel(place, places, counts, rows_ref, *out_refs, window):
    step = pl.program_id(0)
    total = rows_ref.shape[0]
    batch, slots, half = out_refs[0].shape
    levels = pl.num_programs(0) * batch // 4
    for which in range(2):
        core = 1 - place[0] if which == 0 else place[0]
        for axis in range(2):
            for lane in range(batch):
                chip = chip_at(step * batch + lane, place, levels, axis)
                source = 2 * chip + core
                start = places[source]
                base = window_base(start, total, window)
                row = lax.broadcasted_iota(jnp.int32, (slots, window), 0)
                column = lax.broadcasted_iota(jnp.int32, (slots, window), 1) + (base - start)
                chosen = jnp.where((row == column) & (row < counts[source]), 1.0, 0.0)
                moved = matmul(
                    to_low(chosen), rows_ref[pl.ds(base, window), half * axis : half * (axis + 1)]
                )
                out_refs[2 * which + axis][lane] = to_low(moved)


def spread(place, places, counts, rows, slots):
    chips = places.shape[0] // 2
    total, width = rows.shape
    batch = 2
    block = pl.BlockSpec((batch, slots, width // 2), lambda i, *_: (i, 0, 0))
    shape = jax.ShapeDtypeStruct((chips, slots, width // 2), jnp.bfloat16)
    outs = pl.pallas_call(
        functools.partial(spread_kernel, window=slots + 16),
        grid_spec=pltpu.PrefetchScalarGridSpec(
            num_scalar_prefetch=3,
            grid=(chips // batch,),
            in_specs=[
                pl.BlockSpec((total, width), lambda i, *_: (0, 0), pipeline_mode=pl.Buffered(1))
            ],
            out_specs=[block] * 4,
        ),
        out_shape=[shape] * 4,
        compiler_params=pltpu.CompilerParams(dimension_semantics=("arbitrary",)),
        name="spread_rows",
    )(place, places, counts, rows)
    return outs[:2], outs[2:]


def per_device(
    tokens,
    segments,
    mask_flags,
    targets,
    cotangent,
    qkv_weight,
    attn_bias,
    out_weight,
    out_bias,
    attn_gain,
    attn_shift,
    up_weight,
    up_bias,
    down_weight,
    down_bias,
    ffn_gain,
    ffn_shift,
    dense_weight,
    dense_bias,
    head_gain,
    head_shift,
    decoder,
    vocab_bias,
):
    count = lax.axis_size(AXES)
    width = tokens.shape[1]
    core = lax.axis_index("fsdp")
    device = lax.axis_index(AXES)
    here = my_place()
    blocks = qkv_weight.shape[1] // width
    steps = up_weight.shape[1] // width
    share, up_share, down_share = out_weight.shape[0], up_weight.shape[0], down_weight.shape[0]
    label_place = up_share * steps + down_share + share
    later_packed = pack_later(
        [
            (up_weight, [up_share * k for k in range(steps)]),
            (down_weight, [up_share * steps]),
            (dense_weight, [up_share * steps + down_share]),
        ],
        mask_flags,
        targets,
    )
    later_gathered = lax.all_gather(later_packed, AXES, axis=0)
    later = Weights([later_gathered], [*[up_share] * steps, down_share, share])
    small = (
        attn_bias,
        out_bias,
        attn_gain,
        attn_shift,
        down_bias,
        ffn_gain,
        ffn_shift,
        up_bias,
        dense_bias,
        head_gain,
        head_shift,
    )
    small_rows = (0, 2, 3, 4, 5, 6, 7, 8, 12, 13, 14)
    placed = place_shares(device, small, small_rows, 16, width)
    half = 2 * share + 8
    first_packed = pack_rows(
        [
            (qkv_weight, [0, share, half]),
            (placed[:8], [2 * share]),
            (out_weight, [half + share]),
            (placed[8:], [half + 2 * share]),
        ]
    )
    upper, lower = gather_pair(first_packed, half)
    first_group, second_group = (Weights(list(pair), [share, share, 8]) for pair in (upper, lower))
    vectors, more_vectors = (
        sum(jnp.sum(to_full(array[:, 2 * share :]), axis=0) for array in pair)
        for pair in (upper, lower)
    )
    queries, keys_low, values_low, context, score_total, summed1, hidden = attention_forward(
        core,
        tokens,
        segments,
        [(first_group, 0), (first_group, 1), (second_group, 0), (second_group, 1)],
        vectors,
    )
    active, slope, summed2, output = ffn_forward(hidden, later, more_vectors[:4], vectors)
    head_gain_full, head_shift_full = more_vectors[5], more_vectors[6]
    mask_rank = jnp.cumsum(mask_flags) - 1
    slot_place = jnp.where(mask_flags > 0, mask_rank, -1)
    picker_low = (jnp.arange(MAXM)[:, None] == slot_place[None, :]).astype(jnp.bfloat16)
    own_rows, dense, normed_low = head_forward(picker_low, output, later, steps + 1, more_vectors)
    _, tail_back = jax.vjp(head_tail, dense, head_gain_full, head_shift_full)
    chips = count // 2
    group = MASK_DEV * chips
    total = 2 * group
    gathered_late, normed_low = tie(later_gathered, normed_low)
    label_parts = gathered_late[:, label_place : label_place + 2, :MAXM].astype(jnp.int32)
    label_lines = label_parts[:, 0] * 256 + label_parts[:, 1] - 1
    counts = jnp.sum((label_lines >= 0).astype(jnp.int32), axis=1)
    by_core = counts.reshape(chips, 2)
    earlier = jnp.arange(chips)[:, None] < jnp.arange(chips)[None, :]
    places = jnp.sum(jnp.where(earlier[:, :, None], by_core[:, None, :], 0), axis=0)
    places = (places + jnp.arange(2)[None, :] * group).reshape(count)
    all_labels = compact_labels(places, counts, label_lines, total)
    slice_index = lax.axis_index(AXES)
    vocab_rows = decoder.shape[0]
    local_label = all_labels - slice_index * vocab_rows
    label_hit = jnp.arange(vocab_rows)[None, :] == local_label[:, None]

    def pull_labels(chosen):
        hit = jnp.arange(vocab_rows)[None, :] == chosen[:, None]
        return to_low(matmul(hit.astype(jnp.bfloat16), decoder))

    mine, other, label_pull = gather_blocks(normed_low, pull_labels, local_label)
    all_rows = compact(here, places, counts, mine, other, total)
    logits = matmul_nt(all_rows, decoder) + to_full(vocab_bias)
    row_peak = jnp.max(logits, axis=1)
    exp_sums = jnp.sum(jnp.exp(logits - row_peak[:, None]), axis=1)
    label_sum = jnp.sum(jnp.where(label_hit, logits, 0.0))
    local_total = (row_peak + jnp.log(exp_sums)).reshape(-1, 128)
    lines = local_total.shape[0]
    merged = jnp.concatenate(
        [local_total, jnp.pad(label_sum[None, None], ((0, 7), (0, 127)))], axis=0
    )
    is_total = jnp.arange(lines + 8)[:, None] < lines
    pull = None
    stride = 1
    while stride < count:
        arrived = lax.ppermute(merged, AXES, [(place, place ^ stride) for place in range(count)])
        if pull is None:
            pull = matmul(to_low(jnp.exp(logits - row_peak[:, None])), decoder)
            arrived, pull = tie(arrived, pull)
        both = jnp.maximum(merged, arrived) + jnp.log1p(jnp.exp(-jnp.abs(merged - arrived)))
        merged = jnp.where(is_total, both, merged + arrived)
        stride *= 2
    log_total = merged[:lines].reshape(total)
    mean_loss = (jnp.sum(log_total) - merged[lines, 0]) / total
    rows_part = to_low(pull * jnp.exp(row_peak - log_total)[:, None] - to_full(label_pull))
    rows_sum = ChipSum(*spread(here, places, counts, rows_part, MAXM))
    rows_sum.add(rows_sum.arrived)
    rows_sum.start(rows_sum.sends())
    logit_grad = to_low(jnp.exp(logits - log_total[:, None]) - label_hit.astype(jnp.float32))
    vocab_bias_grad = jnp.sum(to_full(logit_grad), axis=0)
    logit_grad, vocab_bias_grad, *arrived = tie(logit_grad, vocab_bias_grad, *rows_sum.arrived)
    rows_sum.add(arrived)
    rows_sum.start(rows_sum.sends())
    decoder_grad = matmul_tn(logit_grad, all_rows)
    decoder_grad, *arrived = tie(decoder_grad, *rows_sum.arrived)
    rows_sum.add(arrived)
    rows_sum.start_levels(rows_sum.level_sends())
    normed_grad = rows_sum.result(rows_sum.arrived)
    dense_grad, head_gain_grad, head_shift_grad = tail_back(normed_grad)
    dense_grad_low = to_low(dense_grad)
    dense_bias_grad = jnp.sum(to_full(dense_grad_low), axis=0)
    dense_full = Weights([gathered_late], later.shares).natural(steps + 1, None)
    picked_grad = to_low(matmul_nt(dense_grad_low, dense_full))
    hidden_grad, feed_sums, *feed_grads = feed_backward(
        here,
        count,
        cotangent,
        picker_low,
        picked_grad,
        summed2,
        vectors,
        own_rows,
        dense_grad_low,
        hidden,
        active,
        slope,
        later,
    )
    first = ChipSum(*feed_grads)
    summed1_grad, branch1_grad, context_grad, out_sums = out_backward(
        core, hidden_grad, summed1, vectors, second_group, 1
    )
    context_grad, *arrived = tie(context_grad, *first.arrived)
    first.add(arrived)
    context_grad, *sent = tie(context_grad, *first.sends())
    first.start(sent)
    saved = (queries, keys_low, values_low, score_total, segments)
    middle = width // 2
    mixed = [list(attention_backward(context_grad, *saved, 0, middle))]
    mixed[0][0], context_grad = tie(mixed[0][0], context_grad)
    mixed.append(list(attention_backward(context_grad, *saved, middle, width - middle)))
    head_sums = jnp.stack(
        [dense_bias_grad, head_gain_grad, head_shift_grad, *[jnp.zeros((width,))] * 5]
    )
    away, kept = last_grads(
        here, count, tokens, context, branch1_grad, (out_sums, feed_sums, head_sums), steps, mixed
    )
    mixed = [part[:3] for part in mixed]
    second = ChipSum(away, kept)
    mixed[0][0], _, *arrived = tie(mixed[0][0], away[0], *first.arrived)
    first.add(arrived)
    mixed[0][0], *sent = tie(mixed[0][0], *first.sends())
    first.start(sent)
    mixed[0][0], *arrived = tie(mixed[0][0], *second.arrived)
    second.add(arrived)
    mixed[0][0], *sent = tie(mixed[0][0], *second.sends())
    second.start(sent)
    tokens_grad = tokens_backward(
        core, summed1_grad, mixed, [(first_group, 0), (first_group, 1), (second_group, 0)]
    )
    first.add(first.arrived)
    first.start_levels(first.level_sends())
    second.add(second.arrived)
    second.start(second.sends())
    second.add(second.arrived)
    second.start_levels(second.level_sends())
    first, second = first.result(first.arrived), second.result(second.arrived)
    up_pieces = [first[share * k : share * (k + 1)] for k in range(steps)]
    down_piece = first[up_share * steps : up_share * steps + down_share]
    dense_piece = first[up_share * steps + down_share :]
    qkv_pieces = [second[share * k : share * (k + 1)] for k in range(blocks)]
    out_piece = second[share * blocks : share * (blocks + 1)]
    small_pieces = take_shares(
        device, second[share * (blocks + 1) :], small_rows, [vector.shape[0] for vector in small]
    )
    return (
        output,
        mean_loss,
        tokens_grad,
        jnp.concatenate(qkv_pieces, axis=1),
        small_pieces[0],
        out_piece,
        *small_pieces[1:4],
        jnp.concatenate(up_pieces, axis=1),
        small_pieces[7],
        down_piece,
        *small_pieces[4:7],
        dense_piece,
        *small_pieces[8:],
        decoder_grad,
        vocab_bias_grad,
    )


def solution(mesh):
    matrix_spec = P(AXES, None)
    vector_spec = P(AXES)
    m, v = matrix_spec, vector_spec
    return jax.shard_map(
        per_device,
        mesh=mesh,
        in_specs=(m, v, v, v, m, m, v, m, v, v, v, m, v, m, v, v, v, m, v, v, v, m, v),
        out_specs=(m, P(), m, m, v, m, v, v, v, m, v, m, v, v, v, m, v, v, v, m, v),
        check_vma=False,
    )
```

```python
import functools

import jax
import jax.numpy as jnp
from jax import lax
from jax.experimental import pallas as pl
from jax.experimental.pallas import tpu as pltpu
from jax.sharding import PartitionSpec as P

HEADS = 12
HEAD_DIM = 64
MASK_DEV = 64
MAXM = 128

EPSILON = 1e-05
NEGATIVE = -1e30
AXES = ("dp", "fsdp")


def to_low(values):
    return values.astype(jnp.bfloat16)


def to_full(values):
    return values.astype(jnp.float32)


def layer_norm(values, gain_vector, shift_vector):
    center = values - jnp.mean(values, axis=-1, keepdims=True)
    spread = jnp.mean(center * center, axis=-1, keepdims=True)
    return center * lax.rsqrt(spread + EPSILON) * gain_vector + shift_vector


def gelu_exact(values):
    return jax.nn.gelu(values, approximate=False)


def head_tail(dense_out, gain_vector, shift_vector):
    return layer_norm(gelu_exact(dense_out), gain_vector, shift_vector)


def matmul(left_side, right_side):
    return jnp.dot(left_side, right_side, preferred_element_type=jnp.float32)


def matmul_tn(left_side, right_side):
    return lax.dot_general(
        left_side, right_side, (((0,), (0,)), ((), ())), preferred_element_type=jnp.float32
    )


def matmul_nt(left_side, right_side):
    return lax.dot_general(
        left_side, right_side, (((1,), (1,)), ((), ())), preferred_element_type=jnp.float32
    )


def column_blocks(matrix, width):
    return [matrix[:, k : k + width] for k in range(0, matrix.shape[1], width)]


def gelu_parts(values):
    size = jnp.abs(values) * 0.7071067811865476
    ratio = 1.0 / (1.0 + 0.3275911 * size)
    bell = jnp.exp(-0.5 * values * values)
    series = 1.421413741 + ratio * (-1.453152027 + ratio * 1.061405429)
    series = ratio * (0.254829592 + ratio * (-0.284496736 + ratio * series))
    tail = 0.5 * series * bell
    below = jnp.where(values < 0, tail, 1.0 - tail)
    return values * below, below + values * bell * 0.3989422804014327


def flat_rows(value):
    return value.reshape(-1, value.shape[-1])


def whole(array):
    return pl.BlockSpec(array.shape, lambda *_: (0,) * array.ndim)


class Weights:
    def __init__(self, arrays, shares):
        self.arrays = arrays
        self.starts = [sum(shares[:k]) for k in range(len(shares))]
        self.shares = shares

    def natural(self, index, core):
        span = slice(self.starts[index], self.starts[index] + self.shares[index])
        pieces = [array[:, span] for array in self.arrays]
        if len(pieces) == 2:
            pieces = [jnp.stack(in_order(*pieces, core), axis=1)]
        return flat_rows(pieces[0].reshape(-1, *pieces[0].shape[-2:]))

    def operands(self, index, core, columns, column_map, parts=1, part_map=lambda *_: 0):
        share, start = self.shares[index], self.starts[index]
        if share % 8 or start % share:
            array = self.natural(index, core)
            rows = array.shape[0] // parts
            spec = pl.BlockSpec((rows, columns), lambda *i: (part_map(*i), column_map(*i)))
            return [array], [spec]
        place = start // share
        specs = [
            pl.BlockSpec(
                (array.shape[0] // parts, share, columns),
                lambda *i: (part_map(*i), place, column_map(*i)),
            )
            for array in self.arrays
        ]
        return list(self.arrays), specs


def up_operands_of(weights, steps):
    share = weights.shares[0]
    width = weights.arrays[0].shape[-1]
    if share % 8:
        array = jnp.concatenate([weights.natural(k, None) for k in range(steps)], axis=1)
        return [array], [pl.BlockSpec((array.shape[0], width), lambda s, *_: (0, s))]
    array = weights.arrays[0]
    return [array], [pl.BlockSpec((array.shape[0], share, width), lambda s, *_: (0, s, 0))]


def in_order(mine, other, core):
    return jnp.where(core == 0, mine, other), jnp.where(core == 0, other, mine)


def read_weight(refs, core):
    if len(refs) == 1:
        return flat_rows(refs[0][...])
    return flat_rows(jnp.stack(in_order(refs[0][...], refs[1][...], core), axis=1))


def pack_kernel(*refs, layout):
    *sources, out_ref = refs
    for source, (column, row, rows, columns) in zip(sources, layout):
        for k in range(column):
            out_ref[row[k] : row[k] + rows, :] = source[:, k * columns : (k + 1) * columns]


def pack_rows(pieces):
    width = pieces[0][0].shape[1] // len(pieces[0][1])
    total = max(row + m.shape[0] for m, rows in pieces for row in rows)
    if any(row % 8 for _, rows in pieces for row in rows):
        placed = sorted(
            (row, m[:, k * width : (k + 1) * width])
            for m, rows in pieces
            for k, row in enumerate(rows)
        )
        return jnp.concatenate([block for _, block in placed], axis=0)
    matrices = [m for m, _ in pieces]
    layout = [(len(rows), tuple(rows), m.shape[0], width) for m, rows in pieces]
    return pl.pallas_call(
        functools.partial(pack_kernel, layout=layout),
        grid=(1,),
        in_specs=[whole(m) for m in matrices],
        out_specs=pl.BlockSpec((total, width), lambda i: (0, 0)),
        out_shape=jax.ShapeDtypeStruct((total, width), matrices[0].dtype),
        name="pack_rows",
    )(*matrices)


def pack_later_kernel(flags_ref, targets_ref, *refs, layout, label_place):
    *sources, out_ref = refs
    pack_kernel(*sources, out_ref, layout=layout)
    count = flags_ref.shape[1]
    flags = jnp.broadcast_to(flags_ref[...], (8, count))
    row = lax.broadcasted_iota(jnp.int32, (count, count), 0)
    column = lax.broadcasted_iota(jnp.int32, (count, count), 1)
    until = to_low(jnp.where(row <= column, 1.0, 0.0))
    rank = matmul(to_low(flags.astype(jnp.float32)), until)[:1] - 1.0
    slot = lax.broadcasted_iota(jnp.int32, (MAXM, count), 0).astype(jnp.float32)
    picker = to_low(jnp.where((slot == rank) & (flags_ref[...] > 0), 1.0, 0.0))
    shifted = targets_ref[...] + 1
    high = lax.shift_right_logical(shifted, 8)
    level = lax.broadcasted_iota(jnp.int32, (8, count), 0)
    halves = jnp.where(level == 0, high, jnp.where(level == 1, shifted - high * 256, 0))
    labels = matmul_nt(to_low(halves.astype(jnp.float32)), picker)
    empty = jnp.zeros((8, out_ref.shape[1] - MAXM), jnp.float32)
    out_ref[label_place : label_place + 8, :] = to_low(jnp.concatenate([labels, empty], axis=1))


def pack_later(pieces, mask_flags, targets):
    width = pieces[0][0].shape[1] // len(pieces[0][1])
    label_place = max(row + m.shape[0] for m, rows in pieces for row in rows)
    if any(row % 8 for _, rows in pieces for row in rows) or label_place % 8:
        rank = jnp.cumsum(mask_flags) - 1
        picker = (jnp.arange(MAXM)[:, None] == rank[None, :]) & (mask_flags > 0)[None, :]
        shifted = jnp.sum(jnp.where(picker, targets[None, :] + 1, 0), axis=1)
        labels = jnp.stack([shifted // 256, shifted % 256]).astype(jnp.bfloat16)
        labels = jnp.pad(labels, ((0, 6), (0, width - MAXM)))
        return pack_rows([*pieces, (labels, [label_place])])
    matrices = [m for m, _ in pieces]
    layout = [(len(rows), tuple(rows), m.shape[0], width) for m, rows in pieces]
    operands = [mask_flags[None], targets[None], *matrices]
    return pl.pallas_call(
        functools.partial(pack_later_kernel, layout=layout, label_place=label_place),
        grid=(1,),
        in_specs=[whole(operand) for operand in operands],
        out_specs=pl.BlockSpec((label_place + 8, width), lambda i: (0, 0)),
        out_shape=jax.ShapeDtypeStruct((label_place + 8, width), matrices[0].dtype),
        name="pack_later",
    )(*operands)


def place_kernel(index, line_ref, out_ref, *, plan):
    rows, width = out_ref.shape
    device = index[0]
    line = jnp.broadcast_to(line_ref[...], (8, width))
    lane = lax.broadcasted_iota(jnp.int32, (rows, width), 1)
    level = lax.broadcasted_iota(jnp.int32, (rows, width), 0)
    out = jnp.zeros((rows, width), jnp.float32)
    for first_row, start, share in plan:
        spot = device * share
        row, place = first_row + spot // width, spot % width
        moved = pltpu.roll(line, lax.rem(place - start + width, width), 1)
        here = (level == row) & (lane >= place) & (lane < place + share)
        out = jnp.where(here, jnp.broadcast_to(moved[:1], (rows, width)), out)
    out_ref[...] = out.astype(out_ref.dtype)


def place_shares(device, vectors, first_rows, rows, width):
    plan = []
    line = 0.0
    start = 0
    for vector, first_row in zip(vectors, first_rows):
        end = start + vector.shape[0]
        plan.append((first_row, start, vector.shape[0]))
        line = line + jnp.pad(to_full(vector), (start, width - end))
        start = end
    line = line[None, :]
    return pl.pallas_call(
        functools.partial(place_kernel, plan=plan),
        grid_spec=pltpu.PrefetchScalarGridSpec(
            num_scalar_prefetch=1,
            grid=(1,),
            in_specs=[whole(line)],
            out_specs=pl.BlockSpec((rows, width), lambda i, d: (0, 0)),
        ),
        out_shape=jax.ShapeDtypeStruct((rows, width), jnp.bfloat16),
        name="place_shares",
    )(device.reshape(1), line)


def double(value, stride, axis):
    chips = lax.axis_size("dp")
    bit = (lax.axis_index("dp") // stride) % 2
    arrived = lax.ppermute(value, "dp", [(chip, chip ^ stride) for chip in range(chips)])
    low, high = in_order(value, arrived, bit)
    return jnp.stack([low, high], axis=axis)


def gather_pair(value, split):
    chips = lax.axis_size("dp")
    stride = 4
    value = value[None]
    while stride < chips:
        value = double(value, stride, 0)
        value = value.reshape(-1, *value.shape[2:])
        stride *= 2
    upper, lower = value[:, :split], value[:, split:]
    upper, lower = double(upper, 1, 1), double(lower, 2, 1)
    upper, lower = double(upper, 2, 1), double(lower, 1, 2)
    upper, lower = (part.reshape(chips, *part.shape[-2:]) for part in (upper, lower))
    swap = [(0, 1), (1, 0)]
    return (upper, lax.ppermute(upper, "fsdp", swap)), (lower, lax.ppermute(lower, "fsdp", swap))


def attention_kernel(core, *refs, sizes):
    ends = [0]
    for size in sizes:
        ends.append(ends[-1] + size)
    weights = [refs[ends[k] : ends[k + 1]] for k in range(len(sizes))]
    (tokens_ref, bias_ref, vector_ref, down_ref, across_ref) = refs[ends[-1] : ends[-1] + 5]
    (q_ref, k_ref, v_ref, context_ref, total_ref, summed_ref, hidden_ref) = refs[ends[-1] + 5 : -2]
    mask_ref, all_ref = refs[-2:]
    step = pl.program_id(0)

    @pl.when(step == 0)
    def _():
        mask_ref[...] = jnp.where(down_ref[...] == across_ref[...], 0.0, NEGATIVE)

    tokens = tokens_ref[...]
    queries = to_low(matmul(tokens, read_weight(weights[0], core[0])) + bias_ref[0:1, :])
    keys = to_low(matmul(tokens, read_weight(weights[1], core[0])))
    values = to_low(matmul(tokens, read_weight(weights[2], core[0])) + bias_ref[1:2, :])
    q_ref[...], k_ref[...], v_ref[...] = queries, keys, values
    heads = queries.shape[1] // HEAD_DIM
    pair_width = 2 * HEAD_DIM
    lane = lax.broadcasted_iota(jnp.int32, (1, pair_width), 1)
    for pair in range(heads // 2):
        span = slice(pair_width * pair, pair_width * (pair + 1))
        scaled = to_full(queries[:, span]) * HEAD_DIM ** (-0.5)
        sides = []
        for side in range(2):
            mine = to_low(jnp.where((lane < HEAD_DIM) == (side == 0), scaled, 0.0))
            scores = matmul_nt(keys[:, span], mine) + mask_ref[...]
            peak = jnp.max(scores, axis=0, keepdims=True)
            exponent = jnp.exp(scores - peak)
            total = jnp.sum(exponent, axis=0, keepdims=True)
            total_ref[pl.ds(step * heads + 2 * pair + side, 1), :] = peak + jnp.log(total)
            softmax_low = to_low(exponent * (1.0 / total))
            mixed = matmul_tn(values[:, span], softmax_low)
            sides.append(mixed[HEAD_DIM * side : HEAD_DIM * (side + 1)])
        context = to_low(jnp.concatenate(sides, axis=0).T)
        context_ref[:, span] = context
        all_ref[step * (heads // 2) + pair] = context

    @pl.when(step == pl.num_programs(0) - 1)
    def _():
        pairs = all_ref.shape[0]
        context = jnp.concatenate([all_ref[k] for k in range(pairs)], axis=1)
        product = matmul(context, read_weight(weights[3], core[0]))
        summed = to_full(tokens_ref[...]) + product + vector_ref[2:3, :]
        summed_ref[...] = summed
        hidden_ref[...] = to_low(layer_norm(summed, vector_ref[3:4, :], vector_ref[4:5, :]))


def attention_forward(core, tokens, segments, weights, vectors):
    rows, width = tokens.shape
    columns = 256
    arrays, specs, sizes = [], [], []
    for k, (group, index) in enumerate(weights):
        size, place = (columns, lambda s, c: s) if k < 3 else (width, lambda s, c: 0)
        some, their = group.operands(index, core, size, place)
        arrays, specs, sizes = arrays + some, specs + their, sizes + [len(some)]
    down, across = segments[:, None], segments[None, :]
    block = pl.BlockSpec((rows, columns), lambda s, c: (0, s))
    head_rows = 16
    return pl.pallas_call(
        functools.partial(attention_kernel, sizes=sizes),
        grid_spec=pltpu.PrefetchScalarGridSpec(
            num_scalar_prefetch=1,
            grid=(width // columns,),
            in_specs=[
                *specs,
                whole(tokens),
                pl.BlockSpec((8, columns), lambda s, c: (0, s)),
                whole(vectors),
                whole(down),
                whole(across),
            ],
            out_specs=[
                block,
                block,
                block,
                block,
                pl.BlockSpec((head_rows, rows), lambda s, c: (0, 0)),
                whole(tokens),
                whole(tokens),
            ],
            scratch_shapes=[
                pltpu.VMEM((rows, rows), jnp.float32),
                pltpu.VMEM((width // (2 * HEAD_DIM), rows, 2 * HEAD_DIM), jnp.bfloat16),
            ],
        ),
        out_shape=[
            *[jax.ShapeDtypeStruct((rows, width), jnp.bfloat16)] * 4,
            jax.ShapeDtypeStruct((head_rows, rows), jnp.float32),
            jax.ShapeDtypeStruct((rows, width), jnp.float32),
            jax.ShapeDtypeStruct((rows, width), jnp.bfloat16),
        ],
        compiler_params=pltpu.CompilerParams(dimension_semantics=("arbitrary",)),
        name="attention_forward",
    )(core.reshape(1), *arrays, tokens, vectors, vectors, down, across)


def ffn_kernel(*refs, sizes):
    up_refs, down_refs = refs[: sizes[0]], refs[sizes[0] : sum(sizes)]
    hidden_ref, bias_ref, vector_ref = refs[sum(sizes) : sum(sizes) + 3]
    active_ref, slope_ref, summed_ref, output_ref, total_ref = refs[sum(sizes) + 3 :]
    step = pl.program_id(0)
    up, down = read_weight(up_refs, None), read_weight(down_refs, None)
    pre_act = matmul(hidden_ref[...], up) + bias_ref[pl.ds(step, 1), :]
    active, slope = gelu_parts(pre_act)
    active = to_low(active)
    active_ref[...] = active
    slope_ref[...] = slope
    part = matmul(active, down)

    @pl.when(step == 0)
    def _():
        total_ref[...] = part

    @pl.when(step > 0)
    def _():
        total_ref[...] += part

    @pl.when(step == pl.num_programs(0) - 1)
    def _():
        summed = to_full(hidden_ref[...]) + total_ref[...] + vector_ref[5:6, :]
        summed_ref[...] = summed
        output_ref[...] = to_low(layer_norm(summed, vector_ref[6:7, :], vector_ref[7:8, :]))


def ffn_forward(hidden, weights, up_bias, vectors):
    rows, width = hidden.shape
    steps = len(weights.shares) - 2
    first, first_specs = up_operands_of(weights, steps)
    second, second_specs = weights.operands(steps, None, width, lambda s: 0, steps, lambda s: s)
    block = pl.BlockSpec((rows, width), lambda s: (0, s))
    return pl.pallas_call(
        functools.partial(ffn_kernel, sizes=[len(first), len(second)]),
        grid=(steps,),
        in_specs=[*first_specs, *second_specs, whole(hidden), whole(up_bias), whole(vectors)],
        out_specs=[block, block, whole(hidden), whole(hidden)],
        out_shape=[
            jax.ShapeDtypeStruct((rows, steps * width), jnp.bfloat16),
            jax.ShapeDtypeStruct((rows, steps * width), jnp.float32),
            jax.ShapeDtypeStruct((rows, width), jnp.float32),
            jax.ShapeDtypeStruct((rows, width), jnp.bfloat16),
        ],
        scratch_shapes=[pltpu.VMEM((rows, width), jnp.float32)],
        compiler_params=pltpu.CompilerParams(dimension_semantics=("arbitrary",)),
        name="ffn_forward",
    )(*first, *second, hidden, up_bias, vectors)


def head_kernel(*refs, size):
    weight_refs = refs[:size]
    picker_ref, output_ref, vector_ref, own_ref, dense_ref, normed_ref = refs[size:]
    own = to_low(matmul(picker_ref[...], output_ref[...]))
    own_ref[...] = own
    dense = matmul(own, read_weight(weight_refs, None)) + vector_ref[4:5, :]
    dense_ref[...] = dense
    active = gelu_parts(dense)[0]
    normed_ref[...] = to_low(layer_norm(active, vector_ref[5:6, :], vector_ref[6:7, :]))


def head_forward(picker, output, group, index, vectors):
    slots, width = picker.shape[0], output.shape[1]
    arrays, specs = group.operands(index, None, width, lambda s: 0)
    operands = [picker, output, vectors]
    out_shape = [
        jax.ShapeDtypeStruct((slots, width), kind)
        for kind in (jnp.bfloat16, jnp.float32, jnp.bfloat16)
    ]
    return pl.pallas_call(
        functools.partial(head_kernel, size=len(arrays)),
        grid=(1,),
        in_specs=[*specs, *[whole(operand) for operand in operands]],
        out_specs=[whole(shape) for shape in out_shape],
        out_shape=out_shape,
        name="head_forward",
    )(*arrays, *operands)


def norm_backward(summed, gain_row, grad):
    center = summed - jnp.mean(summed, axis=-1, keepdims=True)
    scale = lax.rsqrt(jnp.mean(center * center, axis=-1, keepdims=True) + EPSILON)
    unit = center * scale
    inner = grad * gain_row
    mean = jnp.mean(inner, axis=-1, keepdims=True)
    along = jnp.mean(inner * unit, axis=-1, keepdims=True)
    gain_grad = jnp.sum(grad * unit, axis=0, keepdims=True)
    shift_grad = jnp.sum(grad, axis=0, keepdims=True)
    return scale * (inner - mean - unit * along), gain_grad, shift_grad


def feed_back_kernel(place, *refs, sizes, share, down_share):
    up_refs, down_refs = refs[: sizes[0]], refs[sizes[0] : sum(sizes)]
    (cotangent_ref, picker_ref, picked_ref, summed_ref, vector_ref, own_ref, dense_ref) = refs[
        sum(sizes) : sum(sizes) + 7
    ]
    hidden_ref, active_ref, slope_ref, total_ref, sums_ref, *outs = refs[sum(sizes) + 7 : -2]
    low_ref, turned_ref = refs[-2:]
    step = pl.program_id(0)
    width = vector_ref.shape[1]

    @pl.when(step == 0)
    def _():
        grad = to_full(cotangent_ref[...]) + matmul_tn(picker_ref[...], picked_ref[...])
        summed_grad, gain_grad, shift_grad = norm_backward(
            summed_ref[...], vector_ref[6:7, :], grad
        )
        total_ref[...] = summed_grad
        low = to_low(summed_grad)
        low_ref[...] = low
        turned_ref[...] = hidden_ref[...].T
        sums_ref[...] = jnp.zeros_like(sums_ref)
        sums_ref[0:1, :] = jnp.sum(to_full(low), axis=0, keepdims=True)
        sums_ref[1:2, :] = gain_grad
        sums_ref[2:3, :] = shift_grad
        dense_grad = to_low(matmul_tn(own_ref[...], dense_ref[...]))
        if down_share:
            store_blocks(outs, dense_grad, place, share, slice(2 * down_share, None))
        else:
            outs[2][...] = dense_grad

    low = low_ref[...]
    up, down = read_weight(up_refs, None), read_weight(down_refs, None)
    down_grad = to_low(matmul_tn(active_ref[...], low))
    pre_grad = to_low(matmul_nt(low, down) * slope_ref[...])
    total_ref[...] += matmul_nt(pre_grad, up)
    sums_ref[pl.ds(3 + step, 1), :] = jnp.sum(to_full(pre_grad), axis=0, keepdims=True)
    up_grad = to_low(matmul(turned_ref[...], pre_grad))
    if down_share:
        chips = width // (2 * down_share)
        rows = slice(down_share, 2 * down_share)
        store_blocks(outs, down_grad, place, down_share, rows, step * chips)
        rows = pl.ds(pl.multiple_of(step * share, share), share)
        store_blocks(outs, up_grad, place, share, rows)
    else:
        outs[0][...] = up_grad
        outs[1][...] = down_grad


def feed_backward(place, count, cotangent, picker, picked_grad, summed, vectors, own, dense, hidden, active, slope, weights):
    rows, width = cotangent.shape
    steps = active.shape[1] // width
    share, down_share, chips = width // count, active.shape[1] // count, count // 2
    aligned = share % 8 == 0
    first, first_specs = up_operands_of(weights, steps)
    second, second_specs = weights.operands(steps, None, width, lambda s, c: 0, steps, lambda s, c: s)
    operands = [cotangent, picker, picked_grad, summed, vectors, own, dense, hidden]
    block = pl.BlockSpec((rows, width), lambda s, c: (0, s))
    low = jnp.bfloat16
    if aligned:
        shape = jax.ShapeDtypeStruct((chips, 2 * down_share + share, width // 2), low)
        out_shape, out_specs = [shape] * 4, [whole(shape)] * 4
    else:
        out_shape = [
            jax.ShapeDtypeStruct((width, steps * width), low),
            jax.ShapeDtypeStruct((steps * width, width), low),
            jax.ShapeDtypeStruct((width, width), low),
        ]
        out_specs = [
            pl.BlockSpec((width, width), lambda s, c: (0, s)),
            pl.BlockSpec((width, width), lambda s, c: (s, 0)),
            whole(out_shape[2]),
        ]
    common = [
        jax.ShapeDtypeStruct((rows, width), jnp.float32),
        jax.ShapeDtypeStruct((8, width), jnp.float32),
    ]
    kernel = functools.partial(
        feed_back_kernel,
        sizes=[len(first), len(second)],
        share=share,
        down_share=down_share if aligned else 0,
    )
    hidden_grad, sums, *outs = pl.pallas_call(
        kernel,
        grid_spec=pltpu.PrefetchScalarGridSpec(
            num_scalar_prefetch=1,
            grid=(steps,),
            in_specs=[
                *first_specs,
                *second_specs,
                *[whole(operand) for operand in operands],
                block,
                block,
            ],
            out_specs=[*[whole(shape) for shape in common], *out_specs],
            scratch_shapes=[pltpu.VMEM((rows, width), low), pltpu.VMEM((width, rows), low)],
        ),
        out_shape=[*common, *out_shape],
        compiler_params=pltpu.CompilerParams(dimension_semantics=("arbitrary",)),
        name="feed_backward",
    )(place, *first, *second, *operands, active, slope)
    if not aligned:
        away, kept = arranged([*column_blocks(outs[0], width), *outs[1:]], place)
    else:
        away, kept = outs[:2], outs[2:]
    return hidden_grad, sums, away, kept


def out_back_kernel(core, *refs, size):
    weight_refs = refs[:size]
    grad_ref, summed_ref, vector_ref, total_ref, low_ref, back_ref, sums_ref = refs[size:]
    width = vector_ref.shape[1]
    summed_grad, gain_grad, shift_grad = norm_backward(
        summed_ref[...], vector_ref[3:4, :], grad_ref[...]
    )
    total_ref[...] = summed_grad
    low = to_low(summed_grad)
    low_ref[...] = low
    bias_grad = jnp.sum(to_full(low), axis=0, keepdims=True)
    zero = jnp.zeros((5, width), jnp.float32)
    sums_ref[...] = jnp.concatenate([bias_grad, gain_grad, shift_grad, zero], axis=0)
    back_ref[...] = to_low(matmul_nt(low, read_weight(weight_refs, core[0])))


def out_backward(core, hidden_grad, summed, vectors, group, index):
    rows, width = hidden_grad.shape
    arrays, specs = group.operands(index, core, width, lambda s, c: 0)
    operands = [hidden_grad, summed, vectors]
    out_shape = [
        jax.ShapeDtypeStruct((rows, width), jnp.float32),
        jax.ShapeDtypeStruct((rows, width), jnp.bfloat16),
        jax.ShapeDtypeStruct((rows, width), jnp.bfloat16),
        jax.ShapeDtypeStruct((8, width), jnp.float32),
    ]
    return pl.pallas_call(
        functools.partial(out_back_kernel, size=len(arrays)),
        grid_spec=pltpu.PrefetchScalarGridSpec(
            num_scalar_prefetch=1,
            grid=(1,),
            in_specs=[*specs, *[whole(operand) for operand in operands]],
            out_specs=[whole(shape) for shape in out_shape],
        ),
        out_shape=out_shape,
        name="out_backward",
    )(core.reshape(1), *arrays, *operands)


def attention_back_kernel(*refs, first_head):
    (grad_ref, q_ref, k_ref, v_ref, total_ref, down_ref, across_ref) = refs[:7]
    dq_ref, dk_ref, dv_ref, sums_ref, mask_ref = refs[7:]
    step = pl.program_id(0)

    @pl.when(step == 0)
    def _():
        mask_ref[...] = jnp.where(down_ref[...] == across_ref[...], 0.0, NEGATIVE)

    pair_width = 2 * HEAD_DIM
    scale = HEAD_DIM ** (-0.5)
    lane = lax.broadcasted_iota(jnp.int32, (1, pair_width), 1)
    columns = q_ref.shape[1]
    heads = columns // HEAD_DIM
    for pair in range(heads // 2):
        span = slice(pair_width * pair, pair_width * (pair + 1))
        queries, keys, values = q_ref[:, span], k_ref[:, span], v_ref[:, span]
        grads = grad_ref[:, span]
        scaled = to_full(queries) * scale
        sides = []
        for side in range(2):
            here = (lane < HEAD_DIM) == (side == 0)
            mine = to_low(jnp.where(here, scaled, 0.0))
            my_grads = jnp.where(here, grads, jnp.zeros_like(grads))
            head = first_head + step * heads + 2 * pair + side
            scores = matmul_nt(keys, mine) + mask_ref[...]
            softmax = jnp.exp(scores - total_ref[pl.ds(head, 1), :])
            softmax_grad = matmul_nt(values, my_grads)
            inner = jnp.sum(softmax * softmax_grad, axis=0, keepdims=True)
            score_grad = to_low(softmax * (softmax_grad - inner))
            query_grad = matmul_tn(keys, score_grad)[HEAD_DIM * side : HEAD_DIM * (side + 1)]
            sides.append((query_grad, matmul(score_grad, mine), matmul(to_low(softmax), my_grads)))
        query_grad = to_low(jnp.concatenate([sides[0][0], sides[1][0]], axis=0).T * scale)
        value_grad = to_low(sides[0][2] + sides[1][2])
        dq_ref[:, span] = query_grad
        dk_ref[:, span] = to_low(sides[0][1] + sides[1][1])
        dv_ref[:, span] = value_grad
        sums_ref[0:1, span] = jnp.sum(to_full(query_grad), axis=0, keepdims=True)
        sums_ref[1:2, span] = jnp.sum(to_full(value_grad), axis=0, keepdims=True)


def attention_backward(context_grad, queries, keys, values, score_total, segments, start, columns):
    rows = context_grad.shape[0]
    size = 2 * HEAD_DIM
    down, across = segments[:, None], segments[None, :]
    block = pl.BlockSpec((rows, size), lambda s: (0, start // size + s))
    out_block = pl.BlockSpec((rows, size), lambda s: (0, s))
    return pl.pallas_call(
        functools.partial(attention_back_kernel, first_head=start // HEAD_DIM),
        grid=(columns // size,),
        in_specs=[*[block] * 4, whole(score_total), whole(down), whole(across)],
        out_specs=[*[out_block] * 3, pl.BlockSpec((8, size), lambda s: (0, s))],
        out_shape=[
            *[jax.ShapeDtypeStruct((rows, columns), jnp.bfloat16)] * 3,
            jax.ShapeDtypeStruct((8, columns), jnp.float32),
        ],
        scratch_shapes=[pltpu.VMEM((rows, rows), jnp.float32)],
        compiler_params=pltpu.CompilerParams(dimension_semantics=("arbitrary",)),
        name="attention_backward",
    )(context_grad, queries, keys, values, score_total, down, across)


def joined_sums(bias_sums, out_sums, feed_sums, head_sums, steps):
    return jnp.concatenate(
        [
            jnp.concatenate([part[:2] for part in bias_sums], axis=1),
            out_sums[:3],
            feed_sums[: 3 + steps],
            head_sums[: 8 - steps],
        ],
        axis=0,
    )


def last_grads_kernel(place, *refs, parts, share, steps):
    tokens_ref, context_ref, branch_ref, out_sums_ref, feed_sums_ref, head_sums_ref, *rest = refs
    mixed_refs, rest = rest[: 3 * parts], rest[3 * parts :]
    bias_refs, outs = rest[:parts], rest[parts:]
    turned = tokens_ref[...].T
    for which in range(3):
        for part in range(parts):
            mixed = mixed_refs[3 * part + which][...]
            columns = mixed.shape[1]
            grad = to_low(matmul(turned, mixed))
            if share:
                rows = slice(share * which, share * (which + 1))
                store_blocks(outs, grad, place, share, rows, column=columns * part)
            else:
                outs[which][:, columns * part : columns * (part + 1)] = grad
    grad = to_low(matmul_tn(context_ref[...], branch_ref[...]))
    if share:
        store_blocks(outs, grad, place, share, slice(3 * share, 4 * share))
        small = to_low(
            joined_sums(
                [ref[...] for ref in bias_refs],
                out_sums_ref[...],
                feed_sums_ref[...],
                head_sums_ref[...],
                steps,
            )
        )
        half = small.shape[1] // 2
        for index, out_ref in enumerate(outs):
            part = small[:, half * (index % 2) : half * (index % 2 + 1)]
            out_ref[:, 4 * share :, :] = jnp.broadcast_to(
                part[None], (out_ref.shape[0], *part.shape)
            )
    else:
        outs[3][...] = grad


def last_grads(place, count, tokens, context, branch_grad, sums, steps, mixed):
    width = tokens.shape[1]
    share, chips = width // count, count // 2
    aligned = share % 8 == 0
    parts = len(mixed)
    biases = [part[3] for part in mixed]
    mixed = [part[:3] for part in mixed]
    operands = [tokens, context, branch_grad, *sums, *[m for part in mixed for m in part], *biases]
    small = joined_sums(biases, *sums, steps)
    if aligned:
        rows = 4 * share + small.shape[0]
        out_shape = [jax.ShapeDtypeStruct((chips, rows, width // 2), jnp.bfloat16)] * 4
    else:
        out_shape = [jax.ShapeDtypeStruct((width, width), jnp.bfloat16)] * 4
    outs = pl.pallas_call(
        functools.partial(
            last_grads_kernel, parts=parts, share=share if aligned else 0, steps=steps
        ),
        grid_spec=pltpu.PrefetchScalarGridSpec(
            num_scalar_prefetch=1,
            grid=(1,),
            in_specs=[whole(operand) for operand in operands],
            out_specs=[whole(shape) for shape in out_shape],
        ),
        out_shape=out_shape,
        name="last_grads",
    )(place, *operands)
    if not aligned:
        both = jnp.broadcast_to(to_low(small)[None], (count, *small.shape))
        return arranged([*outs, both.reshape(-1, width)], place)
    return outs[:2], outs[2:]


def tokens_back_kernel(core, *refs, sizes, parts):
    ends = [sum(sizes[:k]) for k in range(4)]
    weights = [refs[ends[k] : ends[k + 1]] for k in range(3)]
    summed_ref, *mixed_refs, out_ref = refs[ends[3] :]
    total = summed_ref[...]
    for which in range(3):
        weight = read_weight(weights[which], core[0])
        for part in range(parts):
            mixed = mixed_refs[3 * part + which][...]
            columns = mixed.shape[1]
            total += matmul_nt(mixed, weight[:, columns * part : columns * (part + 1)])
    out_ref[...] = total


def tokens_backward(core, summed_grad, mixed, weights):
    width = summed_grad.shape[1]
    arrays, specs, sizes = [], [], []
    for group, index in weights:
        some, their = group.operands(index, core, width, lambda s, c: 0)
        arrays, specs, sizes = arrays + some, specs + their, sizes + [len(some)]
    operands = [summed_grad, *[matrix for part in mixed for matrix in part]]
    return pl.pallas_call(
        functools.partial(tokens_back_kernel, sizes=sizes, parts=len(mixed)),
        grid_spec=pltpu.PrefetchScalarGridSpec(
            num_scalar_prefetch=1,
            grid=(1,),
            in_specs=[*specs, *[whole(operand) for operand in operands]],
            out_specs=whole(summed_grad),
        ),
        out_shape=jax.ShapeDtypeStruct(summed_grad.shape, jnp.float32),
        name="tokens_backward",
    )(core.reshape(1), *arrays, *operands)


def take_kernel(index, whole_ref, *out_refs, plan):
    width = whole_ref.shape[1]
    for out_ref, (first_row, share) in zip(out_refs, plan):
        spot = index[0] * share
        row, place = first_row + spot // width, spot % width
        line = jnp.broadcast_to(whole_ref[pl.ds(row, 1), :], (8, width))
        moved = pltpu.roll(line, lax.rem(width - place, width), 1)
        out_ref[...] = moved[:1, :share]


def take_shares(device, values, first_rows, shares):
    shapes = [jax.ShapeDtypeStruct((1, share), jnp.float32) for share in shares]
    lines = pl.pallas_call(
        functools.partial(take_kernel, plan=list(zip(first_rows, shares))),
        grid_spec=pltpu.PrefetchScalarGridSpec(
            num_scalar_prefetch=1,
            grid=(1,),
            in_specs=[whole(values)],
            out_specs=[whole(shape) for shape in shapes],
        ),
        out_shape=shapes,
        name="take_shares",
    )(device.reshape(1), values)
    return [line[0] for line in lines]


def take(value, axis, index):
    return lax.dynamic_index_in_dim(value, index, axis, keepdims=False)


def add_low(first, second):
    return to_low(to_full(first) + to_full(second))


def halve(value, axis, stride):
    chips = lax.axis_size("dp")
    bit = (lax.axis_index("dp") // stride) % 2
    pairs = [(chip, chip ^ stride) for chip in range(chips)]
    arrived = lax.ppermute(take(value, axis, 1 - bit), "dp", pairs)
    return add_low(take(value, axis, bit), arrived)


def core_swap(away):
    return lax.ppermute(away, "fsdp", [(0, 1), (1, 0)])


def along(sent, stride):
    chips = lax.axis_size("dp")
    return lax.ppermute(sent, "dp", [(chip, chip ^ stride) for chip in range(chips)])


def total_of(addends):
    total = to_full(addends[0])
    for addend in addends[1:]:
        total = total + to_full(addend)
    return total


def my_place():
    chip = lax.axis_index("dp")
    return jnp.stack([lax.axis_index("fsdp"), chip % 2, (chip // 2) % 2, chip // 4])


def chip_at(index, place, levels, first_axis):
    outer, level = index // levels, index % levels
    bits = (outer // 2, outer % 2) if first_axis == 0 else (outer % 2, outer // 2)
    return ((place[3] ^ level) * 2 + (place[2] ^ bits[1])) * 2 + (place[1] ^ bits[0])


def index_of(chip, place, levels, first_axis):
    bits = ((chip % 2) ^ place[1], ((chip // 2) % 2) ^ place[2])
    outer = 2 * bits[first_axis] + bits[1 - first_axis]
    return outer * levels + ((chip // 4) ^ place[3])


class ChipSum:
    def __init__(self, away, kept):
        self.sides = [[part] for part in kept]
        self.strides = [[1, 2], [2, 1]]
        self.arrived = [core_swap(part) for part in away]

    def add(self, arrived):
        for side, part in zip(self.sides, arrived):
            side.append(part)

    def sends(self):
        sent = [to_low(total_of([a[a.shape[0] // 2 :] for a in side])) for side in self.sides]
        self.sides = [[a[: a.shape[0] // 2] for a in side] for side in self.sides]
        return sent

    def start(self, sent):
        self.arrived = [along(part, strides.pop(0)) for part, strides in zip(sent, self.strides)]

    def level_block(self, level):
        return jnp.concatenate(
            [total_of([a[level] for a in side]) for side in self.sides], axis=-1
        )

    def level_sends(self):
        while self.sides[0][0].shape[0] > 4:
            stride = 4 * (self.sides[0][0].shape[0] // 2)
            sent = self.sends()
            self.add([along(part, stride) for part in sent])
        levels = self.sides[0][0].shape[0]
        return [to_low(self.level_block(level)) for level in range(1, levels)]

    def start_levels(self, sent):
        self.arrived = [along(part, 4 * (level + 1)) for level, part in enumerate(sent)]

    def result(self, arrived):
        return total_of([self.level_block(0), *arrived])


def arranged(matrices, place):
    chips = lax.axis_size("dp")
    value = jnp.concatenate(
        [matrix.reshape(chips, 2, -1, matrix.shape[-1]) for matrix in matrices], axis=2
    )
    half = value.shape[-1] // 2
    sides = []
    for core in (1 - place[0], place[0]):
        mine = take(value, 1, core)
        sides.append(
            [
                jnp.take(
                    mine[..., axis * half : (axis + 1) * half],
                    chip_at(jnp.arange(chips), place, chips // 4, axis),
                    axis=0,
                )
                for axis in range(2)
            ]
        )
    return sides


def store_blocks(outs, value, place, share, rows, first_chip=0, column=0):
    columns = value.shape[-1]
    split = value.reshape(-1, 2, share, columns)
    kept, away = in_order(split[:, 0], split[:, 1], place[0])
    levels = outs[0].shape[0] // 4
    width = outs[0].shape[-1]
    for chip in range(split.shape[0]):
        for which, half in enumerate((away, kept)):
            for axis in range(2):
                low, high = max(column, axis * width), min(column + columns, (axis + 1) * width)
                if low >= high:
                    continue
                spot = index_of(first_chip + chip, place, levels, axis)
                outs[2 * which + axis][
                    pl.ds(spot, 1), rows, low - axis * width : high - axis * width
                ] = half[chip : chip + 1, :, low - column : high - column]


def tie(value, *others):
    return lax.optimization_barrier((value, *others))


def window_base(start, total, window):
    return pl.multiple_of(jnp.minimum((start // 16) * 16, total - window), 16)


def compact_kernel(place, places, counts, indices, mine_ref, other_ref, *refs, window, levels):
    step = pl.program_id(0)
    *before, out_ref = refs

    @pl.when(step == 0)
    def _():
        out_ref[...] = before[0][...] if before else jnp.zeros_like(out_ref)

    _, batch, slots, half = mine_ref.shape
    total = out_ref.shape[0]
    for which, ref in enumerate((mine_ref, other_ref)):
        core = place[0] if which == 0 else 1 - place[0]
        for axis in range(2):
            for lane in range(batch):
                index = indices[step * batch + lane]
                source = 2 * chip_at(index, place, levels, axis) + core
                start = places[source]
                base = window_base(start, total, window)
                row = lax.broadcasted_iota(jnp.int32, (window, slots), 0) + (base - start)
                column = lax.broadcasted_iota(jnp.int32, (window, slots), 1)
                chosen = jnp.where((row == column) & (column < counts[source]), 1.0, 0.0)
                moved = matmul(to_low(chosen), ref[axis, lane])
                out_ref[pl.ds(base, window), half * axis : half * (axis + 1)] += to_low(moved)


def compact(place, places, counts, mine, other, indices, total, before=()):
    _, blocks, slots, half = mine.shape
    levels = lax.axis_size("dp") // 4
    batch = blocks // 2 if blocks <= 16 else 2
    block = pl.BlockSpec((2, batch, slots, half), lambda i, *_: (0, i, 0, 0))
    return pl.pallas_call(
        functools.partial(compact_kernel, window=slots + 16, levels=levels),
        grid_spec=pltpu.PrefetchScalarGridSpec(
            num_scalar_prefetch=4,
            grid=(blocks // batch,),
            in_specs=[block, block, *[whole(rows) for rows in before]],
            out_specs=pl.BlockSpec((total, 2 * half), lambda i, *_: (0, 0)),
        ),
        out_shape=jax.ShapeDtypeStruct((total, 2 * half), jnp.bfloat16),
        compiler_params=pltpu.CompilerParams(dimension_semantics=("arbitrary",)),
        name="compact_rows",
    )(place, places, counts, jnp.array(indices, jnp.int32), mine, other, *before)


def compact_labels_kernel(places, counts, lines_ref, out_ref):
    out_ref[...] = jnp.zeros_like(out_ref)
    sources, slots = lines_ref.shape
    total = out_ref.shape[1]
    wide = 2 * slots
    lane = lax.broadcasted_iota(jnp.int32, (8, wide), 1)

    def place_one(source, carry):
        start = places[source]
        base = pl.multiple_of(jnp.minimum(start // slots * slots, total - wide), slots)
        shift = start - base
        line = jnp.broadcast_to(to_full(lines_ref[pl.ds(source, 1), :]), (8, slots))
        line = jnp.concatenate([line, jnp.zeros_like(line)], axis=1)
        moved = pltpu.roll(line, lax.rem(shift, wide), 1)
        here = (lane >= shift) & (lane < shift + counts[source])
        span = pl.ds(base, wide)
        out_ref[:, span] = jnp.where(here, moved, out_ref[:, span])
        return carry

    lax.fori_loop(0, sources, place_one, 0)


def compact_labels(places, counts, lines, total):
    out = pl.pallas_call(
        compact_labels_kernel,
        grid_spec=pltpu.PrefetchScalarGridSpec(
            num_scalar_prefetch=2,
            grid=(1,),
            in_specs=[whole(lines)],
            out_specs=pl.BlockSpec((8, total), lambda *_: (0, 0)),
        ),
        out_shape=jax.ShapeDtypeStruct((8, total), jnp.float32),
        name="compact_labels",
    )(places, counts, lines)
    return out[0].astype(jnp.int32)


def block_order():
    levels = lax.axis_size("dp") // 4
    near = [*range(levels), *range(2 * levels, 3 * levels), levels, 3 * levels]
    return near, [k for k in range(4 * levels) if k not in near]


def gather_blocks(value, beside, given):
    chips = lax.axis_size("dp")
    levels = chips // 4
    half = value.shape[-1] // 2
    if levels <= 4:
        others = jnp.stack([along(value, 4 * level) for level in range(1, levels)])
    else:
        others = value[None]
        while others.shape[0] < levels:
            others = jnp.concatenate([others, along(others, 4 * others.shape[0])])
        others = others[1:]
    own = [value[:, :half], value[:, half:]]
    strides = [(1, 2), (2, 1)]
    near = [along(part, first) for part, (first, _) in zip(own, strides)]
    far_sent = [jnp.stack([part, got]) for part, got in zip(own, near)]
    others = tie(others, *far_sent)[0]
    far = [along(sent, second) for sent, (_, second) in zip(far_sent, strides)]
    rest = [others[..., :half], others[..., half:]]
    near_rest = [along(part, first) for part, (first, _) in zip(rest, strides)]
    given, *near_rest = tie(given, *near_rest)
    far_rest = [
        along(jnp.concatenate([part, got]), second)
        for part, got, (_, second) in zip(rest, near_rest, strides)
    ]
    early = jnp.stack(
        [
            jnp.concatenate([own[k][None], rest[k], near[k][None], near_rest[k], far[k]])
            for k in range(2)
        ]
    )
    results = beside(early, core_swap(early), given)
    tied = tie(*far_rest, *results)
    late = jnp.stack(tied[:2])
    return late, core_swap(late), tied[2:]


def spread_kernel(place, places, counts, rows_ref, *out_refs, window):
    step = pl.program_id(0)
    total = rows_ref.shape[0]
    batch, slots, half = out_refs[0].shape
    levels = pl.num_programs(0) * batch // 4
    for which in range(2):
        core = 1 - place[0] if which == 0 else place[0]
        for axis in range(2):
            for lane in range(batch):
                chip = chip_at(step * batch + lane, place, levels, axis)
                source = 2 * chip + core
                start = places[source]
                base = window_base(start, total, window)
                row = lax.broadcasted_iota(jnp.int32, (slots, window), 0)
                column = lax.broadcasted_iota(jnp.int32, (slots, window), 1) + (base - start)
                chosen = jnp.where((row == column) & (row < counts[source]), 1.0, 0.0)
                moved = matmul(
                    to_low(chosen), rows_ref[pl.ds(base, window), half * axis : half * (axis + 1)]
                )
                out_refs[2 * which + axis][lane] = to_low(moved)


def spread(place, places, counts, rows, slots):
    chips = places.shape[0] // 2
    total, width = rows.shape
    batch = 2
    block = pl.BlockSpec((batch, slots, width // 2), lambda i, *_: (i, 0, 0))
    shape = jax.ShapeDtypeStruct((chips, slots, width // 2), jnp.bfloat16)
    outs = pl.pallas_call(
        functools.partial(spread_kernel, window=slots + 16),
        grid_spec=pltpu.PrefetchScalarGridSpec(
            num_scalar_prefetch=3,
            grid=(chips // batch,),
            in_specs=[
                pl.BlockSpec((total, width), lambda i, *_: (0, 0), pipeline_mode=pl.Buffered(1))
            ],
            out_specs=[block] * 4,
        ),
        out_shape=[shape] * 4,
        compiler_params=pltpu.CompilerParams(dimension_semantics=("arbitrary",)),
        name="spread_rows",
    )(place, places, counts, rows)
    return outs[:2], outs[2:]


def per_device(
    tokens,
    segments,
    mask_flags,
    targets,
    cotangent,
    qkv_weight,
    attn_bias,
    out_weight,
    out_bias,
    attn_gain,
    attn_shift,
    up_weight,
    up_bias,
    down_weight,
    down_bias,
    ffn_gain,
    ffn_shift,
    dense_weight,
    dense_bias,
    head_gain,
    head_shift,
    decoder,
    vocab_bias,
):
    count = lax.axis_size(AXES)
    width = tokens.shape[1]
    core = lax.axis_index("fsdp")
    device = lax.axis_index(AXES)
    here = my_place()
    blocks = qkv_weight.shape[1] // width
    steps = up_weight.shape[1] // width
    share, up_share, down_share = out_weight.shape[0], up_weight.shape[0], down_weight.shape[0]
    label_place = up_share * steps + down_share + share
    later_packed = pack_later(
        [
            (up_weight, [up_share * k for k in range(steps)]),
            (down_weight, [up_share * steps]),
            (dense_weight, [up_share * steps + down_share]),
        ],
        mask_flags,
        targets,
    )
    later_gathered = lax.all_gather(later_packed, AXES, axis=0)
    later = Weights([later_gathered], [*[up_share] * steps, down_share, share])
    small = (
        attn_bias,
        out_bias,
        attn_gain,
        attn_shift,
        down_bias,
        ffn_gain,
        ffn_shift,
        up_bias,
        dense_bias,
        head_gain,
        head_shift,
    )
    small_rows = (0, 2, 3, 4, 5, 6, 7, 8, 12, 13, 14)
    placed = place_shares(device, small, small_rows, 16, width)
    half = 2 * share + 8
    first_packed = pack_rows(
        [
            (qkv_weight, [0, share, half]),
            (placed[:8], [2 * share]),
            (out_weight, [half + share]),
            (placed[8:], [half + 2 * share]),
        ]
    )
    upper, lower = gather_pair(first_packed, half)
    first_group, second_group = (Weights(list(pair), [share, share, 8]) for pair in (upper, lower))
    vectors, more_vectors = (
        sum(jnp.sum(to_full(array[:, 2 * share :]), axis=0) for array in pair)
        for pair in (upper, lower)
    )
    queries, keys_low, values_low, context, score_total, summed1, hidden = attention_forward(
        core,
        tokens,
        segments,
        [(first_group, 0), (first_group, 1), (second_group, 0), (second_group, 1)],
        vectors,
    )
    active, slope, summed2, output = ffn_forward(hidden, later, more_vectors[:4], vectors)
    head_gain_full, head_shift_full = more_vectors[5], more_vectors[6]
    mask_rank = jnp.cumsum(mask_flags) - 1
    slot_place = jnp.where(mask_flags > 0, mask_rank, -1)
    picker_low = (jnp.arange(MAXM)[:, None] == slot_place[None, :]).astype(jnp.bfloat16)
    own_rows, dense, normed_low = head_forward(picker_low, output, later, steps + 1, more_vectors)
    _, tail_back = jax.vjp(head_tail, dense, head_gain_full, head_shift_full)
    chips = count // 2
    group = MASK_DEV * chips
    total = 2 * group
    gathered_late, normed_low = tie(later_gathered, normed_low)
    label_parts = gathered_late[:, label_place : label_place + 2, :MAXM].astype(jnp.int32)
    label_lines = label_parts[:, 0] * 256 + label_parts[:, 1] - 1
    counts = jnp.sum((label_lines >= 0).astype(jnp.int32), axis=1)
    by_core = counts.reshape(chips, 2)
    earlier = jnp.arange(chips)[:, None] < jnp.arange(chips)[None, :]
    places = jnp.sum(jnp.where(earlier[:, :, None], by_core[:, None, :], 0), axis=0)
    places = (places + jnp.arange(2)[None, :] * group).reshape(count)
    all_labels = compact_labels(places, counts, label_lines, total)
    slice_index = lax.axis_index(AXES)
    vocab_rows = decoder.shape[0]
    local_label = all_labels - slice_index * vocab_rows
    label_hit = jnp.arange(vocab_rows)[None, :] == local_label[:, None]

    early_order, late_order = block_order()

    def beside_last(mine, other, chosen):
        hit = jnp.arange(vocab_rows)[None, :] == chosen[:, None]
        pulled = to_low(matmul(hit.astype(jnp.bfloat16), decoder))
        return compact(here, places, counts, mine, other, early_order, total), pulled

    mine, other, (early_rows, label_pull) = gather_blocks(normed_low, beside_last, local_label)
    late = (here, places, counts, mine, other, late_order, total)
    small_total = total <= 4096
    all_rows = compact(*late, (early_rows,)) if small_total else early_rows + compact(*late)
    logits = matmul_nt(all_rows, decoder) + to_full(vocab_bias)
    row_peak = jnp.max(logits, axis=1)
    exp_sums = jnp.sum(jnp.exp(logits - row_peak[:, None]), axis=1)
    label_sum = jnp.sum(jnp.where(label_hit, logits, 0.0))
    local_total = (row_peak + jnp.log(exp_sums)).reshape(-1, 128)
    lines = local_total.shape[0]
    merged = jnp.concatenate(
        [local_total, jnp.pad(label_sum[None, None], ((0, 7), (0, 127)))], axis=0
    )
    is_total = jnp.arange(lines + 8)[:, None] < lines
    middle = total // 2
    pulls = []
    rounds = [[1], [2, 4, 6]]
    rounds += [[8, 16, 24]] if count == 32 else [[8 << k] for k in range((count // 8).bit_length() - 1)]
    for distances in rounds:
        arrived = [
            lax.ppermute(merged, AXES, [(place, place ^ far) for place in range(count)])
            for far in distances
        ]
        if len(pulls) < 2:
            rows = slice(middle * len(pulls), middle * (len(pulls) + 1))
            pull = matmul(to_low(jnp.exp(logits[rows] - row_peak[rows, None])), decoder)
            *arrived, pull = tie(*arrived, pull)
            pulls.append(pull)
        every = [merged, *arrived]
        peak = functools.reduce(jnp.maximum, every)
        both = peak + jnp.log(sum(jnp.exp(part - peak) for part in every))
        merged = jnp.where(is_total, both, sum(every))
    log_total = merged[:lines].reshape(total)
    mean_loss = (jnp.sum(log_total) - merged[lines, 0]) / total
    scale = jnp.exp(row_peak - log_total)[:, None]
    rows_part = jnp.concatenate(
        [
            to_low(pull * scale[rows] - to_full(label_pull[rows]))
            for pull, rows in zip(pulls, (slice(0, middle), slice(middle, total)))
        ]
    )
    rows_sum = ChipSum(*spread(here, places, counts, rows_part, MAXM))
    rows_sum.add(rows_sum.arrived)
    rows_sum.start(rows_sum.sends())
    logit_grad = to_low(jnp.exp(logits - log_total[:, None]) - label_hit.astype(jnp.float32))
    vocab_bias_grad = jnp.sum(to_full(logit_grad), axis=0)
    logit_grad, vocab_bias_grad, *arrived = tie(logit_grad, vocab_bias_grad, *rows_sum.arrived)
    rows_sum.add(arrived)
    rows_sum.start(rows_sum.sends())
    decoder_grad = matmul_tn(logit_grad, all_rows)
    decoder_grad, *arrived = tie(decoder_grad, *rows_sum.arrived)
    rows_sum.add(arrived)
    rows_sum.start_levels(rows_sum.level_sends())
    normed_grad = rows_sum.result(rows_sum.arrived)
    dense_grad, head_gain_grad, head_shift_grad = tail_back(normed_grad)
    dense_grad_low = to_low(dense_grad)
    dense_bias_grad = jnp.sum(to_full(dense_grad_low), axis=0)
    dense_full = Weights([gathered_late], later.shares).natural(steps + 1, None)
    picked_grad = to_low(matmul_nt(dense_grad_low, dense_full))
    hidden_grad, feed_sums, *feed_grads = feed_backward(
        here,
        count,
        cotangent,
        picker_low,
        picked_grad,
        summed2,
        vectors,
        own_rows,
        dense_grad_low,
        hidden,
        active,
        slope,
        later,
    )
    first = ChipSum(*feed_grads)
    summed1_grad, branch1_grad, context_grad, out_sums = out_backward(
        core, hidden_grad, summed1, vectors, second_group, 1
    )
    context_grad, *arrived = tie(context_grad, *first.arrived)
    first.add(arrived)
    context_grad, *sent = tie(context_grad, *first.sends())
    first.start(sent)
    saved = (queries, keys_low, values_low, score_total, segments)
    middle = width // 2
    mixed = [list(attention_backward(context_grad, *saved, 0, middle))]
    mixed[0][0], context_grad = tie(mixed[0][0], context_grad)
    mixed.append(list(attention_backward(context_grad, *saved, middle, width - middle)))
    head_sums = jnp.stack(
        [dense_bias_grad, head_gain_grad, head_shift_grad, *[jnp.zeros((width,))] * 5]
    )
    away, kept = last_grads(
        here, count, tokens, context, branch1_grad, (out_sums, feed_sums, head_sums), steps, mixed
    )
    mixed = [part[:3] for part in mixed]
    second = ChipSum(away, kept)
    mixed[0][0], _, *arrived = tie(mixed[0][0], away[0], *first.arrived)
    first.add(arrived)
    mixed[0][0], *sent = tie(mixed[0][0], *first.sends())
    first.start(sent)
    mixed[0][0], *arrived = tie(mixed[0][0], *second.arrived)
    second.add(arrived)
    mixed[0][0], *sent = tie(mixed[0][0], *second.sends())
    second.start(sent)
    tokens_grad = tokens_backward(
        core, summed1_grad, mixed, [(first_group, 0), (first_group, 1), (second_group, 0)]
    )
    first.add(first.arrived)
    first.start_levels(first.level_sends())
    second.add(second.arrived)
    second.start(second.sends())
    second.add(second.arrived)
    second.start_levels(second.level_sends())
    first, second = first.result(first.arrived), second.result(second.arrived)
    up_pieces = [first[share * k : share * (k + 1)] for k in range(steps)]
    down_piece = first[up_share * steps : up_share * steps + down_share]
    dense_piece = first[up_share * steps + down_share :]
    qkv_pieces = [second[share * k : share * (k + 1)] for k in range(blocks)]
    out_piece = second[share * blocks : share * (blocks + 1)]
    small_pieces = take_shares(
        device, second[share * (blocks + 1) :], small_rows, [vector.shape[0] for vector in small]
    )
    return (
        output,
        mean_loss,
        tokens_grad,
        jnp.concatenate(qkv_pieces, axis=1),
        small_pieces[0],
        out_piece,
        *small_pieces[1:4],
        jnp.concatenate(up_pieces, axis=1),
        small_pieces[7],
        down_piece,
        *small_pieces[4:7],
        dense_piece,
        *small_pieces[8:],
        decoder_grad,
        vocab_bias_grad,
    )


def solution(mesh):
    matrix_spec = P(AXES, None)
    vector_spec = P(AXES)
    m, v = matrix_spec, vector_spec
    return jax.shard_map(
        per_device,
        mesh=mesh,
        in_specs=(m, v, v, v, m, m, v, m, v, v, v, m, v, m, v, v, v, m, v, v, v, m, v),
        out_specs=(m, P(), m, m, v, m, v, v, v, m, v, m, v, v, v, m, v, v, v, m, v),
        check_vma=False,
    )
```

```python
import functools

import jax
import jax.numpy as jnp
from jax import lax
from jax.experimental import pallas as pl
from jax.experimental.pallas import tpu as pltpu
from jax.sharding import PartitionSpec as P

HEADS = 12
HEAD_DIM = 64
MASK_DEV = 64
MAXM = 128

EPSILON = 1e-05
NEGATIVE = -1e30
AXES = ("dp", "fsdp")


def to_low(values):
    return values.astype(jnp.bfloat16)


def to_full(values):
    return values.astype(jnp.float32)


def layer_norm(values, gain_vector, shift_vector):
    center = values - jnp.mean(values, axis=-1, keepdims=True)
    spread = jnp.mean(center * center, axis=-1, keepdims=True)
    return center * lax.rsqrt(spread + EPSILON) * gain_vector + shift_vector


def gelu_exact(values):
    return jax.nn.gelu(values, approximate=False)


def head_tail(dense_out, gain_vector, shift_vector):
    return layer_norm(gelu_exact(dense_out), gain_vector, shift_vector)


def matmul(left_side, right_side):
    return jnp.dot(left_side, right_side, preferred_element_type=jnp.float32)


def matmul_tn(left_side, right_side):
    return lax.dot_general(
        left_side, right_side, (((0,), (0,)), ((), ())), preferred_element_type=jnp.float32
    )


def matmul_nt(left_side, right_side):
    return lax.dot_general(
        left_side, right_side, (((1,), (1,)), ((), ())), preferred_element_type=jnp.float32
    )


def column_blocks(matrix, width):
    return [matrix[:, k : k + width] for k in range(0, matrix.shape[1], width)]


def gelu_parts(values):
    size = jnp.abs(values) * 0.7071067811865476
    ratio = 1.0 / (1.0 + 0.3275911 * size)
    bell = jnp.exp(-0.5 * values * values)
    series = 1.421413741 + ratio * (-1.453152027 + ratio * 1.061405429)
    series = ratio * (0.254829592 + ratio * (-0.284496736 + ratio * series))
    tail = 0.5 * series * bell
    below = jnp.where(values < 0, tail, 1.0 - tail)
    return values * below, below + values * bell * 0.3989422804014327


def flat_rows(value):
    return value.reshape(-1, value.shape[-1])


def whole(array):
    return pl.BlockSpec(array.shape, lambda *_: (0,) * array.ndim)


class Weights:
    def __init__(self, arrays, shares):
        self.arrays = arrays
        self.starts = [sum(shares[:k]) for k in range(len(shares))]
        self.shares = shares

    def natural(self, index, core):
        span = slice(self.starts[index], self.starts[index] + self.shares[index])
        pieces = [array[:, span] for array in self.arrays]
        if len(pieces) == 2:
            pieces = [jnp.stack(in_order(*pieces, core), axis=1)]
        return flat_rows(pieces[0].reshape(-1, *pieces[0].shape[-2:]))

    def operands(self, index, core, columns, column_map, parts=1, part_map=lambda *_: 0):
        share, start = self.shares[index], self.starts[index]
        if share % 8 or start % share:
            array = self.natural(index, core)
            rows = array.shape[0] // parts
            spec = pl.BlockSpec((rows, columns), lambda *i: (part_map(*i), column_map(*i)))
            return [array], [spec]
        place = start // share
        specs = [
            pl.BlockSpec(
                (array.shape[0] // parts, share, columns),
                lambda *i: (part_map(*i), place, column_map(*i)),
            )
            for array in self.arrays
        ]
        return list(self.arrays), specs


def up_operands_of(weights, steps):
    share = weights.shares[0]
    width = weights.arrays[0].shape[-1]
    if share % 8:
        array = jnp.concatenate([weights.natural(k, None) for k in range(steps)], axis=1)
        return [array], [pl.BlockSpec((array.shape[0], width), lambda s, *_: (0, s))]
    array = weights.arrays[0]
    return [array], [pl.BlockSpec((array.shape[0], share, width), lambda s, *_: (0, s, 0))]


def in_order(mine, other, core):
    return jnp.where(core == 0, mine, other), jnp.where(core == 0, other, mine)


def read_weight(refs, core):
    if len(refs) == 1:
        return flat_rows(refs[0][...])
    return flat_rows(jnp.stack(in_order(refs[0][...], refs[1][...], core), axis=1))


def pack_kernel(*refs, layout):
    *sources, out_ref = refs
    for source, (column, row, rows, columns) in zip(sources, layout):
        for k in range(column):
            out_ref[row[k] : row[k] + rows, :] = source[:, k * columns : (k + 1) * columns]


def pack_rows(pieces):
    width = pieces[0][0].shape[1] // len(pieces[0][1])
    total = max(row + m.shape[0] for m, rows in pieces for row in rows)
    if any(row % 8 for _, rows in pieces for row in rows):
        placed = sorted(
            (row, m[:, k * width : (k + 1) * width])
            for m, rows in pieces
            for k, row in enumerate(rows)
        )
        return jnp.concatenate([block for _, block in placed], axis=0)
    matrices = [m for m, _ in pieces]
    layout = [(len(rows), tuple(rows), m.shape[0], width) for m, rows in pieces]
    return pl.pallas_call(
        functools.partial(pack_kernel, layout=layout),
        grid=(1,),
        in_specs=[whole(m) for m in matrices],
        out_specs=pl.BlockSpec((total, width), lambda i: (0, 0)),
        out_shape=jax.ShapeDtypeStruct((total, width), matrices[0].dtype),
        name="pack_rows",
    )(*matrices)


def pack_later_kernel(flags_ref, targets_ref, *refs, layout, label_place):
    *sources, out_ref = refs
    pack_kernel(*sources, out_ref, layout=layout)
    count = flags_ref.shape[1]
    flags = jnp.broadcast_to(flags_ref[...], (8, count))
    row = lax.broadcasted_iota(jnp.int32, (count, count), 0)
    column = lax.broadcasted_iota(jnp.int32, (count, count), 1)
    until = to_low(jnp.where(row <= column, 1.0, 0.0))
    rank = matmul(to_low(flags.astype(jnp.float32)), until)[:1] - 1.0
    slot = lax.broadcasted_iota(jnp.int32, (MAXM, count), 0).astype(jnp.float32)
    picker = to_low(jnp.where((slot == rank) & (flags_ref[...] > 0), 1.0, 0.0))
    shifted = targets_ref[...] + 1
    high = lax.shift_right_logical(shifted, 8)
    level = lax.broadcasted_iota(jnp.int32, (8, count), 0)
    halves = jnp.where(level == 0, high, jnp.where(level == 1, shifted - high * 256, 0))
    labels = matmul_nt(to_low(halves.astype(jnp.float32)), picker)
    empty = jnp.zeros((8, out_ref.shape[1] - MAXM), jnp.float32)
    out_ref[label_place : label_place + 8, :] = to_low(jnp.concatenate([labels, empty], axis=1))


def pack_later(pieces, mask_flags, targets):
    width = pieces[0][0].shape[1] // len(pieces[0][1])
    label_place = max(row + m.shape[0] for m, rows in pieces for row in rows)
    if any(row % 8 for _, rows in pieces for row in rows) or label_place % 8:
        rank = jnp.cumsum(mask_flags) - 1
        picker = (jnp.arange(MAXM)[:, None] == rank[None, :]) & (mask_flags > 0)[None, :]
        shifted = jnp.sum(jnp.where(picker, targets[None, :] + 1, 0), axis=1)
        labels = jnp.stack([shifted // 256, shifted % 256]).astype(jnp.bfloat16)
        labels = jnp.pad(labels, ((0, 6), (0, width - MAXM)))
        return pack_rows([*pieces, (labels, [label_place])])
    matrices = [m for m, _ in pieces]
    layout = [(len(rows), tuple(rows), m.shape[0], width) for m, rows in pieces]
    operands = [mask_flags[None], targets[None], *matrices]
    return pl.pallas_call(
        functools.partial(pack_later_kernel, layout=layout, label_place=label_place),
        grid=(1,),
        in_specs=[whole(operand) for operand in operands],
        out_specs=pl.BlockSpec((label_place + 8, width), lambda i: (0, 0)),
        out_shape=jax.ShapeDtypeStruct((label_place + 8, width), matrices[0].dtype),
        name="pack_later",
    )(*operands)


def place_kernel(index, line_ref, out_ref, *, plan):
    rows, width = out_ref.shape
    device = index[0]
    line = jnp.broadcast_to(line_ref[...], (8, width))
    lane = lax.broadcasted_iota(jnp.int32, (rows, width), 1)
    level = lax.broadcasted_iota(jnp.int32, (rows, width), 0)
    out = jnp.zeros((rows, width), jnp.float32)
    for first_row, start, share in plan:
        spot = device * share
        row, place = first_row + spot // width, spot % width
        moved = pltpu.roll(line, lax.rem(place - start + width, width), 1)
        here = (level == row) & (lane >= place) & (lane < place + share)
        out = jnp.where(here, jnp.broadcast_to(moved[:1], (rows, width)), out)
    out_ref[...] = out.astype(out_ref.dtype)


def place_shares(device, vectors, first_rows, rows, width):
    plan = []
    line = 0.0
    start = 0
    for vector, first_row in zip(vectors, first_rows):
        end = start + vector.shape[0]
        plan.append((first_row, start, vector.shape[0]))
        line = line + jnp.pad(to_full(vector), (start, width - end))
        start = end
    line = line[None, :]
    return pl.pallas_call(
        functools.partial(place_kernel, plan=plan),
        grid_spec=pltpu.PrefetchScalarGridSpec(
            num_scalar_prefetch=1,
            grid=(1,),
            in_specs=[whole(line)],
            out_specs=pl.BlockSpec((rows, width), lambda i, d: (0, 0)),
        ),
        out_shape=jax.ShapeDtypeStruct((rows, width), jnp.bfloat16),
        name="place_shares",
    )(device.reshape(1), line)


def double(value, stride, axis):
    chips = lax.axis_size("dp")
    bit = (lax.axis_index("dp") // stride) % 2
    arrived = lax.ppermute(value, "dp", [(chip, chip ^ stride) for chip in range(chips)])
    low, high = in_order(value, arrived, bit)
    return jnp.stack([low, high], axis=axis)


def gather_pair(value, split):
    chips = lax.axis_size("dp")
    stride = 4
    value = value[None]
    while stride < chips:
        value = double(value, stride, 0)
        value = value.reshape(-1, *value.shape[2:])
        stride *= 2
    upper, lower = value[:, :split], value[:, split:]
    upper, lower = double(upper, 1, 1), double(lower, 2, 1)
    upper, lower = double(upper, 2, 1), double(lower, 1, 2)
    upper, lower = (part.reshape(chips, *part.shape[-2:]) for part in (upper, lower))
    swap = [(0, 1), (1, 0)]
    return (upper, lax.ppermute(upper, "fsdp", swap)), (lower, lax.ppermute(lower, "fsdp", swap))


def attention_kernel(core, *refs, sizes):
    ends = [0]
    for size in sizes:
        ends.append(ends[-1] + size)
    weights = [refs[ends[k] : ends[k + 1]] for k in range(len(sizes))]
    (tokens_ref, bias_ref, vector_ref, down_ref, across_ref) = refs[ends[-1] : ends[-1] + 5]
    (q_ref, k_ref, v_ref, context_ref, total_ref, summed_ref, hidden_ref) = refs[ends[-1] + 5 : -2]
    mask_ref, all_ref = refs[-2:]
    step = pl.program_id(0)

    @pl.when(step == 0)
    def _():
        mask_ref[...] = jnp.where(down_ref[...] == across_ref[...], 0.0, NEGATIVE)

    tokens = tokens_ref[...]
    queries = to_low(matmul(tokens, read_weight(weights[0], core[0])) + bias_ref[0:1, :])
    keys = to_low(matmul(tokens, read_weight(weights[1], core[0])))
    values = to_low(matmul(tokens, read_weight(weights[2], core[0])) + bias_ref[1:2, :])
    q_ref[...], k_ref[...], v_ref[...] = queries, keys, values
    heads = queries.shape[1] // HEAD_DIM
    pair_width = 2 * HEAD_DIM
    lane = lax.broadcasted_iota(jnp.int32, (1, pair_width), 1)
    for pair in range(heads // 2):
        span = slice(pair_width * pair, pair_width * (pair + 1))
        scaled = to_full(queries[:, span]) * HEAD_DIM ** (-0.5)
        sides = []
        for side in range(2):
            mine = to_low(jnp.where((lane < HEAD_DIM) == (side == 0), scaled, 0.0))
            scores = matmul_nt(keys[:, span], mine) + mask_ref[...]
            peak = jnp.max(scores, axis=0, keepdims=True)
            exponent = jnp.exp(scores - peak)
            total = jnp.sum(exponent, axis=0, keepdims=True)
            total_ref[pl.ds(step * heads + 2 * pair + side, 1), :] = peak + jnp.log(total)
            softmax_low = to_low(exponent * (1.0 / total))
            mixed = matmul_tn(values[:, span], softmax_low)
            sides.append(mixed[HEAD_DIM * side : HEAD_DIM * (side + 1)])
        context = to_low(jnp.concatenate(sides, axis=0).T)
        context_ref[:, span] = context
        all_ref[step * (heads // 2) + pair] = context

    @pl.when(step == pl.num_programs(0) - 1)
    def _():
        pairs = all_ref.shape[0]
        context = jnp.concatenate([all_ref[k] for k in range(pairs)], axis=1)
        product = matmul(context, read_weight(weights[3], core[0]))
        summed = to_full(tokens_ref[...]) + product + vector_ref[2:3, :]
        summed_ref[...] = summed
        hidden_ref[...] = to_low(layer_norm(summed, vector_ref[3:4, :], vector_ref[4:5, :]))


def attention_forward(core, tokens, segments, weights, vectors):
    rows, width = tokens.shape
    columns = 256
    arrays, specs, sizes = [], [], []
    for k, (group, index) in enumerate(weights):
        size, place = (columns, lambda s, c: s) if k < 3 else (width, lambda s, c: 0)
        some, their = group.operands(index, core, size, place)
        arrays, specs, sizes = arrays + some, specs + their, sizes + [len(some)]
    down, across = segments[:, None], segments[None, :]
    block = pl.BlockSpec((rows, columns), lambda s, c: (0, s))
    head_rows = 16
    return pl.pallas_call(
        functools.partial(attention_kernel, sizes=sizes),
        grid_spec=pltpu.PrefetchScalarGridSpec(
            num_scalar_prefetch=1,
            grid=(width // columns,),
            in_specs=[
                *specs,
                whole(tokens),
                pl.BlockSpec((8, columns), lambda s, c: (0, s)),
                whole(vectors),
                whole(down),
                whole(across),
            ],
            out_specs=[
                block,
                block,
                block,
                block,
                pl.BlockSpec((head_rows, rows), lambda s, c: (0, 0)),
                whole(tokens),
                whole(tokens),
            ],
            scratch_shapes=[
                pltpu.VMEM((rows, rows), jnp.float32),
                pltpu.VMEM((width // (2 * HEAD_DIM), rows, 2 * HEAD_DIM), jnp.bfloat16),
            ],
        ),
        out_shape=[
            *[jax.ShapeDtypeStruct((rows, width), jnp.bfloat16)] * 4,
            jax.ShapeDtypeStruct((head_rows, rows), jnp.float32),
            jax.ShapeDtypeStruct((rows, width), jnp.float32),
            jax.ShapeDtypeStruct((rows, width), jnp.bfloat16),
        ],
        compiler_params=pltpu.CompilerParams(dimension_semantics=("arbitrary",)),
        name="attention_forward",
    )(core.reshape(1), *arrays, tokens, vectors, vectors, down, across)


def ffn_kernel(*refs, sizes):
    up_refs, down_refs = refs[: sizes[0]], refs[sizes[0] : sum(sizes)]
    hidden_ref, bias_ref, vector_ref = refs[sum(sizes) : sum(sizes) + 3]
    active_ref, slope_ref, summed_ref, output_ref, total_ref = refs[sum(sizes) + 3 :]
    step = pl.program_id(0)
    up, down = read_weight(up_refs, None), read_weight(down_refs, None)
    pre_act = matmul(hidden_ref[...], up) + bias_ref[pl.ds(step, 1), :]
    active, slope = gelu_parts(pre_act)
    active = to_low(active)
    active_ref[...] = active
    slope_ref[...] = slope
    part = matmul(active, down)

    @pl.when(step == 0)
    def _():
        total_ref[...] = part

    @pl.when(step > 0)
    def _():
        total_ref[...] += part

    @pl.when(step == pl.num_programs(0) - 1)
    def _():
        summed = to_full(hidden_ref[...]) + total_ref[...] + vector_ref[5:6, :]
        summed_ref[...] = summed
        output_ref[...] = to_low(layer_norm(summed, vector_ref[6:7, :], vector_ref[7:8, :]))


def ffn_forward(hidden, weights, up_bias, vectors):
    rows, width = hidden.shape
    steps = len(weights.shares) - 2
    first, first_specs = up_operands_of(weights, steps)
    second, second_specs = weights.operands(steps, None, width, lambda s: 0, steps, lambda s: s)
    block = pl.BlockSpec((rows, width), lambda s: (0, s))
    return pl.pallas_call(
        functools.partial(ffn_kernel, sizes=[len(first), len(second)]),
        grid=(steps,),
        in_specs=[*first_specs, *second_specs, whole(hidden), whole(up_bias), whole(vectors)],
        out_specs=[block, block, whole(hidden), whole(hidden)],
        out_shape=[
            jax.ShapeDtypeStruct((rows, steps * width), jnp.bfloat16),
            jax.ShapeDtypeStruct((rows, steps * width), jnp.float32),
            jax.ShapeDtypeStruct((rows, width), jnp.float32),
            jax.ShapeDtypeStruct((rows, width), jnp.bfloat16),
        ],
        scratch_shapes=[pltpu.VMEM((rows, width), jnp.float32)],
        compiler_params=pltpu.CompilerParams(dimension_semantics=("arbitrary",)),
        name="ffn_forward",
    )(*first, *second, hidden, up_bias, vectors)


def head_kernel(*refs, size):
    weight_refs = refs[:size]
    picker_ref, output_ref, vector_ref, own_ref, dense_ref, normed_ref = refs[size:]
    own = to_low(matmul(picker_ref[...], output_ref[...]))
    own_ref[...] = own
    dense = matmul(own, read_weight(weight_refs, None)) + vector_ref[4:5, :]
    dense_ref[...] = dense
    active = gelu_parts(dense)[0]
    normed_ref[...] = to_low(layer_norm(active, vector_ref[5:6, :], vector_ref[6:7, :]))


def head_forward(picker, output, group, index, vectors):
    slots, width = picker.shape[0], output.shape[1]
    arrays, specs = group.operands(index, None, width, lambda s: 0)
    operands = [picker, output, vectors]
    out_shape = [
        jax.ShapeDtypeStruct((slots, width), kind)
        for kind in (jnp.bfloat16, jnp.float32, jnp.bfloat16)
    ]
    return pl.pallas_call(
        functools.partial(head_kernel, size=len(arrays)),
        grid=(1,),
        in_specs=[*specs, *[whole(operand) for operand in operands]],
        out_specs=[whole(shape) for shape in out_shape],
        out_shape=out_shape,
        name="head_forward",
    )(*arrays, *operands)


def norm_backward(summed, gain_row, grad):
    center = summed - jnp.mean(summed, axis=-1, keepdims=True)
    scale = lax.rsqrt(jnp.mean(center * center, axis=-1, keepdims=True) + EPSILON)
    unit = center * scale
    inner = grad * gain_row
    mean = jnp.mean(inner, axis=-1, keepdims=True)
    along = jnp.mean(inner * unit, axis=-1, keepdims=True)
    gain_grad = jnp.sum(grad * unit, axis=0, keepdims=True)
    shift_grad = jnp.sum(grad, axis=0, keepdims=True)
    return scale * (inner - mean - unit * along), gain_grad, shift_grad


def feed_back_kernel(place, *refs, sizes, share, down_share):
    up_refs, down_refs = refs[: sizes[0]], refs[sizes[0] : sizes[0] + sizes[1]]
    head_refs = refs[sizes[0] + sizes[1] : sum(sizes)]
    (cotangent_ref, picker_ref, summed_ref, vector_ref, own_ref, dense_ref) = refs[
        sum(sizes) : sum(sizes) + 6
    ]
    hidden_ref, active_ref, slope_ref, total_ref, sums_ref, *outs = refs[sum(sizes) + 6 : -2]
    low_ref, turned_ref = refs[-2:]
    step = pl.program_id(0)
    width = vector_ref.shape[1]

    @pl.when(step == 0)
    def _():
        picked_grad = to_low(matmul_nt(dense_ref[...], read_weight(head_refs, None)))
        grad = to_full(cotangent_ref[...]) + matmul_tn(picker_ref[...], picked_grad)
        summed_grad, gain_grad, shift_grad = norm_backward(
            summed_ref[...], vector_ref[6:7, :], grad
        )
        total_ref[...] = summed_grad
        low = to_low(summed_grad)
        low_ref[...] = low
        turned_ref[...] = hidden_ref[...].T
        sums_ref[...] = jnp.zeros_like(sums_ref)
        sums_ref[0:1, :] = jnp.sum(to_full(low), axis=0, keepdims=True)
        sums_ref[1:2, :] = gain_grad
        sums_ref[2:3, :] = shift_grad
        dense_grad = to_low(matmul_tn(own_ref[...], dense_ref[...]))
        if down_share:
            store_blocks(outs, dense_grad, place, share, slice(2 * down_share, None))
        else:
            outs[2][...] = dense_grad

    low = low_ref[...]
    up, down = read_weight(up_refs, None), read_weight(down_refs, None)
    down_grad = to_low(matmul_tn(active_ref[...], low))
    pre_grad = to_low(matmul_nt(low, down) * slope_ref[...])
    total_ref[...] += matmul_nt(pre_grad, up)
    sums_ref[pl.ds(3 + step, 1), :] = jnp.sum(to_full(pre_grad), axis=0, keepdims=True)
    up_grad = to_low(matmul(turned_ref[...], pre_grad))
    if down_share:
        chips = width // (2 * down_share)
        rows = slice(down_share, 2 * down_share)
        store_blocks(outs, down_grad, place, down_share, rows, step * chips)
        rows = pl.ds(pl.multiple_of(step * share, share), share)
        store_blocks(outs, up_grad, place, share, rows)
    else:
        outs[0][...] = up_grad
        outs[1][...] = down_grad


def feed_backward(place, count, cotangent, picker, summed, vectors, own, dense, hidden, active, slope, weights):
    rows, width = cotangent.shape
    steps = active.shape[1] // width
    share, down_share, chips = width // count, active.shape[1] // count, count // 2
    aligned = share % 8 == 0
    first, first_specs = up_operands_of(weights, steps)
    second, second_specs = weights.operands(steps, None, width, lambda s, c: 0, steps, lambda s, c: s)
    third, third_specs = weights.operands(steps + 1, None, width, lambda s, c: 0)
    operands = [cotangent, picker, summed, vectors, own, dense, hidden]
    block = pl.BlockSpec((rows, width), lambda s, c: (0, s))
    low = jnp.bfloat16
    if aligned:
        shape = jax.ShapeDtypeStruct((chips, 2 * down_share + share, width // 2), low)
        out_shape, out_specs = [shape] * 4, [whole(shape)] * 4
    else:
        out_shape = [
            jax.ShapeDtypeStruct((width, steps * width), low),
            jax.ShapeDtypeStruct((steps * width, width), low),
            jax.ShapeDtypeStruct((width, width), low),
        ]
        out_specs = [
            pl.BlockSpec((width, width), lambda s, c: (0, s)),
            pl.BlockSpec((width, width), lambda s, c: (s, 0)),
            whole(out_shape[2]),
        ]
    common = [
        jax.ShapeDtypeStruct((rows, width), jnp.float32),
        jax.ShapeDtypeStruct((8, width), jnp.float32),
    ]
    kernel = functools.partial(
        feed_back_kernel,
        sizes=[len(first), len(second), len(third)],
        share=share,
        down_share=down_share if aligned else 0,
    )
    hidden_grad, sums, *outs = pl.pallas_call(
        kernel,
        grid_spec=pltpu.PrefetchScalarGridSpec(
            num_scalar_prefetch=1,
            grid=(steps,),
            in_specs=[
                *first_specs,
                *second_specs,
                *third_specs,
                *[whole(operand) for operand in operands],
                block,
                block,
            ],
            out_specs=[*[whole(shape) for shape in common], *out_specs],
            scratch_shapes=[pltpu.VMEM((rows, width), low), pltpu.VMEM((width, rows), low)],
        ),
        out_shape=[*common, *out_shape],
        compiler_params=pltpu.CompilerParams(dimension_semantics=("arbitrary",)),
        name="feed_backward",
    )(place, *first, *second, *third, *operands, active, slope)
    if not aligned:
        away, kept = arranged([*column_blocks(outs[0], width), *outs[1:]], place)
    else:
        away, kept = outs[:2], outs[2:]
    return hidden_grad, sums, away, kept


def out_back_kernel(core, *refs, size):
    weight_refs = refs[:size]
    grad_ref, summed_ref, vector_ref, total_ref, low_ref, back_ref, sums_ref = refs[size:]
    width = vector_ref.shape[1]
    summed_grad, gain_grad, shift_grad = norm_backward(
        summed_ref[...], vector_ref[3:4, :], grad_ref[...]
    )
    total_ref[...] = summed_grad
    low = to_low(summed_grad)
    low_ref[...] = low
    bias_grad = jnp.sum(to_full(low), axis=0, keepdims=True)
    zero = jnp.zeros((5, width), jnp.float32)
    sums_ref[...] = jnp.concatenate([bias_grad, gain_grad, shift_grad, zero], axis=0)
    back_ref[...] = to_low(matmul_nt(low, read_weight(weight_refs, core[0])))


def out_backward(core, hidden_grad, summed, vectors, group, index):
    rows, width = hidden_grad.shape
    arrays, specs = group.operands(index, core, width, lambda s, c: 0)
    operands = [hidden_grad, summed, vectors]
    out_shape = [
        jax.ShapeDtypeStruct((rows, width), jnp.float32),
        jax.ShapeDtypeStruct((rows, width), jnp.bfloat16),
        jax.ShapeDtypeStruct((rows, width), jnp.bfloat16),
        jax.ShapeDtypeStruct((8, width), jnp.float32),
    ]
    return pl.pallas_call(
        functools.partial(out_back_kernel, size=len(arrays)),
        grid_spec=pltpu.PrefetchScalarGridSpec(
            num_scalar_prefetch=1,
            grid=(1,),
            in_specs=[*specs, *[whole(operand) for operand in operands]],
            out_specs=[whole(shape) for shape in out_shape],
        ),
        out_shape=out_shape,
        name="out_backward",
    )(core.reshape(1), *arrays, *operands)


def attention_back_kernel(*refs, first_head):
    (grad_ref, q_ref, k_ref, v_ref, total_ref, down_ref, across_ref) = refs[:7]
    dq_ref, dk_ref, dv_ref, sums_ref, mask_ref = refs[7:]
    step = pl.program_id(0)

    @pl.when(step == 0)
    def _():
        mask_ref[...] = jnp.where(down_ref[...] == across_ref[...], 0.0, NEGATIVE)

    pair_width = 2 * HEAD_DIM
    scale = HEAD_DIM ** (-0.5)
    lane = lax.broadcasted_iota(jnp.int32, (1, pair_width), 1)
    columns = q_ref.shape[1]
    heads = columns // HEAD_DIM
    for pair in range(heads // 2):
        span = slice(pair_width * pair, pair_width * (pair + 1))
        queries, keys, values = q_ref[:, span], k_ref[:, span], v_ref[:, span]
        grads = grad_ref[:, span]
        scaled = to_full(queries) * scale
        sides = []
        for side in range(2):
            here = (lane < HEAD_DIM) == (side == 0)
            mine = to_low(jnp.where(here, scaled, 0.0))
            my_grads = jnp.where(here, grads, jnp.zeros_like(grads))
            head = first_head + step * heads + 2 * pair + side
            scores = matmul_nt(keys, mine) + mask_ref[...]
            softmax = jnp.exp(scores - total_ref[pl.ds(head, 1), :])
            softmax_grad = matmul_nt(values, my_grads)
            inner = jnp.sum(softmax * softmax_grad, axis=0, keepdims=True)
            score_grad = to_low(softmax * (softmax_grad - inner))
            query_grad = matmul_tn(keys, score_grad)[HEAD_DIM * side : HEAD_DIM * (side + 1)]
            sides.append((query_grad, matmul(score_grad, mine), matmul(to_low(softmax), my_grads)))
        query_grad = to_low(jnp.concatenate([sides[0][0], sides[1][0]], axis=0).T * scale)
        value_grad = to_low(sides[0][2] + sides[1][2])
        dq_ref[:, span] = query_grad
        dk_ref[:, span] = to_low(sides[0][1] + sides[1][1])
        dv_ref[:, span] = value_grad
        sums_ref[0:1, span] = jnp.sum(to_full(query_grad), axis=0, keepdims=True)
        sums_ref[1:2, span] = jnp.sum(to_full(value_grad), axis=0, keepdims=True)


def attention_backward(context_grad, queries, keys, values, score_total, segments, start, columns):
    rows = context_grad.shape[0]
    size = 2 * HEAD_DIM
    down, across = segments[:, None], segments[None, :]
    block = pl.BlockSpec((rows, size), lambda s: (0, start // size + s))
    out_block = pl.BlockSpec((rows, size), lambda s: (0, s))
    return pl.pallas_call(
        functools.partial(attention_back_kernel, first_head=start // HEAD_DIM),
        grid=(columns // size,),
        in_specs=[*[block] * 4, whole(score_total), whole(down), whole(across)],
        out_specs=[*[out_block] * 3, pl.BlockSpec((8, size), lambda s: (0, s))],
        out_shape=[
            *[jax.ShapeDtypeStruct((rows, columns), jnp.bfloat16)] * 3,
            jax.ShapeDtypeStruct((8, columns), jnp.float32),
        ],
        scratch_shapes=[pltpu.VMEM((rows, rows), jnp.float32)],
        compiler_params=pltpu.CompilerParams(dimension_semantics=("arbitrary",)),
        name="attention_backward",
    )(context_grad, queries, keys, values, score_total, down, across)


def joined_sums(bias_sums, out_sums, feed_sums, head_sums, steps):
    return jnp.concatenate(
        [
            jnp.concatenate([part[:2] for part in bias_sums], axis=1),
            out_sums[:3],
            feed_sums[: 3 + steps],
            head_sums[: 8 - steps],
        ],
        axis=0,
    )


def last_grads_kernel(place, *refs, parts, share, steps):
    tokens_ref, context_ref, branch_ref, out_sums_ref, feed_sums_ref, head_sums_ref, *rest = refs
    mixed_refs, rest = rest[: 3 * parts], rest[3 * parts :]
    bias_refs, outs = rest[:parts], rest[parts:]
    turned = tokens_ref[...].T
    for which in range(3):
        for part in range(parts):
            mixed = mixed_refs[3 * part + which][...]
            columns = mixed.shape[1]
            grad = to_low(matmul(turned, mixed))
            if share:
                rows = slice(share * which, share * (which + 1))
                store_blocks(outs, grad, place, share, rows, column=columns * part)
            else:
                outs[which][:, columns * part : columns * (part + 1)] = grad
    grad = to_low(matmul_tn(context_ref[...], branch_ref[...]))
    if share:
        store_blocks(outs, grad, place, share, slice(3 * share, 4 * share))
        small = to_low(
            joined_sums(
                [ref[...] for ref in bias_refs],
                out_sums_ref[...],
                feed_sums_ref[...],
                head_sums_ref[...],
                steps,
            )
        )
        half = small.shape[1] // 2
        for index, out_ref in enumerate(outs):
            part = small[:, half * (index % 2) : half * (index % 2 + 1)]
            out_ref[:, 4 * share :, :] = jnp.broadcast_to(
                part[None], (out_ref.shape[0], *part.shape)
            )
    else:
        outs[3][...] = grad


def last_grads(place, count, tokens, context, branch_grad, sums, steps, mixed):
    width = tokens.shape[1]
    share, chips = width // count, count // 2
    aligned = share % 8 == 0
    parts = len(mixed)
    biases = [part[3] for part in mixed]
    mixed = [part[:3] for part in mixed]
    operands = [tokens, context, branch_grad, *sums, *[m for part in mixed for m in part], *biases]
    small = joined_sums(biases, *sums, steps)
    if aligned:
        rows = 4 * share + small.shape[0]
        out_shape = [jax.ShapeDtypeStruct((chips, rows, width // 2), jnp.bfloat16)] * 4
    else:
        out_shape = [jax.ShapeDtypeStruct((width, width), jnp.bfloat16)] * 4
    outs = pl.pallas_call(
        functools.partial(
            last_grads_kernel, parts=parts, share=share if aligned else 0, steps=steps
        ),
        grid_spec=pltpu.PrefetchScalarGridSpec(
            num_scalar_prefetch=1,
            grid=(1,),
            in_specs=[whole(operand) for operand in operands],
            out_specs=[whole(shape) for shape in out_shape],
        ),
        out_shape=out_shape,
        name="last_grads",
    )(place, *operands)
    if not aligned:
        both = jnp.broadcast_to(to_low(small)[None], (count, *small.shape))
        return arranged([*outs, both.reshape(-1, width)], place)
    return outs[:2], outs[2:]


def tokens_back_kernel(core, *refs, sizes, parts):
    ends = [sum(sizes[:k]) for k in range(4)]
    weights = [refs[ends[k] : ends[k + 1]] for k in range(3)]
    summed_ref, *mixed_refs, out_ref = refs[ends[3] :]
    total = summed_ref[...]
    for which in range(3):
        weight = read_weight(weights[which], core[0])
        for part in range(parts):
            mixed = mixed_refs[3 * part + which][...]
            columns = mixed.shape[1]
            total += matmul_nt(mixed, weight[:, columns * part : columns * (part + 1)])
    out_ref[...] = total


def tokens_backward(core, summed_grad, mixed, weights):
    width = summed_grad.shape[1]
    arrays, specs, sizes = [], [], []
    for group, index in weights:
        some, their = group.operands(index, core, width, lambda s, c: 0)
        arrays, specs, sizes = arrays + some, specs + their, sizes + [len(some)]
    operands = [summed_grad, *[matrix for part in mixed for matrix in part]]
    return pl.pallas_call(
        functools.partial(tokens_back_kernel, sizes=sizes, parts=len(mixed)),
        grid_spec=pltpu.PrefetchScalarGridSpec(
            num_scalar_prefetch=1,
            grid=(1,),
            in_specs=[*specs, *[whole(operand) for operand in operands]],
            out_specs=whole(summed_grad),
        ),
        out_shape=jax.ShapeDtypeStruct(summed_grad.shape, jnp.float32),
        name="tokens_backward",
    )(core.reshape(1), *arrays, *operands)


def take_kernel(index, whole_ref, *out_refs, plan):
    width = whole_ref.shape[1]
    for out_ref, (first_row, share) in zip(out_refs, plan):
        spot = index[0] * share
        row, place = first_row + spot // width, spot % width
        line = jnp.broadcast_to(whole_ref[pl.ds(row, 1), :], (8, width))
        moved = pltpu.roll(line, lax.rem(width - place, width), 1)
        out_ref[...] = moved[:1, :share]


def take_shares(device, values, first_rows, shares):
    shapes = [jax.ShapeDtypeStruct((1, share), jnp.float32) for share in shares]
    lines = pl.pallas_call(
        functools.partial(take_kernel, plan=list(zip(first_rows, shares))),
        grid_spec=pltpu.PrefetchScalarGridSpec(
            num_scalar_prefetch=1,
            grid=(1,),
            in_specs=[whole(values)],
            out_specs=[whole(shape) for shape in shapes],
        ),
        out_shape=shapes,
        name="take_shares",
    )(device.reshape(1), values)
    return [line[0] for line in lines]


def take(value, axis, index):
    return lax.dynamic_index_in_dim(value, index, axis, keepdims=False)


def add_low(first, second):
    return to_low(to_full(first) + to_full(second))


def halve(value, axis, stride):
    chips = lax.axis_size("dp")
    bit = (lax.axis_index("dp") // stride) % 2
    pairs = [(chip, chip ^ stride) for chip in range(chips)]
    arrived = lax.ppermute(take(value, axis, 1 - bit), "dp", pairs)
    return add_low(take(value, axis, bit), arrived)


def core_swap(away):
    return lax.ppermute(away, "fsdp", [(0, 1), (1, 0)])


def along(sent, stride):
    chips = lax.axis_size("dp")
    return lax.ppermute(sent, "dp", [(chip, chip ^ stride) for chip in range(chips)])


def total_of(addends):
    total = to_full(addends[0])
    for addend in addends[1:]:
        total = total + to_full(addend)
    return total


def my_place():
    chip = lax.axis_index("dp")
    return jnp.stack([lax.axis_index("fsdp"), chip % 2, (chip // 2) % 2, chip // 4])


def chip_at(index, place, levels, first_axis):
    outer, level = index // levels, index % levels
    bits = (outer // 2, outer % 2) if first_axis == 0 else (outer % 2, outer // 2)
    return ((place[3] ^ level) * 2 + (place[2] ^ bits[1])) * 2 + (place[1] ^ bits[0])


def index_of(chip, place, levels, first_axis):
    bits = ((chip % 2) ^ place[1], ((chip // 2) % 2) ^ place[2])
    outer = 2 * bits[first_axis] + bits[1 - first_axis]
    return outer * levels + ((chip // 4) ^ place[3])


class ChipSum:
    def __init__(self, away, kept):
        self.sides = [[part] for part in kept]
        self.strides = [[1, 2], [2, 1]]
        self.arrived = [core_swap(part) for part in away]

    def add(self, arrived):
        for side, part in zip(self.sides, arrived):
            side.append(part)

    def sends(self):
        sent = [to_low(total_of([a[a.shape[0] // 2 :] for a in side])) for side in self.sides]
        self.sides = [[a[: a.shape[0] // 2] for a in side] for side in self.sides]
        return sent

    def start(self, sent):
        self.arrived = [along(part, strides.pop(0)) for part, strides in zip(sent, self.strides)]

    def level_block(self, level):
        return jnp.concatenate(
            [total_of([a[level] for a in side]) for side in self.sides], axis=-1
        )

    def level_sends(self):
        while self.sides[0][0].shape[0] > 4:
            stride = 4 * (self.sides[0][0].shape[0] // 2)
            sent = self.sends()
            self.add([along(part, stride) for part in sent])
        levels = self.sides[0][0].shape[0]
        return [to_low(self.level_block(level)) for level in range(1, levels)]

    def start_levels(self, sent):
        self.arrived = [along(part, 4 * (level + 1)) for level, part in enumerate(sent)]

    def result(self, arrived):
        return total_of([self.level_block(0), *arrived])


def arranged(matrices, place):
    chips = lax.axis_size("dp")
    value = jnp.concatenate(
        [matrix.reshape(chips, 2, -1, matrix.shape[-1]) for matrix in matrices], axis=2
    )
    half = value.shape[-1] // 2
    sides = []
    for core in (1 - place[0], place[0]):
        mine = take(value, 1, core)
        sides.append(
            [
                jnp.take(
                    mine[..., axis * half : (axis + 1) * half],
                    chip_at(jnp.arange(chips), place, chips // 4, axis),
                    axis=0,
                )
                for axis in range(2)
            ]
        )
    return sides


def store_blocks(outs, value, place, share, rows, first_chip=0, column=0):
    columns = value.shape[-1]
    split = value.reshape(-1, 2, share, columns)
    kept, away = in_order(split[:, 0], split[:, 1], place[0])
    levels = outs[0].shape[0] // 4
    width = outs[0].shape[-1]
    for chip in range(split.shape[0]):
        for which, half in enumerate((away, kept)):
            for axis in range(2):
                low, high = max(column, axis * width), min(column + columns, (axis + 1) * width)
                if low >= high:
                    continue
                spot = index_of(first_chip + chip, place, levels, axis)
                outs[2 * which + axis][
                    pl.ds(spot, 1), rows, low - axis * width : high - axis * width
                ] = half[chip : chip + 1, :, low - column : high - column]


def tie(value, *others):
    return lax.optimization_barrier((value, *others))


def window_base(start, total, window):
    return pl.multiple_of(jnp.minimum((start // 16) * 16, total - window), 16)


def compact_kernel(place, places, counts, indices, mine_ref, other_ref, *refs, window, levels):
    step = pl.program_id(0)
    *before, out_ref = refs

    @pl.when(step == 0)
    def _():
        out_ref[...] = before[0][...] if before else jnp.zeros_like(out_ref)

    _, batch, slots, half = mine_ref.shape
    total = out_ref.shape[0]
    for which, ref in enumerate((mine_ref, other_ref)):
        core = place[0] if which == 0 else 1 - place[0]
        for axis in range(2):
            for lane in range(batch):
                index = indices[step * batch + lane]
                source = 2 * chip_at(index, place, levels, axis) + core
                start = places[source]
                base = window_base(start, total, window)
                row = lax.broadcasted_iota(jnp.int32, (window, slots), 0) + (base - start)
                column = lax.broadcasted_iota(jnp.int32, (window, slots), 1)
                chosen = jnp.where((row == column) & (column < counts[source]), 1.0, 0.0)
                moved = matmul(to_low(chosen), ref[axis, lane])
                out_ref[pl.ds(base, window), half * axis : half * (axis + 1)] += to_low(moved)


def compact(place, places, counts, mine, other, indices, total, before=()):
    _, blocks, slots, half = mine.shape
    levels = lax.axis_size("dp") // 4
    batch = blocks // 2 if blocks <= 16 else 2
    block = pl.BlockSpec((2, batch, slots, half), lambda i, *_: (0, i, 0, 0))
    return pl.pallas_call(
        functools.partial(compact_kernel, window=slots + 16, levels=levels),
        grid_spec=pltpu.PrefetchScalarGridSpec(
            num_scalar_prefetch=4,
            grid=(blocks // batch,),
            in_specs=[block, block, *[whole(rows) for rows in before]],
            out_specs=pl.BlockSpec((total, 2 * half), lambda i, *_: (0, 0)),
        ),
        out_shape=jax.ShapeDtypeStruct((total, 2 * half), jnp.bfloat16),
        compiler_params=pltpu.CompilerParams(dimension_semantics=("arbitrary",)),
        name="compact_rows",
    )(place, places, counts, jnp.array(indices, jnp.int32), mine, other, *before)


def compact_labels_kernel(places, counts, lines_ref, out_ref):
    out_ref[...] = jnp.zeros_like(out_ref)
    sources, slots = lines_ref.shape
    total = out_ref.shape[1]
    wide = 2 * slots
    lane = lax.broadcasted_iota(jnp.int32, (8, wide), 1)

    def place_one(source, carry):
        start = places[source]
        base = pl.multiple_of(jnp.minimum(start // slots * slots, total - wide), slots)
        shift = start - base
        line = jnp.broadcast_to(to_full(lines_ref[pl.ds(source, 1), :]), (8, slots))
        line = jnp.concatenate([line, jnp.zeros_like(line)], axis=1)
        moved = pltpu.roll(line, lax.rem(shift, wide), 1)
        here = (lane >= shift) & (lane < shift + counts[source])
        span = pl.ds(base, wide)
        out_ref[:, span] = jnp.where(here, moved, out_ref[:, span])
        return carry

    lax.fori_loop(0, sources, place_one, 0)


def compact_labels(places, counts, lines, total):
    out = pl.pallas_call(
        compact_labels_kernel,
        grid_spec=pltpu.PrefetchScalarGridSpec(
            num_scalar_prefetch=2,
            grid=(1,),
            in_specs=[whole(lines)],
            out_specs=pl.BlockSpec((8, total), lambda *_: (0, 0)),
        ),
        out_shape=jax.ShapeDtypeStruct((8, total), jnp.float32),
        name="compact_labels",
    )(places, counts, lines)
    return out[0].astype(jnp.int32)


def block_order():
    levels = lax.axis_size("dp") // 4
    near = [*range(levels), *range(2 * levels, 3 * levels), levels, 3 * levels]
    return near, [k for k in range(4 * levels) if k not in near]


def gather_blocks(value, beside, given):
    chips = lax.axis_size("dp")
    levels = chips // 4
    half = value.shape[-1] // 2
    if levels <= 4:
        others = jnp.stack([along(value, 4 * level) for level in range(1, levels)])
    else:
        others = value[None]
        while others.shape[0] < levels:
            others = jnp.concatenate([others, along(others, 4 * others.shape[0])])
        others = others[1:]
    own = [value[:, :half], value[:, half:]]
    strides = [(1, 2), (2, 1)]
    near = [along(part, first) for part, (first, _) in zip(own, strides)]
    far_sent = [jnp.stack([part, got]) for part, got in zip(own, near)]
    others = tie(others, *far_sent)[0]
    far = [along(sent, second) for sent, (_, second) in zip(far_sent, strides)]
    rest = [others[..., :half], others[..., half:]]
    near_rest = [along(part, first) for part, (first, _) in zip(rest, strides)]
    given, *near_rest = tie(given, *near_rest)
    far_rest = [
        along(jnp.concatenate([part, got]), second)
        for part, got, (_, second) in zip(rest, near_rest, strides)
    ]
    early = jnp.stack(
        [
            jnp.concatenate([own[k][None], rest[k], near[k][None], near_rest[k], far[k]])
            for k in range(2)
        ]
    )
    results = beside(early, core_swap(early), given)
    tied = tie(*far_rest, *results)
    late = jnp.stack(tied[:2])
    return late, core_swap(late), tied[2:]


def spread_kernel(place, places, counts, rows_ref, *out_refs, window):
    step = pl.program_id(0)
    total = rows_ref.shape[0]
    batch, slots, half = out_refs[0].shape
    levels = pl.num_programs(0) * batch // 4
    for which in range(2):
        core = 1 - place[0] if which == 0 else place[0]
        for axis in range(2):
            for lane in range(batch):
                chip = chip_at(step * batch + lane, place, levels, axis)
                source = 2 * chip + core
                start = places[source]
                base = window_base(start, total, window)
                row = lax.broadcasted_iota(jnp.int32, (slots, window), 0)
                column = lax.broadcasted_iota(jnp.int32, (slots, window), 1) + (base - start)
                chosen = jnp.where((row == column) & (row < counts[source]), 1.0, 0.0)
                moved = matmul(
                    to_low(chosen), rows_ref[pl.ds(base, window), half * axis : half * (axis + 1)]
                )
                out_refs[2 * which + axis][lane] = to_low(moved)


def spread(place, places, counts, rows, slots):
    chips = places.shape[0] // 2
    total, width = rows.shape
    batch = 4
    block = pl.BlockSpec((batch, slots, width // 2), lambda i, *_: (i, 0, 0))
    shape = jax.ShapeDtypeStruct((chips, slots, width // 2), jnp.bfloat16)
    outs = pl.pallas_call(
        functools.partial(spread_kernel, window=slots + 16),
        grid_spec=pltpu.PrefetchScalarGridSpec(
            num_scalar_prefetch=3,
            grid=(chips // batch,),
            in_specs=[
                pl.BlockSpec((total, width), lambda i, *_: (0, 0), pipeline_mode=pl.Buffered(1))
            ],
            out_specs=[block] * 4,
        ),
        out_shape=[shape] * 4,
        compiler_params=pltpu.CompilerParams(dimension_semantics=("arbitrary",)),
        name="spread_rows",
    )(place, places, counts, rows)
    return outs[:2], outs[2:]


def per_device(
    tokens,
    segments,
    mask_flags,
    targets,
    cotangent,
    qkv_weight,
    attn_bias,
    out_weight,
    out_bias,
    attn_gain,
    attn_shift,
    up_weight,
    up_bias,
    down_weight,
    down_bias,
    ffn_gain,
    ffn_shift,
    dense_weight,
    dense_bias,
    head_gain,
    head_shift,
    decoder,
    vocab_bias,
):
    count = lax.axis_size(AXES)
    width = tokens.shape[1]
    core = lax.axis_index("fsdp")
    device = lax.axis_index(AXES)
    here = my_place()
    blocks = qkv_weight.shape[1] // width
    steps = up_weight.shape[1] // width
    share, up_share, down_share = out_weight.shape[0], up_weight.shape[0], down_weight.shape[0]
    label_place = up_share * steps + down_share + share
    later_packed = pack_later(
        [
            (up_weight, [up_share * k for k in range(steps)]),
            (down_weight, [up_share * steps]),
            (dense_weight, [up_share * steps + down_share]),
        ],
        mask_flags,
        targets,
    )
    later_gathered = lax.all_gather(later_packed, AXES, axis=0)
    later = Weights([later_gathered], [*[up_share] * steps, down_share, share])
    small = (
        attn_bias,
        out_bias,
        attn_gain,
        attn_shift,
        down_bias,
        ffn_gain,
        ffn_shift,
        up_bias,
        dense_bias,
        head_gain,
        head_shift,
    )
    small_rows = (0, 2, 3, 4, 5, 6, 7, 8, 12, 13, 14)
    placed = place_shares(device, small, small_rows, 16, width)
    half = 2 * share + 8
    first_packed = pack_rows(
        [
            (qkv_weight, [0, share, half]),
            (placed[:8], [2 * share]),
            (out_weight, [half + share]),
            (placed[8:], [half + 2 * share]),
        ]
    )
    upper, lower = gather_pair(first_packed, half)
    first_group, second_group = (Weights(list(pair), [share, share, 8]) for pair in (upper, lower))
    vectors, more_vectors = (
        sum(jnp.sum(to_full(array[:, 2 * share :]), axis=0) for array in pair)
        for pair in (upper, lower)
    )
    queries, keys_low, values_low, context, score_total, summed1, hidden = attention_forward(
        core,
        tokens,
        segments,
        [(first_group, 0), (first_group, 1), (second_group, 0), (second_group, 1)],
        vectors,
    )
    active, slope, summed2, output = ffn_forward(hidden, later, more_vectors[:4], vectors)
    head_gain_full, head_shift_full = more_vectors[5], more_vectors[6]
    mask_rank = jnp.cumsum(mask_flags) - 1
    slot_place = jnp.where(mask_flags > 0, mask_rank, -1)
    picker_low = (jnp.arange(MAXM)[:, None] == slot_place[None, :]).astype(jnp.bfloat16)
    own_rows, dense, normed_low = head_forward(picker_low, output, later, steps + 1, more_vectors)
    _, tail_back = jax.vjp(head_tail, dense, head_gain_full, head_shift_full)
    chips = count // 2
    group = MASK_DEV * chips
    total = 2 * group
    gathered_late, normed_low = tie(later_gathered, normed_low)
    label_parts = gathered_late[:, label_place : label_place + 2, :MAXM].astype(jnp.int32)
    label_lines = label_parts[:, 0] * 256 + label_parts[:, 1] - 1
    counts = jnp.sum((label_lines >= 0).astype(jnp.int32), axis=1)
    by_core = counts.reshape(chips, 2)
    earlier = jnp.arange(chips)[:, None] < jnp.arange(chips)[None, :]
    places = jnp.sum(jnp.where(earlier[:, :, None], by_core[:, None, :], 0), axis=0)
    places = (places + jnp.arange(2)[None, :] * group).reshape(count)
    all_labels = compact_labels(places, counts, label_lines, total)
    slice_index = lax.axis_index(AXES)
    vocab_rows = decoder.shape[0]
    local_label = all_labels - slice_index * vocab_rows
    label_hit = jnp.arange(vocab_rows)[None, :] == local_label[:, None]

    early_order, late_order = block_order()

    def beside_last(mine, other, chosen):
        hit = jnp.arange(vocab_rows)[None, :] == chosen[:, None]
        pulled = to_low(matmul(hit.astype(jnp.bfloat16), decoder))
        return compact(here, places, counts, mine, other, early_order, total), pulled

    mine, other, (early_rows, label_pull) = gather_blocks(normed_low, beside_last, local_label)
    late = (here, places, counts, mine, other, late_order, total)
    small_total = total <= 4096
    all_rows = compact(*late, (early_rows,)) if small_total else early_rows + compact(*late)
    logits = matmul_nt(all_rows, decoder) + to_full(vocab_bias)
    row_peak = jnp.max(logits, axis=1)
    exp_sums = jnp.sum(jnp.exp(logits - row_peak[:, None]), axis=1)
    label_sum = jnp.sum(jnp.where(label_hit, logits, 0.0))
    local_total = (row_peak + jnp.log(exp_sums)).reshape(-1, 128)
    lines = local_total.shape[0]
    merged = jnp.concatenate(
        [local_total, jnp.pad(label_sum[None, None], ((0, 7), (0, 127)))], axis=0
    )
    is_total = jnp.arange(lines + 8)[:, None] < lines
    middle = total // 2
    pulls = []
    rounds = [[1], [2, 4, 6]]
    rounds += [[8, 16, 24]] if count == 32 else [[8 << k] for k in range((count // 8).bit_length() - 1)]
    for distances in rounds:
        arrived = [
            lax.ppermute(merged, AXES, [(place, place ^ far) for place in range(count)])
            for far in distances
        ]
        if len(pulls) < 2:
            rows = slice(middle * len(pulls), middle * (len(pulls) + 1))
            pull = matmul(to_low(jnp.exp(logits[rows] - row_peak[rows, None])), decoder)
            *arrived, pull = tie(*arrived, pull)
            pulls.append(pull)
        every = [merged, *arrived]
        peak = functools.reduce(jnp.maximum, every)
        both = peak + jnp.log(sum(jnp.exp(part - peak) for part in every))
        merged = jnp.where(is_total, both, sum(every))
    log_total = merged[:lines].reshape(total)
    mean_loss = (jnp.sum(log_total) - merged[lines, 0]) / total
    scale = jnp.exp(row_peak - log_total)[:, None]
    rows_part = jnp.concatenate(
        [
            to_low(pull * scale[rows] - to_full(label_pull[rows]))
            for pull, rows in zip(pulls, (slice(0, middle), slice(middle, total)))
        ]
    )
    rows_sum = ChipSum(*spread(here, places, counts, rows_part, MAXM))
    rows_sum.add(rows_sum.arrived)
    rows_sum.start(rows_sum.sends())
    logit_grad = to_low(jnp.exp(logits - log_total[:, None]) - label_hit.astype(jnp.float32))
    vocab_bias_grad = jnp.sum(to_full(logit_grad), axis=0)
    logit_grad, vocab_bias_grad, *arrived = tie(logit_grad, vocab_bias_grad, *rows_sum.arrived)
    rows_sum.add(arrived)
    rows_sum.start(rows_sum.sends())
    decoder_grad = matmul_tn(logit_grad, all_rows)
    decoder_grad, *arrived = tie(decoder_grad, *rows_sum.arrived)
    rows_sum.add(arrived)
    rows_sum.start_levels(rows_sum.level_sends())
    normed_grad = rows_sum.result(rows_sum.arrived)
    dense_grad, head_gain_grad, head_shift_grad = tail_back(normed_grad)
    dense_grad_low = to_low(dense_grad)
    dense_bias_grad = jnp.sum(to_full(dense_grad_low), axis=0)
    hidden_grad, feed_sums, *feed_grads = feed_backward(
        here,
        count,
        cotangent,
        picker_low,
        summed2,
        vectors,
        own_rows,
        dense_grad_low,
        hidden,
        active,
        slope,
        later,
    )
    first = ChipSum(*feed_grads)
    summed1_grad, branch1_grad, context_grad, out_sums = out_backward(
        core, hidden_grad, summed1, vectors, second_group, 1
    )
    context_grad, *arrived = tie(context_grad, *first.arrived)
    first.add(arrived)
    context_grad, *sent = tie(context_grad, *first.sends())
    first.start(sent)
    saved = (queries, keys_low, values_low, score_total, segments)
    middle = width // 2
    mixed = [list(attention_backward(context_grad, *saved, 0, middle))]
    mixed[0][0], context_grad = tie(mixed[0][0], context_grad)
    mixed.append(list(attention_backward(context_grad, *saved, middle, width - middle)))
    head_sums = jnp.stack(
        [dense_bias_grad, head_gain_grad, head_shift_grad, *[jnp.zeros((width,))] * 5]
    )
    away, kept = last_grads(
        here, count, tokens, context, branch1_grad, (out_sums, feed_sums, head_sums), steps, mixed
    )
    mixed = [part[:3] for part in mixed]
    second = ChipSum(away, kept)
    mixed[0][0], _, *arrived = tie(mixed[0][0], away[0], *first.arrived)
    first.add(arrived)
    mixed[0][0], *sent = tie(mixed[0][0], *first.sends())
    first.start(sent)
    mixed[0][0], *arrived = tie(mixed[0][0], *second.arrived)
    second.add(arrived)
    mixed[0][0], *sent = tie(mixed[0][0], *second.sends())
    second.start(sent)
    tokens_grad = tokens_backward(
        core, summed1_grad, mixed, [(first_group, 0), (first_group, 1), (second_group, 0)]
    )
    first.add(first.arrived)
    first.start_levels(first.level_sends())
    second.add(second.arrived)
    second.start(second.sends())
    second.add(second.arrived)
    second.start_levels(second.level_sends())
    first, second = first.result(first.arrived), second.result(second.arrived)
    up_pieces = [first[share * k : share * (k + 1)] for k in range(steps)]
    down_piece = first[up_share * steps : up_share * steps + down_share]
    dense_piece = first[up_share * steps + down_share :]
    qkv_pieces = [second[share * k : share * (k + 1)] for k in range(blocks)]
    out_piece = second[share * blocks : share * (blocks + 1)]
    small_pieces = take_shares(
        device, second[share * (blocks + 1) :], small_rows, [vector.shape[0] for vector in small]
    )
    return (
        output,
        mean_loss,
        tokens_grad,
        jnp.concatenate(qkv_pieces, axis=1),
        small_pieces[0],
        out_piece,
        *small_pieces[1:4],
        jnp.concatenate(up_pieces, axis=1),
        small_pieces[7],
        down_piece,
        *small_pieces[4:7],
        dense_piece,
        *small_pieces[8:],
        decoder_grad,
        vocab_bias_grad,
    )


def solution(mesh):
    matrix_spec = P(AXES, None)
    vector_spec = P(AXES)
    m, v = matrix_spec, vector_spec
    return jax.shard_map(
        per_device,
        mesh=mesh,
        in_specs=(m, v, v, v, m, m, v, m, v, v, v, m, v, m, v, v, v, m, v, v, v, m, v),
        out_specs=(m, P(), m, m, v, m, v, v, v, m, v, m, v, v, v, m, v, v, v, m, v),
        check_vma=False,
    )
```

```python
import functools

import jax
import jax.numpy as jnp
from jax import lax
from jax.experimental import pallas as pl
from jax.experimental.pallas import tpu as pltpu
from jax.sharding import PartitionSpec as P

HEADS = 12
HEAD_DIM = 64
MASK_DEV = 64
MAXM = 128

EPSILON = 1e-05
NEGATIVE = -1e30
AXES = ("dp", "fsdp")


def to_low(values):
    return values.astype(jnp.bfloat16)


def to_full(values):
    return values.astype(jnp.float32)


def layer_norm(values, gain_vector, shift_vector):
    center = values - jnp.mean(values, axis=-1, keepdims=True)
    spread = jnp.mean(center * center, axis=-1, keepdims=True)
    return center * lax.rsqrt(spread + EPSILON) * gain_vector + shift_vector


def gelu_exact(values):
    return jax.nn.gelu(values, approximate=False)


def head_tail(dense_out, gain_vector, shift_vector):
    return layer_norm(gelu_exact(dense_out), gain_vector, shift_vector)


def matmul(left_side, right_side):
    return jnp.dot(left_side, right_side, preferred_element_type=jnp.float32)


def matmul_tn(left_side, right_side):
    return lax.dot_general(
        left_side, right_side, (((0,), (0,)), ((), ())), preferred_element_type=jnp.float32
    )


def matmul_nt(left_side, right_side):
    return lax.dot_general(
        left_side, right_side, (((1,), (1,)), ((), ())), preferred_element_type=jnp.float32
    )


def column_blocks(matrix, width):
    return [matrix[:, k : k + width] for k in range(0, matrix.shape[1], width)]


def gelu_parts(values):
    size = jnp.abs(values) * 0.7071067811865476
    ratio = 1.0 / (1.0 + 0.3275911 * size)
    bell = jnp.exp(-0.5 * values * values)
    series = 1.421413741 + ratio * (-1.453152027 + ratio * 1.061405429)
    series = ratio * (0.254829592 + ratio * (-0.284496736 + ratio * series))
    tail = 0.5 * series * bell
    below = jnp.where(values < 0, tail, 1.0 - tail)
    return values * below, below + values * bell * 0.3989422804014327


def flat_rows(value):
    return value.reshape(-1, value.shape[-1])


def whole(array):
    return pl.BlockSpec(array.shape, lambda *_: (0,) * array.ndim)


class Weights:
    def __init__(self, arrays, shares):
        self.arrays = arrays
        self.starts = [sum(shares[:k]) for k in range(len(shares))]
        self.shares = shares

    def natural(self, index, core):
        span = slice(self.starts[index], self.starts[index] + self.shares[index])
        pieces = [array[:, span] for array in self.arrays]
        if len(pieces) == 2:
            pieces = [jnp.stack(in_order(*pieces, core), axis=1)]
        return flat_rows(pieces[0].reshape(-1, *pieces[0].shape[-2:]))

    def operands(self, index, core, columns, column_map, parts=1, part_map=lambda *_: 0):
        share, start = self.shares[index], self.starts[index]
        if share % 8 or start % share:
            array = self.natural(index, core)
            rows = array.shape[0] // parts
            spec = pl.BlockSpec((rows, columns), lambda *i: (part_map(*i), column_map(*i)))
            return [array], [spec]
        place = start // share
        specs = [
            pl.BlockSpec(
                (array.shape[0] // parts, share, columns),
                lambda *i: (part_map(*i), place, column_map(*i)),
            )
            for array in self.arrays
        ]
        return list(self.arrays), specs


def up_operands_of(weights, steps):
    share = weights.shares[0]
    width = weights.arrays[0].shape[-1]
    if share % 8:
        array = jnp.concatenate([weights.natural(k, None) for k in range(steps)], axis=1)
        return [array], [pl.BlockSpec((array.shape[0], width), lambda s, *_: (0, s))]
    array = weights.arrays[0]
    return [array], [pl.BlockSpec((array.shape[0], share, width), lambda s, *_: (0, s, 0))]


def in_order(mine, other, core):
    return jnp.where(core == 0, mine, other), jnp.where(core == 0, other, mine)


def read_weight(refs, core):
    if len(refs) == 1:
        return flat_rows(refs[0][...])
    return flat_rows(jnp.stack(in_order(refs[0][...], refs[1][...], core), axis=1))


def pack_kernel(*refs, layout):
    *sources, out_ref = refs
    for source, (column, row, rows, columns) in zip(sources, layout):
        for k in range(column):
            out_ref[row[k] : row[k] + rows, :] = source[:, k * columns : (k + 1) * columns]


def pack_rows(pieces):
    width = pieces[0][0].shape[1] // len(pieces[0][1])
    total = max(row + m.shape[0] for m, rows in pieces for row in rows)
    if any(row % 8 for _, rows in pieces for row in rows):
        placed = sorted(
            (row, m[:, k * width : (k + 1) * width])
            for m, rows in pieces
            for k, row in enumerate(rows)
        )
        return jnp.concatenate([block for _, block in placed], axis=0)
    matrices = [m for m, _ in pieces]
    layout = [(len(rows), tuple(rows), m.shape[0], width) for m, rows in pieces]
    return pl.pallas_call(
        functools.partial(pack_kernel, layout=layout),
        grid=(1,),
        in_specs=[whole(m) for m in matrices],
        out_specs=pl.BlockSpec((total, width), lambda i: (0, 0)),
        out_shape=jax.ShapeDtypeStruct((total, width), matrices[0].dtype),
        name="pack_rows",
    )(*matrices)


def pack_later_kernel(flags_ref, targets_ref, *refs, layout, label_place):
    *sources, out_ref = refs
    pack_kernel(*sources, out_ref, layout=layout)
    count = flags_ref.shape[1]
    flags = jnp.broadcast_to(flags_ref[...], (8, count))
    row = lax.broadcasted_iota(jnp.int32, (count, count), 0)
    column = lax.broadcasted_iota(jnp.int32, (count, count), 1)
    until = to_low(jnp.where(row <= column, 1.0, 0.0))
    rank = matmul(to_low(flags.astype(jnp.float32)), until)[:1] - 1.0
    slot = lax.broadcasted_iota(jnp.int32, (MAXM, count), 0).astype(jnp.float32)
    picker = to_low(jnp.where((slot == rank) & (flags_ref[...] > 0), 1.0, 0.0))
    shifted = targets_ref[...] + 1
    high = lax.shift_right_logical(shifted, 8)
    level = lax.broadcasted_iota(jnp.int32, (8, count), 0)
    halves = jnp.where(level == 0, high, jnp.where(level == 1, shifted - high * 256, 0))
    labels = matmul_nt(to_low(halves.astype(jnp.float32)), picker)
    empty = jnp.zeros((8, out_ref.shape[1] - MAXM), jnp.float32)
    out_ref[label_place : label_place + 8, :] = to_low(jnp.concatenate([labels, empty], axis=1))


def pack_later(pieces, mask_flags, targets):
    width = pieces[0][0].shape[1] // len(pieces[0][1])
    label_place = max(row + m.shape[0] for m, rows in pieces for row in rows)
    if any(row % 8 for _, rows in pieces for row in rows) or label_place % 8:
        rank = jnp.cumsum(mask_flags) - 1
        picker = (jnp.arange(MAXM)[:, None] == rank[None, :]) & (mask_flags > 0)[None, :]
        shifted = jnp.sum(jnp.where(picker, targets[None, :] + 1, 0), axis=1)
        labels = jnp.stack([shifted // 256, shifted % 256]).astype(jnp.bfloat16)
        labels = jnp.pad(labels, ((0, 6), (0, width - MAXM)))
        return pack_rows([*pieces, (labels, [label_place])])
    matrices = [m for m, _ in pieces]
    layout = [(len(rows), tuple(rows), m.shape[0], width) for m, rows in pieces]
    operands = [mask_flags[None], targets[None], *matrices]
    return pl.pallas_call(
        functools.partial(pack_later_kernel, layout=layout, label_place=label_place),
        grid=(1,),
        in_specs=[whole(operand) for operand in operands],
        out_specs=pl.BlockSpec((label_place + 8, width), lambda i: (0, 0)),
        out_shape=jax.ShapeDtypeStruct((label_place + 8, width), matrices[0].dtype),
        name="pack_later",
    )(*operands)


def place_kernel(index, line_ref, out_ref, *, plan):
    rows, width = out_ref.shape
    device = index[0]
    line = jnp.broadcast_to(line_ref[...], (8, width))
    lane = lax.broadcasted_iota(jnp.int32, (rows, width), 1)
    level = lax.broadcasted_iota(jnp.int32, (rows, width), 0)
    out = jnp.zeros((rows, width), jnp.float32)
    for first_row, start, share in plan:
        spot = device * share
        row, place = first_row + spot // width, spot % width
        moved = pltpu.roll(line, lax.rem(place - start + width, width), 1)
        here = (level == row) & (lane >= place) & (lane < place + share)
        out = jnp.where(here, jnp.broadcast_to(moved[:1], (rows, width)), out)
    out_ref[...] = out.astype(out_ref.dtype)


def place_shares(device, vectors, first_rows, rows, width):
    plan = []
    line = 0.0
    start = 0
    for vector, first_row in zip(vectors, first_rows):
        end = start + vector.shape[0]
        plan.append((first_row, start, vector.shape[0]))
        line = line + jnp.pad(to_full(vector), (start, width - end))
        start = end
    line = line[None, :]
    return pl.pallas_call(
        functools.partial(place_kernel, plan=plan),
        grid_spec=pltpu.PrefetchScalarGridSpec(
            num_scalar_prefetch=1,
            grid=(1,),
            in_specs=[whole(line)],
            out_specs=pl.BlockSpec((rows, width), lambda i, d: (0, 0)),
        ),
        out_shape=jax.ShapeDtypeStruct((rows, width), jnp.bfloat16),
        name="place_shares",
    )(device.reshape(1), line)


def double(value, stride, axis):
    chips = lax.axis_size("dp")
    bit = (lax.axis_index("dp") // stride) % 2
    arrived = lax.ppermute(value, "dp", [(chip, chip ^ stride) for chip in range(chips)])
    low, high = in_order(value, arrived, bit)
    return jnp.stack([low, high], axis=axis)


def gather_pair(value, split):
    chips = lax.axis_size("dp")
    stride = 4
    value = value[None]
    while stride < chips:
        value = double(value, stride, 0)
        value = value.reshape(-1, *value.shape[2:])
        stride *= 2
    upper, lower = value[:, :split], value[:, split:]
    upper, lower = double(upper, 1, 1), double(lower, 2, 1)
    upper, lower = double(upper, 2, 1), double(lower, 1, 2)
    upper, lower = (part.reshape(chips, *part.shape[-2:]) for part in (upper, lower))
    swap = [(0, 1), (1, 0)]
    return (upper, lax.ppermute(upper, "fsdp", swap)), (lower, lax.ppermute(lower, "fsdp", swap))


def attention_kernel(core, *refs, sizes):
    ends = [0]
    for size in sizes:
        ends.append(ends[-1] + size)
    weights = [refs[ends[k] : ends[k + 1]] for k in range(len(sizes))]
    (tokens_ref, bias_ref, vector_ref, down_ref, across_ref) = refs[ends[-1] : ends[-1] + 5]
    (q_ref, k_ref, v_ref, context_ref, total_ref, summed_ref, hidden_ref) = refs[ends[-1] + 5 : -2]
    mask_ref, all_ref = refs[-2:]
    step = pl.program_id(0)

    @pl.when(step == 0)
    def _():
        mask_ref[...] = jnp.where(down_ref[...] == across_ref[...], 0.0, NEGATIVE)

    tokens = tokens_ref[...]
    queries = to_low(matmul(tokens, read_weight(weights[0], core[0])) + bias_ref[0:1, :])
    keys = to_low(matmul(tokens, read_weight(weights[1], core[0])))
    values = to_low(matmul(tokens, read_weight(weights[2], core[0])) + bias_ref[1:2, :])
    q_ref[...], k_ref[...], v_ref[...] = queries, keys, values
    heads = queries.shape[1] // HEAD_DIM
    pair_width = 2 * HEAD_DIM
    lane = lax.broadcasted_iota(jnp.int32, (1, pair_width), 1)
    for pair in range(heads // 2):
        span = slice(pair_width * pair, pair_width * (pair + 1))
        scaled = to_full(queries[:, span]) * HEAD_DIM ** (-0.5)
        sides = []
        for side in range(2):
            mine = to_low(jnp.where((lane < HEAD_DIM) == (side == 0), scaled, 0.0))
            scores = matmul_nt(keys[:, span], mine) + mask_ref[...]
            peak = jnp.max(scores, axis=0, keepdims=True)
            exponent = jnp.exp(scores - peak)
            total = jnp.sum(exponent, axis=0, keepdims=True)
            total_ref[pl.ds(step * heads + 2 * pair + side, 1), :] = peak + jnp.log(total)
            softmax_low = to_low(exponent * (1.0 / total))
            mixed = matmul_tn(values[:, span], softmax_low)
            sides.append(mixed[HEAD_DIM * side : HEAD_DIM * (side + 1)])
        context = to_low(jnp.concatenate(sides, axis=0).T)
        context_ref[:, span] = context
        all_ref[step * (heads // 2) + pair] = context

    @pl.when(step == pl.num_programs(0) - 1)
    def _():
        pairs = all_ref.shape[0]
        context = jnp.concatenate([all_ref[k] for k in range(pairs)], axis=1)
        product = matmul(context, read_weight(weights[3], core[0]))
        summed = to_full(tokens_ref[...]) + product + vector_ref[2:3, :]
        summed_ref[...] = summed
        hidden_ref[...] = to_low(layer_norm(summed, vector_ref[3:4, :], vector_ref[4:5, :]))


def attention_forward(core, tokens, segments, weights, vectors):
    rows, width = tokens.shape
    columns = 256
    arrays, specs, sizes = [], [], []
    for k, (group, index) in enumerate(weights):
        size, place = (columns, lambda s, c: s) if k < 3 else (width, lambda s, c: 0)
        some, their = group.operands(index, core, size, place)
        arrays, specs, sizes = arrays + some, specs + their, sizes + [len(some)]
    down, across = segments[:, None], segments[None, :]
    block = pl.BlockSpec((rows, columns), lambda s, c: (0, s))
    head_rows = 16
    return pl.pallas_call(
        functools.partial(attention_kernel, sizes=sizes),
        grid_spec=pltpu.PrefetchScalarGridSpec(
            num_scalar_prefetch=1,
            grid=(width // columns,),
            in_specs=[
                *specs,
                whole(tokens),
                pl.BlockSpec((8, columns), lambda s, c: (0, s)),
                whole(vectors),
                whole(down),
                whole(across),
            ],
            out_specs=[
                block,
                block,
                block,
                block,
                pl.BlockSpec((head_rows, rows), lambda s, c: (0, 0)),
                whole(tokens),
                whole(tokens),
            ],
            scratch_shapes=[
                pltpu.VMEM((rows, rows), jnp.float32),
                pltpu.VMEM((width // (2 * HEAD_DIM), rows, 2 * HEAD_DIM), jnp.bfloat16),
            ],
        ),
        out_shape=[
            *[jax.ShapeDtypeStruct((rows, width), jnp.bfloat16)] * 4,
            jax.ShapeDtypeStruct((head_rows, rows), jnp.float32),
            jax.ShapeDtypeStruct((rows, width), jnp.float32),
            jax.ShapeDtypeStruct((rows, width), jnp.bfloat16),
        ],
        compiler_params=pltpu.CompilerParams(dimension_semantics=("arbitrary",)),
        name="attention_forward",
    )(core.reshape(1), *arrays, tokens, vectors, vectors, down, across)


def ffn_kernel(*refs, sizes):
    up_refs, down_refs = refs[: sizes[0]], refs[sizes[0] : sum(sizes)]
    hidden_ref, bias_ref, vector_ref = refs[sum(sizes) : sum(sizes) + 3]
    active_ref, slope_ref, summed_ref, output_ref, total_ref = refs[sum(sizes) + 3 :]
    step = pl.program_id(0)
    up, down = read_weight(up_refs, None), read_weight(down_refs, None)
    pre_act = matmul(hidden_ref[...], up) + bias_ref[pl.ds(step, 1), :]
    active, slope = gelu_parts(pre_act)
    active = to_low(active)
    active_ref[...] = active
    slope_ref[...] = slope
    part = matmul(active, down)

    @pl.when(step == 0)
    def _():
        total_ref[...] = part

    @pl.when(step > 0)
    def _():
        total_ref[...] += part

    @pl.when(step == pl.num_programs(0) - 1)
    def _():
        summed = to_full(hidden_ref[...]) + total_ref[...] + vector_ref[5:6, :]
        summed_ref[...] = summed
        output_ref[...] = to_low(layer_norm(summed, vector_ref[6:7, :], vector_ref[7:8, :]))


def ffn_forward(hidden, weights, up_bias, vectors):
    rows, width = hidden.shape
    steps = len(weights.shares) - 2
    first, first_specs = up_operands_of(weights, steps)
    second, second_specs = weights.operands(steps, None, width, lambda s: 0, steps, lambda s: s)
    block = pl.BlockSpec((rows, width), lambda s: (0, s))
    return pl.pallas_call(
        functools.partial(ffn_kernel, sizes=[len(first), len(second)]),
        grid=(steps,),
        in_specs=[*first_specs, *second_specs, whole(hidden), whole(up_bias), whole(vectors)],
        out_specs=[block, block, whole(hidden), whole(hidden)],
        out_shape=[
            jax.ShapeDtypeStruct((rows, steps * width), jnp.bfloat16),
            jax.ShapeDtypeStruct((rows, steps * width), jnp.float32),
            jax.ShapeDtypeStruct((rows, width), jnp.float32),
            jax.ShapeDtypeStruct((rows, width), jnp.bfloat16),
        ],
        scratch_shapes=[pltpu.VMEM((rows, width), jnp.float32)],
        compiler_params=pltpu.CompilerParams(dimension_semantics=("arbitrary",)),
        name="ffn_forward",
    )(*first, *second, hidden, up_bias, vectors)


def head_kernel(*refs, size):
    weight_refs = refs[:size]
    picker_ref, output_ref, vector_ref, own_ref, dense_ref, normed_ref = refs[size:]
    own = to_low(matmul(picker_ref[...], output_ref[...]))
    own_ref[...] = own
    dense = matmul(own, read_weight(weight_refs, None)) + vector_ref[4:5, :]
    dense_ref[...] = dense
    active = gelu_parts(dense)[0]
    normed_ref[...] = to_low(layer_norm(active, vector_ref[5:6, :], vector_ref[6:7, :]))


def head_forward(picker, output, group, index, vectors):
    slots, width = picker.shape[0], output.shape[1]
    arrays, specs = group.operands(index, None, width, lambda s: 0)
    operands = [picker, output, vectors]
    out_shape = [
        jax.ShapeDtypeStruct((slots, width), kind)
        for kind in (jnp.bfloat16, jnp.float32, jnp.bfloat16)
    ]
    return pl.pallas_call(
        functools.partial(head_kernel, size=len(arrays)),
        grid=(1,),
        in_specs=[*specs, *[whole(operand) for operand in operands]],
        out_specs=[whole(shape) for shape in out_shape],
        out_shape=out_shape,
        name="head_forward",
    )(*arrays, *operands)


def norm_backward(summed, gain_row, grad):
    center = summed - jnp.mean(summed, axis=-1, keepdims=True)
    scale = lax.rsqrt(jnp.mean(center * center, axis=-1, keepdims=True) + EPSILON)
    unit = center * scale
    inner = grad * gain_row
    mean = jnp.mean(inner, axis=-1, keepdims=True)
    along = jnp.mean(inner * unit, axis=-1, keepdims=True)
    gain_grad = jnp.sum(grad * unit, axis=0, keepdims=True)
    shift_grad = jnp.sum(grad, axis=0, keepdims=True)
    return scale * (inner - mean - unit * along), gain_grad, shift_grad


def feed_back_kernel(place, *refs, sizes, share, down_share):
    up_refs, down_refs = refs[: sizes[0]], refs[sizes[0] : sizes[0] + sizes[1]]
    head_refs = refs[sizes[0] + sizes[1] : sum(sizes)]
    (cotangent_ref, picker_ref, summed_ref, vector_ref, own_ref, dense_ref) = refs[
        sum(sizes) : sum(sizes) + 6
    ]
    hidden_ref, active_ref, slope_ref, total_ref, sums_ref, *outs = refs[sum(sizes) + 6 : -2]
    low_ref, turned_ref = refs[-2:]
    step = pl.program_id(0)
    width = vector_ref.shape[1]

    @pl.when(step == 0)
    def _():
        picked_grad = to_low(matmul_nt(dense_ref[...], read_weight(head_refs, None)))
        grad = to_full(cotangent_ref[...]) + matmul_tn(picker_ref[...], picked_grad)
        summed_grad, gain_grad, shift_grad = norm_backward(
            summed_ref[...], vector_ref[6:7, :], grad
        )
        total_ref[...] = summed_grad
        low = to_low(summed_grad)
        low_ref[...] = low
        turned_ref[...] = hidden_ref[...].T
        sums_ref[...] = jnp.zeros_like(sums_ref)
        sums_ref[0:1, :] = jnp.sum(to_full(low), axis=0, keepdims=True)
        sums_ref[1:2, :] = gain_grad
        sums_ref[2:3, :] = shift_grad
        dense_grad = to_low(matmul_tn(own_ref[...], dense_ref[...]))
        if down_share:
            store_blocks(outs, dense_grad, place, share, slice(2 * down_share, None))
        else:
            outs[2][...] = dense_grad

    low = low_ref[...]
    up, down = read_weight(up_refs, None), read_weight(down_refs, None)
    down_grad = to_low(matmul_tn(active_ref[...], low))
    pre_grad = to_low(matmul_nt(low, down) * slope_ref[...])
    total_ref[...] += matmul_nt(pre_grad, up)
    sums_ref[pl.ds(3 + step, 1), :] = jnp.sum(to_full(pre_grad), axis=0, keepdims=True)
    up_grad = to_low(matmul(turned_ref[...], pre_grad))
    if down_share:
        chips = width // (2 * down_share)
        rows = slice(down_share, 2 * down_share)
        store_blocks(outs, down_grad, place, down_share, rows, step * chips)
        rows = pl.ds(pl.multiple_of(step * share, share), share)
        store_blocks(outs, up_grad, place, share, rows)
    else:
        outs[0][...] = up_grad
        outs[1][...] = down_grad


def feed_backward(place, count, cotangent, picker, summed, vectors, own, dense, hidden, active, slope, weights):
    rows, width = cotangent.shape
    steps = active.shape[1] // width
    share, down_share, chips = width // count, active.shape[1] // count, count // 2
    aligned = share % 8 == 0
    first, first_specs = up_operands_of(weights, steps)
    second, second_specs = weights.operands(steps, None, width, lambda s, c: 0, steps, lambda s, c: s)
    third, third_specs = weights.operands(steps + 1, None, width, lambda s, c: 0)
    operands = [cotangent, picker, summed, vectors, own, dense, hidden]
    block = pl.BlockSpec((rows, width), lambda s, c: (0, s))
    low = jnp.bfloat16
    if aligned:
        shape = jax.ShapeDtypeStruct((chips, 2 * down_share + share, width // 2), low)
        out_shape, out_specs = [shape] * 4, [whole(shape)] * 4
    else:
        out_shape = [
            jax.ShapeDtypeStruct((width, steps * width), low),
            jax.ShapeDtypeStruct((steps * width, width), low),
            jax.ShapeDtypeStruct((width, width), low),
        ]
        out_specs = [
            pl.BlockSpec((width, width), lambda s, c: (0, s)),
            pl.BlockSpec((width, width), lambda s, c: (s, 0)),
            whole(out_shape[2]),
        ]
    common = [
        jax.ShapeDtypeStruct((rows, width), jnp.float32),
        jax.ShapeDtypeStruct((8, width), jnp.float32),
    ]
    kernel = functools.partial(
        feed_back_kernel,
        sizes=[len(first), len(second), len(third)],
        share=share,
        down_share=down_share if aligned else 0,
    )
    hidden_grad, sums, *outs = pl.pallas_call(
        kernel,
        grid_spec=pltpu.PrefetchScalarGridSpec(
            num_scalar_prefetch=1,
            grid=(steps,),
            in_specs=[
                *first_specs,
                *second_specs,
                *third_specs,
                *[whole(operand) for operand in operands],
                block,
                block,
            ],
            out_specs=[*[whole(shape) for shape in common], *out_specs],
            scratch_shapes=[pltpu.VMEM((rows, width), low), pltpu.VMEM((width, rows), low)],
        ),
        out_shape=[*common, *out_shape],
        compiler_params=pltpu.CompilerParams(dimension_semantics=("arbitrary",)),
        name="feed_backward",
    )(place, *first, *second, *third, *operands, active, slope)
    if not aligned:
        away, kept = arranged([*column_blocks(outs[0], width), *outs[1:]], place)
    else:
        away, kept = outs[:2], outs[2:]
    return hidden_grad, sums, away, kept


def out_back_kernel(core, *refs, size):
    weight_refs = refs[:size]
    grad_ref, summed_ref, vector_ref, total_ref, low_ref, back_ref, sums_ref = refs[size:]
    width = vector_ref.shape[1]
    summed_grad, gain_grad, shift_grad = norm_backward(
        summed_ref[...], vector_ref[3:4, :], grad_ref[...]
    )
    total_ref[...] = summed_grad
    low = to_low(summed_grad)
    low_ref[...] = low
    bias_grad = jnp.sum(to_full(low), axis=0, keepdims=True)
    zero = jnp.zeros((5, width), jnp.float32)
    sums_ref[...] = jnp.concatenate([bias_grad, gain_grad, shift_grad, zero], axis=0)
    back_ref[...] = to_low(matmul_nt(low, read_weight(weight_refs, core[0])))


def out_backward(core, hidden_grad, summed, vectors, group, index):
    rows, width = hidden_grad.shape
    arrays, specs = group.operands(index, core, width, lambda s, c: 0)
    operands = [hidden_grad, summed, vectors]
    out_shape = [
        jax.ShapeDtypeStruct((rows, width), jnp.float32),
        jax.ShapeDtypeStruct((rows, width), jnp.bfloat16),
        jax.ShapeDtypeStruct((rows, width), jnp.bfloat16),
        jax.ShapeDtypeStruct((8, width), jnp.float32),
    ]
    return pl.pallas_call(
        functools.partial(out_back_kernel, size=len(arrays)),
        grid_spec=pltpu.PrefetchScalarGridSpec(
            num_scalar_prefetch=1,
            grid=(1,),
            in_specs=[*specs, *[whole(operand) for operand in operands]],
            out_specs=[whole(shape) for shape in out_shape],
        ),
        out_shape=out_shape,
        name="out_backward",
    )(core.reshape(1), *arrays, *operands)


def attention_back_kernel(*refs, first_head):
    (grad_ref, q_ref, k_ref, v_ref, total_ref, down_ref, across_ref) = refs[:7]
    dq_ref, dk_ref, dv_ref, sums_ref, mask_ref = refs[7:]
    step = pl.program_id(0)

    @pl.when(step == 0)
    def _():
        mask_ref[...] = jnp.where(down_ref[...] == across_ref[...], 0.0, NEGATIVE)

    pair_width = 2 * HEAD_DIM
    scale = HEAD_DIM ** (-0.5)
    lane = lax.broadcasted_iota(jnp.int32, (1, pair_width), 1)
    columns = q_ref.shape[1]
    heads = columns // HEAD_DIM
    for pair in range(heads // 2):
        span = slice(pair_width * pair, pair_width * (pair + 1))
        queries, keys, values = q_ref[:, span], k_ref[:, span], v_ref[:, span]
        grads = grad_ref[:, span]
        scaled = to_full(queries) * scale
        sides = []
        for side in range(2):
            here = (lane < HEAD_DIM) == (side == 0)
            mine = to_low(jnp.where(here, scaled, 0.0))
            my_grads = jnp.where(here, grads, jnp.zeros_like(grads))
            head = first_head + step * heads + 2 * pair + side
            scores = matmul_nt(keys, mine) + mask_ref[...]
            softmax = jnp.exp(scores - total_ref[pl.ds(head, 1), :])
            softmax_grad = matmul_nt(values, my_grads)
            inner = jnp.sum(softmax * softmax_grad, axis=0, keepdims=True)
            score_grad = to_low(softmax * (softmax_grad - inner))
            query_grad = matmul_tn(keys, score_grad)[HEAD_DIM * side : HEAD_DIM * (side + 1)]
            sides.append((query_grad, matmul(score_grad, mine), matmul(to_low(softmax), my_grads)))
        query_grad = to_low(jnp.concatenate([sides[0][0], sides[1][0]], axis=0).T * scale)
        value_grad = to_low(sides[0][2] + sides[1][2])
        dq_ref[:, span] = query_grad
        dk_ref[:, span] = to_low(sides[0][1] + sides[1][1])
        dv_ref[:, span] = value_grad
        sums_ref[0:1, span] = jnp.sum(to_full(query_grad), axis=0, keepdims=True)
        sums_ref[1:2, span] = jnp.sum(to_full(value_grad), axis=0, keepdims=True)


def attention_backward(context_grad, queries, keys, values, score_total, segments, start, columns):
    rows = context_grad.shape[0]
    size = 2 * HEAD_DIM
    down, across = segments[:, None], segments[None, :]
    block = pl.BlockSpec((rows, size), lambda s: (0, start // size + s))
    out_block = pl.BlockSpec((rows, size), lambda s: (0, s))
    return pl.pallas_call(
        functools.partial(attention_back_kernel, first_head=start // HEAD_DIM),
        grid=(columns // size,),
        in_specs=[*[block] * 4, whole(score_total), whole(down), whole(across)],
        out_specs=[*[out_block] * 3, pl.BlockSpec((8, size), lambda s: (0, s))],
        out_shape=[
            *[jax.ShapeDtypeStruct((rows, columns), jnp.bfloat16)] * 3,
            jax.ShapeDtypeStruct((8, columns), jnp.float32),
        ],
        scratch_shapes=[pltpu.VMEM((rows, rows), jnp.float32)],
        compiler_params=pltpu.CompilerParams(dimension_semantics=("arbitrary",)),
        name="attention_backward",
    )(context_grad, queries, keys, values, score_total, down, across)


def joined_sums(bias_sums, out_sums, feed_sums, head_sums, steps):
    return jnp.concatenate(
        [
            jnp.concatenate([part[:2] for part in bias_sums], axis=1),
            out_sums[:3],
            feed_sums[: 3 + steps],
            head_sums[: 8 - steps],
        ],
        axis=0,
    )


def last_grads_kernel(place, *refs, parts, share, steps):
    tokens_ref, context_ref, branch_ref, out_sums_ref, feed_sums_ref, head_sums_ref, *rest = refs
    mixed_refs, rest = rest[: 3 * parts], rest[3 * parts :]
    bias_refs, outs = rest[:parts], rest[parts:]
    turned = tokens_ref[...].T
    for which in range(3):
        for part in range(parts):
            mixed = mixed_refs[3 * part + which][...]
            columns = mixed.shape[1]
            grad = to_low(matmul(turned, mixed))
            if share:
                rows = slice(share * which, share * (which + 1))
                store_blocks(outs, grad, place, share, rows, column=columns * part)
            else:
                outs[which][:, columns * part : columns * (part + 1)] = grad
    grad = to_low(matmul_tn(context_ref[...], branch_ref[...]))
    if share:
        store_blocks(outs, grad, place, share, slice(3 * share, 4 * share))
        small = to_low(
            joined_sums(
                [ref[...] for ref in bias_refs],
                out_sums_ref[...],
                feed_sums_ref[...],
                head_sums_ref[...],
                steps,
            )
        )
        half = small.shape[1] // 2
        for index, out_ref in enumerate(outs):
            part = small[:, half * (index % 2) : half * (index % 2 + 1)]
            out_ref[:, 4 * share :, :] = jnp.broadcast_to(
                part[None], (out_ref.shape[0], *part.shape)
            )
    else:
        outs[3][...] = grad


def last_grads(place, count, tokens, context, branch_grad, sums, steps, mixed):
    width = tokens.shape[1]
    share, chips = width // count, count // 2
    aligned = share % 8 == 0
    parts = len(mixed)
    biases = [part[3] for part in mixed]
    mixed = [part[:3] for part in mixed]
    operands = [tokens, context, branch_grad, *sums, *[m for part in mixed for m in part], *biases]
    small = joined_sums(biases, *sums, steps)
    if aligned:
        rows = 4 * share + small.shape[0]
        out_shape = [jax.ShapeDtypeStruct((chips, rows, width // 2), jnp.bfloat16)] * 4
    else:
        out_shape = [jax.ShapeDtypeStruct((width, width), jnp.bfloat16)] * 4
    outs = pl.pallas_call(
        functools.partial(
            last_grads_kernel, parts=parts, share=share if aligned else 0, steps=steps
        ),
        grid_spec=pltpu.PrefetchScalarGridSpec(
            num_scalar_prefetch=1,
            grid=(1,),
            in_specs=[whole(operand) for operand in operands],
            out_specs=[whole(shape) for shape in out_shape],
        ),
        out_shape=out_shape,
        name="last_grads",
    )(place, *operands)
    if not aligned:
        both = jnp.broadcast_to(to_low(small)[None], (count, *small.shape))
        return arranged([*outs, both.reshape(-1, width)], place)
    return outs[:2], outs[2:]


def tokens_back_kernel(core, *refs, sizes, parts):
    ends = [sum(sizes[:k]) for k in range(4)]
    weights = [refs[ends[k] : ends[k + 1]] for k in range(3)]
    summed_ref, *mixed_refs, out_ref = refs[ends[3] :]
    total = summed_ref[...]
    for which in range(3):
        weight = read_weight(weights[which], core[0])
        for part in range(parts):
            mixed = mixed_refs[3 * part + which][...]
            columns = mixed.shape[1]
            total += matmul_nt(mixed, weight[:, columns * part : columns * (part + 1)])
    out_ref[...] = total


def tokens_backward(core, summed_grad, mixed, weights):
    width = summed_grad.shape[1]
    arrays, specs, sizes = [], [], []
    for group, index in weights:
        some, their = group.operands(index, core, width, lambda s, c: 0)
        arrays, specs, sizes = arrays + some, specs + their, sizes + [len(some)]
    operands = [summed_grad, *[matrix for part in mixed for matrix in part]]
    return pl.pallas_call(
        functools.partial(tokens_back_kernel, sizes=sizes, parts=len(mixed)),
        grid_spec=pltpu.PrefetchScalarGridSpec(
            num_scalar_prefetch=1,
            grid=(1,),
            in_specs=[*specs, *[whole(operand) for operand in operands]],
            out_specs=whole(summed_grad),
        ),
        out_shape=jax.ShapeDtypeStruct(summed_grad.shape, jnp.float32),
        name="tokens_backward",
    )(core.reshape(1), *arrays, *operands)


def take_kernel(index, whole_ref, *out_refs, plan):
    width = whole_ref.shape[1]
    for out_ref, (first_row, share) in zip(out_refs, plan):
        spot = index[0] * share
        row, place = first_row + spot // width, spot % width
        line = jnp.broadcast_to(whole_ref[pl.ds(row, 1), :], (8, width))
        moved = pltpu.roll(line, lax.rem(width - place, width), 1)
        out_ref[...] = moved[:1, :share]


def take_shares(device, values, first_rows, shares):
    shapes = [jax.ShapeDtypeStruct((1, share), jnp.float32) for share in shares]
    lines = pl.pallas_call(
        functools.partial(take_kernel, plan=list(zip(first_rows, shares))),
        grid_spec=pltpu.PrefetchScalarGridSpec(
            num_scalar_prefetch=1,
            grid=(1,),
            in_specs=[whole(values)],
            out_specs=[whole(shape) for shape in shapes],
        ),
        out_shape=shapes,
        name="take_shares",
    )(device.reshape(1), values)
    return [line[0] for line in lines]


def take(value, axis, index):
    return lax.dynamic_index_in_dim(value, index, axis, keepdims=False)


def add_low(first, second):
    return to_low(to_full(first) + to_full(second))


def halve(value, axis, stride):
    chips = lax.axis_size("dp")
    bit = (lax.axis_index("dp") // stride) % 2
    pairs = [(chip, chip ^ stride) for chip in range(chips)]
    arrived = lax.ppermute(take(value, axis, 1 - bit), "dp", pairs)
    return add_low(take(value, axis, bit), arrived)


def core_swap(away):
    return lax.ppermute(away, "fsdp", [(0, 1), (1, 0)])


def along(sent, stride):
    chips = lax.axis_size("dp")
    return lax.ppermute(sent, "dp", [(chip, chip ^ stride) for chip in range(chips)])


def total_of(addends):
    total = to_full(addends[0])
    for addend in addends[1:]:
        total = total + to_full(addend)
    return total


def my_place():
    chip = lax.axis_index("dp")
    return jnp.stack([lax.axis_index("fsdp"), chip % 2, (chip // 2) % 2, chip // 4])


def chip_at(index, place, levels, first_axis):
    outer, level = index // levels, index % levels
    bits = (outer // 2, outer % 2) if first_axis == 0 else (outer % 2, outer // 2)
    return ((place[3] ^ level) * 2 + (place[2] ^ bits[1])) * 2 + (place[1] ^ bits[0])


def index_of(chip, place, levels, first_axis):
    bits = ((chip % 2) ^ place[1], ((chip // 2) % 2) ^ place[2])
    outer = 2 * bits[first_axis] + bits[1 - first_axis]
    return outer * levels + ((chip // 4) ^ place[3])


class ChipSum:
    def __init__(self, away, kept):
        self.sides = [[part] for part in kept]
        self.strides = [[1, 2], [2, 1]]
        self.arrived = [core_swap(part) for part in away]

    def add(self, arrived):
        for side, part in zip(self.sides, arrived):
            side.append(part)

    def sends(self):
        sent = [to_low(total_of([a[a.shape[0] // 2 :] for a in side])) for side in self.sides]
        self.sides = [[a[: a.shape[0] // 2] for a in side] for side in self.sides]
        return sent

    def start(self, sent):
        self.arrived = [along(part, strides.pop(0)) for part, strides in zip(sent, self.strides)]

    def level_block(self, level):
        return jnp.concatenate(
            [total_of([a[level] for a in side]) for side in self.sides], axis=-1
        )

    def level_sends(self):
        while self.sides[0][0].shape[0] > 4:
            stride = 4 * (self.sides[0][0].shape[0] // 2)
            sent = self.sends()
            self.add([along(part, stride) for part in sent])
        levels = self.sides[0][0].shape[0]
        return [to_low(self.level_block(level)) for level in range(1, levels)]

    def start_levels(self, sent):
        self.arrived = [along(part, 4 * (level + 1)) for level, part in enumerate(sent)]

    def result(self, arrived):
        return total_of([self.level_block(0), *arrived])


def arranged(matrices, place):
    chips = lax.axis_size("dp")
    value = jnp.concatenate(
        [matrix.reshape(chips, 2, -1, matrix.shape[-1]) for matrix in matrices], axis=2
    )
    half = value.shape[-1] // 2
    sides = []
    for core in (1 - place[0], place[0]):
        mine = take(value, 1, core)
        sides.append(
            [
                jnp.take(
                    mine[..., axis * half : (axis + 1) * half],
                    chip_at(jnp.arange(chips), place, chips // 4, axis),
                    axis=0,
                )
                for axis in range(2)
            ]
        )
    return sides


def store_blocks(outs, value, place, share, rows, first_chip=0, column=0):
    columns = value.shape[-1]
    split = value.reshape(-1, 2, share, columns)
    kept, away = in_order(split[:, 0], split[:, 1], place[0])
    levels = outs[0].shape[0] // 4
    width = outs[0].shape[-1]
    for chip in range(split.shape[0]):
        for which, half in enumerate((away, kept)):
            for axis in range(2):
                low, high = max(column, axis * width), min(column + columns, (axis + 1) * width)
                if low >= high:
                    continue
                spot = index_of(first_chip + chip, place, levels, axis)
                outs[2 * which + axis][
                    pl.ds(spot, 1), rows, low - axis * width : high - axis * width
                ] = half[chip : chip + 1, :, low - column : high - column]


def tie(value, *others):
    return lax.optimization_barrier((value, *others))


def window_base(start, total, window):
    return pl.multiple_of(jnp.minimum((start // 16) * 16, total - window), 16)


def compact_kernel(place, places, counts, indices, mine_ref, other_ref, *refs, window, levels):
    step = pl.program_id(0)
    *before, out_ref = refs

    @pl.when(step == 0)
    def _():
        out_ref[...] = before[0][...] if before else jnp.zeros_like(out_ref)

    _, batch, slots, half = mine_ref.shape
    total = out_ref.shape[0]
    for which, ref in enumerate((mine_ref, other_ref)):
        core = place[0] if which == 0 else 1 - place[0]
        for axis in range(2):
            for lane in range(batch):
                index = indices[step * batch + lane]
                source = 2 * chip_at(index, place, levels, axis) + core
                start = places[source]
                base = window_base(start, total, window)
                row = lax.broadcasted_iota(jnp.int32, (window, slots), 0) + (base - start)
                column = lax.broadcasted_iota(jnp.int32, (window, slots), 1)
                chosen = jnp.where((row == column) & (column < counts[source]), 1.0, 0.0)
                moved = matmul(to_low(chosen), ref[axis, lane])
                out_ref[pl.ds(base, window), half * axis : half * (axis + 1)] += to_low(moved)


def compact(place, places, counts, mine, other, indices, total, before=()):
    _, blocks, slots, half = mine.shape
    levels = lax.axis_size("dp") // 4
    batch = blocks // 2 if blocks <= 16 else 2
    block = pl.BlockSpec((2, batch, slots, half), lambda i, *_: (0, i, 0, 0))
    return pl.pallas_call(
        functools.partial(compact_kernel, window=slots + 16, levels=levels),
        grid_spec=pltpu.PrefetchScalarGridSpec(
            num_scalar_prefetch=4,
            grid=(blocks // batch,),
            in_specs=[block, block, *[whole(rows) for rows in before]],
            out_specs=pl.BlockSpec((total, 2 * half), lambda i, *_: (0, 0)),
        ),
        out_shape=jax.ShapeDtypeStruct((total, 2 * half), jnp.bfloat16),
        compiler_params=pltpu.CompilerParams(dimension_semantics=("arbitrary",)),
        name="compact_rows",
    )(place, places, counts, jnp.array(indices, jnp.int32), mine, other, *before)


def compact_labels_kernel(places, counts, lines_ref, out_ref):
    out_ref[...] = jnp.zeros_like(out_ref)
    sources, slots = lines_ref.shape
    total = out_ref.shape[1]
    wide = 2 * slots
    lane = lax.broadcasted_iota(jnp.int32, (8, wide), 1)

    def place_one(source, carry):
        start = places[source]
        base = pl.multiple_of(jnp.minimum(start // slots * slots, total - wide), slots)
        shift = start - base
        line = jnp.broadcast_to(to_full(lines_ref[pl.ds(source, 1), :]), (8, slots))
        line = jnp.concatenate([line, jnp.zeros_like(line)], axis=1)
        moved = pltpu.roll(line, lax.rem(shift, wide), 1)
        here = (lane >= shift) & (lane < shift + counts[source])
        span = pl.ds(base, wide)
        out_ref[:, span] = jnp.where(here, moved, out_ref[:, span])
        return carry

    lax.fori_loop(0, sources, place_one, 0)


def compact_labels(places, counts, lines, total):
    out = pl.pallas_call(
        compact_labels_kernel,
        grid_spec=pltpu.PrefetchScalarGridSpec(
            num_scalar_prefetch=2,
            grid=(1,),
            in_specs=[whole(lines)],
            out_specs=pl.BlockSpec((8, total), lambda *_: (0, 0)),
        ),
        out_shape=jax.ShapeDtypeStruct((8, total), jnp.float32),
        name="compact_labels",
    )(places, counts, lines)
    return out[0].astype(jnp.int32)


def block_order():
    levels = lax.axis_size("dp") // 4
    near = [*range(levels), *range(2 * levels, 3 * levels), levels, 3 * levels]
    return near, [k for k in range(4 * levels) if k not in near]


def gather_blocks(value, beside, given):
    chips = lax.axis_size("dp")
    levels = chips // 4
    half = value.shape[-1] // 2
    if levels <= 4:
        others = jnp.stack([along(value, 4 * level) for level in range(1, levels)])
    else:
        others = value[None]
        while others.shape[0] < levels:
            others = jnp.concatenate([others, along(others, 4 * others.shape[0])])
        others = others[1:]
    own = [value[:, :half], value[:, half:]]
    strides = [(1, 2), (2, 1)]
    near = [along(part, first) for part, (first, _) in zip(own, strides)]
    far_sent = [jnp.stack([part, got]) for part, got in zip(own, near)]
    others = tie(others, *far_sent)[0]
    far = [along(sent, second) for sent, (_, second) in zip(far_sent, strides)]
    rest = [others[..., :half], others[..., half:]]
    near_rest = [along(part, first) for part, (first, _) in zip(rest, strides)]
    given, *near_rest = tie(given, *near_rest)
    far_rest = [
        along(jnp.concatenate([part, got]), second)
        for part, got, (_, second) in zip(rest, near_rest, strides)
    ]
    early = jnp.stack(
        [
            jnp.concatenate([own[k][None], rest[k], near[k][None], near_rest[k], far[k]])
            for k in range(2)
        ]
    )
    results = beside(early, core_swap(early), given)
    tied = tie(*far_rest, *results)
    late = jnp.stack(tied[:2])
    return late, core_swap(late), tied[2:]


def spread_kernel(place, places, counts, rows_ref, *out_refs, window):
    step = pl.program_id(0)
    total = rows_ref.shape[0]
    batch, slots, half = out_refs[0].shape
    levels = pl.num_programs(0) * batch // 4
    for which in range(2):
        core = 1 - place[0] if which == 0 else place[0]
        for axis in range(2):
            for lane in range(batch):
                chip = chip_at(step * batch + lane, place, levels, axis)
                source = 2 * chip + core
                start = places[source]
                base = window_base(start, total, window)
                row = lax.broadcasted_iota(jnp.int32, (slots, window), 0)
                column = lax.broadcasted_iota(jnp.int32, (slots, window), 1) + (base - start)
                chosen = jnp.where((row == column) & (row < counts[source]), 1.0, 0.0)
                moved = matmul(
                    to_low(chosen), rows_ref[pl.ds(base, window), half * axis : half * (axis + 1)]
                )
                out_refs[2 * which + axis][lane] = to_low(moved)


def spread(place, places, counts, rows, slots):
    chips = places.shape[0] // 2
    total, width = rows.shape
    batch = 4
    block = pl.BlockSpec((batch, slots, width // 2), lambda i, *_: (i, 0, 0))
    shape = jax.ShapeDtypeStruct((chips, slots, width // 2), jnp.bfloat16)
    outs = pl.pallas_call(
        functools.partial(spread_kernel, window=slots + 16),
        grid_spec=pltpu.PrefetchScalarGridSpec(
            num_scalar_prefetch=3,
            grid=(chips // batch,),
            in_specs=[
                pl.BlockSpec((total, width), lambda i, *_: (0, 0), pipeline_mode=pl.Buffered(1))
            ],
            out_specs=[block] * 4,
        ),
        out_shape=[shape] * 4,
        compiler_params=pltpu.CompilerParams(dimension_semantics=("arbitrary",)),
        name="spread_rows",
    )(place, places, counts, rows)
    return outs[:2], outs[2:]


def per_device(
    tokens,
    segments,
    mask_flags,
    targets,
    cotangent,
    qkv_weight,
    attn_bias,
    out_weight,
    out_bias,
    attn_gain,
    attn_shift,
    up_weight,
    up_bias,
    down_weight,
    down_bias,
    ffn_gain,
    ffn_shift,
    dense_weight,
    dense_bias,
    head_gain,
    head_shift,
    decoder,
    vocab_bias,
):
    count = lax.axis_size(AXES)
    width = tokens.shape[1]
    core = lax.axis_index("fsdp")
    device = lax.axis_index(AXES)
    here = my_place()
    blocks = qkv_weight.shape[1] // width
    steps = up_weight.shape[1] // width
    share, up_share, down_share = out_weight.shape[0], up_weight.shape[0], down_weight.shape[0]
    label_place = up_share * steps + down_share + share
    later_packed = pack_later(
        [
            (up_weight, [up_share * k for k in range(steps)]),
            (down_weight, [up_share * steps]),
            (dense_weight, [up_share * steps + down_share]),
        ],
        mask_flags,
        targets,
    )
    later_gathered = lax.all_gather(later_packed, AXES, axis=0)
    later = Weights([later_gathered], [*[up_share] * steps, down_share, share])
    small = (
        attn_bias,
        out_bias,
        attn_gain,
        attn_shift,
        down_bias,
        ffn_gain,
        ffn_shift,
        up_bias,
        dense_bias,
        head_gain,
        head_shift,
    )
    small_rows = (0, 2, 3, 4, 5, 6, 7, 8, 12, 13, 14)
    placed = place_shares(device, small, small_rows, 16, width)
    half = 2 * share + 8
    first_packed = pack_rows(
        [
            (qkv_weight, [0, share, half]),
            (placed[:8], [2 * share]),
            (out_weight, [half + share]),
            (placed[8:], [half + 2 * share]),
        ]
    )
    upper, lower = gather_pair(first_packed, half)
    first_group, second_group = (Weights(list(pair), [share, share, 8]) for pair in (upper, lower))
    vectors, more_vectors = (
        sum(jnp.sum(to_full(array[:, 2 * share :]), axis=0) for array in pair)
        for pair in (upper, lower)
    )
    queries, keys_low, values_low, context, score_total, summed1, hidden = attention_forward(
        core,
        tokens,
        segments,
        [(first_group, 0), (first_group, 1), (second_group, 0), (second_group, 1)],
        vectors,
    )
    active, slope, summed2, output = ffn_forward(hidden, later, more_vectors[:4], vectors)
    head_gain_full, head_shift_full = more_vectors[5], more_vectors[6]
    mask_rank = jnp.cumsum(mask_flags) - 1
    slot_place = jnp.where(mask_flags > 0, mask_rank, -1)
    picker_low = (jnp.arange(MAXM)[:, None] == slot_place[None, :]).astype(jnp.bfloat16)
    own_rows, dense, normed_low = head_forward(picker_low, output, later, steps + 1, more_vectors)
    _, tail_back = jax.vjp(head_tail, dense, head_gain_full, head_shift_full)
    chips = count // 2
    group = MASK_DEV * chips
    total = 2 * group
    gathered_late, normed_low = tie(later_gathered, normed_low)
    label_parts = gathered_late[:, label_place : label_place + 2, :MAXM].astype(jnp.int32)
    label_lines = label_parts[:, 0] * 256 + label_parts[:, 1] - 1
    counts = jnp.sum((label_lines >= 0).astype(jnp.int32), axis=1)
    by_core = counts.reshape(chips, 2)
    earlier = jnp.arange(chips)[:, None] < jnp.arange(chips)[None, :]
    places = jnp.sum(jnp.where(earlier[:, :, None], by_core[:, None, :], 0), axis=0)
    places = (places + jnp.arange(2)[None, :] * group).reshape(count)
    all_labels = compact_labels(places, counts, label_lines, total)
    slice_index = lax.axis_index(AXES)
    vocab_rows = decoder.shape[0]
    local_label = all_labels - slice_index * vocab_rows
    label_hit = jnp.arange(vocab_rows)[None, :] == local_label[:, None]

    early_order, late_order = block_order()

    def beside_last(mine, other, chosen):
        hit = jnp.arange(vocab_rows)[None, :] == chosen[:, None]
        pulled = to_low(matmul(hit.astype(jnp.bfloat16), decoder))
        return compact(here, places, counts, mine, other, early_order, total), pulled

    mine, other, (early_rows, label_pull) = gather_blocks(normed_low, beside_last, local_label)
    late = (here, places, counts, mine, other, late_order, total)
    small_total = total <= 4096
    all_rows = compact(*late, (early_rows,)) if small_total else early_rows + compact(*late)
    logits = matmul_nt(all_rows, decoder) + to_full(vocab_bias)
    row_peak = jnp.max(logits, axis=1)
    exp_sums = jnp.sum(jnp.exp(logits - row_peak[:, None]), axis=1)
    label_sum = jnp.sum(jnp.where(label_hit, logits, 0.0))
    local_total = (row_peak + jnp.log(exp_sums)).reshape(-1, 128)
    lines = local_total.shape[0]
    merged = jnp.concatenate(
        [local_total, jnp.pad(label_sum[None, None], ((0, 7), (0, 127)))], axis=0
    )
    is_total = jnp.arange(lines + 8)[:, None] < lines
    middle = total // 2
    pulls = []
    rounds = [[1], [2, 4, 6]]
    rounds += [[8, 16, 24]] if count == 32 else [[8 << k] for k in range((count // 8).bit_length() - 1)]
    for distances in rounds:
        arrived = [
            lax.ppermute(merged, AXES, [(place, place ^ far) for place in range(count)])
            for far in distances
        ]
        if len(pulls) < 2:
            rows = slice(middle * len(pulls), middle * (len(pulls) + 1))
            pull = matmul(to_low(jnp.exp(logits[rows] - row_peak[rows, None])), decoder)
            *arrived, pull = tie(*arrived, pull)
            pulls.append(pull)
        every = [merged, *arrived]
        peak = functools.reduce(jnp.maximum, every)
        both = peak + jnp.log(sum(jnp.exp(part - peak) for part in every))
        merged = jnp.where(is_total, both, sum(every))
    log_total = merged[:lines].reshape(total)
    mean_loss = (jnp.sum(log_total) - merged[lines, 0]) / total
    scale = jnp.exp(row_peak - log_total)[:, None]
    rows_part = jnp.concatenate(
        [
            to_low(pull * scale[rows] - to_full(label_pull[rows]))
            for pull, rows in zip(pulls, (slice(0, middle), slice(middle, total)))
        ]
    )
    rows_sum = ChipSum(*spread(here, places, counts, rows_part, MAXM))
    rows_sum.add(rows_sum.arrived)
    rows_sum.start(rows_sum.sends())
    logit_grad = to_low(jnp.exp(logits - log_total[:, None]) - label_hit.astype(jnp.float32))
    vocab_bias_grad = jnp.sum(to_full(logit_grad), axis=0)
    logit_grad, vocab_bias_grad, *arrived = tie(logit_grad, vocab_bias_grad, *rows_sum.arrived)
    rows_sum.add(arrived)
    rows_sum.start(rows_sum.sends())
    decoder_grad = matmul_tn(logit_grad, all_rows)
    decoder_grad, *arrived = tie(decoder_grad, *rows_sum.arrived)
    rows_sum.add(arrived)
    rows_sum.start_levels(rows_sum.level_sends())
    normed_grad = rows_sum.result(rows_sum.arrived)
    dense_grad, head_gain_grad, head_shift_grad = tail_back(normed_grad)
    dense_grad_low = to_low(dense_grad)
    dense_bias_grad = jnp.sum(to_full(dense_grad_low), axis=0)
    hidden_grad, feed_sums, *feed_grads = feed_backward(
        here,
        count,
        cotangent,
        picker_low,
        summed2,
        vectors,
        own_rows,
        dense_grad_low,
        hidden,
        active,
        slope,
        later,
    )
    first = ChipSum(*feed_grads)
    summed1_grad, branch1_grad, context_grad, out_sums = out_backward(
        core, hidden_grad, summed1, vectors, second_group, 1
    )
    context_grad, *arrived = tie(context_grad, *first.arrived)
    first.add(arrived)
    context_grad, *sent = tie(context_grad, *first.sends())
    first.start(sent)
    saved = (queries, keys_low, values_low, score_total, segments)
    middle = width // 2
    mixed = [list(attention_backward(context_grad, *saved, 0, middle))]
    mixed[0][0], context_grad = tie(mixed[0][0], context_grad)
    mixed.append(list(attention_backward(context_grad, *saved, middle, width - middle)))
    head_sums = jnp.stack(
        [dense_bias_grad, head_gain_grad, head_shift_grad, *[jnp.zeros((width,))] * 5]
    )
    away, kept = last_grads(
        here, count, tokens, context, branch1_grad, (out_sums, feed_sums, head_sums), steps, mixed
    )
    mixed = [part[:3] for part in mixed]
    second = ChipSum(away, kept)
    mixed[0][0], _, *arrived = tie(mixed[0][0], away[0], *first.arrived)
    first.add(arrived)
    mixed[0][0], *sent = tie(mixed[0][0], *first.sends())
    first.start(sent)
    mixed[0][0], *arrived = tie(mixed[0][0], *second.arrived)
    second.add(arrived)
    mixed[0][0], *sent = tie(mixed[0][0], *second.sends())
    second.start(sent)
    tokens_grad = tokens_backward(
        core, summed1_grad, mixed, [(first_group, 0), (first_group, 1), (second_group, 0)]
    )
    first.add(first.arrived)
    first.start_levels(first.level_sends())
    second.add(second.arrived)
    second.start(second.sends())
    second.add(second.arrived)
    sent = second.level_sends()
    first.arrived[0] = tie(first.arrived[0], *sent)[0]
    second.start_levels(sent)
    first, second = first.result(first.arrived), second.result(second.arrived)
    up_pieces = [first[share * k : share * (k + 1)] for k in range(steps)]
    down_piece = first[up_share * steps : up_share * steps + down_share]
    dense_piece = first[up_share * steps + down_share :]
    qkv_pieces = [second[share * k : share * (k + 1)] for k in range(blocks)]
    out_piece = second[share * blocks : share * (blocks + 1)]
    small_pieces = take_shares(
        device, second[share * (blocks + 1) :], small_rows, [vector.shape[0] for vector in small]
    )
    return (
        output,
        mean_loss,
        tokens_grad,
        jnp.concatenate(qkv_pieces, axis=1),
        small_pieces[0],
        out_piece,
        *small_pieces[1:4],
        jnp.concatenate(up_pieces, axis=1),
        small_pieces[7],
        down_piece,
        *small_pieces[4:7],
        dense_piece,
        *small_pieces[8:],
        decoder_grad,
        vocab_bias_grad,
    )


def solution(mesh):
    matrix_spec = P(AXES, None)
    vector_spec = P(AXES)
    m, v = matrix_spec, vector_spec
    return jax.shard_map(
        per_device,
        mesh=mesh,
        in_specs=(m, v, v, v, m, m, v, m, v, v, v, m, v, m, v, v, v, m, v, v, v, m, v),
        out_specs=(m, P(), m, m, v, m, v, v, v, m, v, m, v, v, v, m, v, v, v, m, v),
        check_vma=False,
    )
```

```python
import functools

import jax
import jax.numpy as jnp
from jax import lax
from jax.experimental import pallas as pl
from jax.experimental.pallas import tpu as pltpu
from jax.sharding import PartitionSpec as P

HEADS = 12
HEAD_DIM = 64
MASK_DEV = 64
MAXM = 128

EPSILON = 1e-05
NEGATIVE = -1e30
AXES = ("dp", "fsdp")


def to_low(values):
    return values.astype(jnp.bfloat16)


def to_full(values):
    return values.astype(jnp.float32)


def layer_norm(values, gain_vector, shift_vector):
    center = values - jnp.mean(values, axis=-1, keepdims=True)
    spread = jnp.mean(center * center, axis=-1, keepdims=True)
    return center * lax.rsqrt(spread + EPSILON) * gain_vector + shift_vector


def gelu_exact(values):
    return jax.nn.gelu(values, approximate=False)


def head_tail(dense_out, gain_vector, shift_vector):
    return layer_norm(gelu_exact(dense_out), gain_vector, shift_vector)


def matmul(left_side, right_side):
    return jnp.dot(left_side, right_side, preferred_element_type=jnp.float32)


def matmul_tn(left_side, right_side):
    return lax.dot_general(
        left_side, right_side, (((0,), (0,)), ((), ())), preferred_element_type=jnp.float32
    )


def matmul_nt(left_side, right_side):
    return lax.dot_general(
        left_side, right_side, (((1,), (1,)), ((), ())), preferred_element_type=jnp.float32
    )


def column_blocks(matrix, width):
    return [matrix[:, k : k + width] for k in range(0, matrix.shape[1], width)]


def gelu_parts(values):
    size = jnp.abs(values) * 0.7071067811865476
    ratio = 1.0 / (1.0 + 0.3275911 * size)
    bell = jnp.exp(-0.5 * values * values)
    series = 1.421413741 + ratio * (-1.453152027 + ratio * 1.061405429)
    series = ratio * (0.254829592 + ratio * (-0.284496736 + ratio * series))
    tail = 0.5 * series * bell
    below = jnp.where(values < 0, tail, 1.0 - tail)
    return values * below, below + values * bell * 0.3989422804014327


def flat_rows(value):
    return value.reshape(-1, value.shape[-1])


def whole(array):
    return pl.BlockSpec(array.shape, lambda *_: (0,) * array.ndim)


class Weights:
    def __init__(self, arrays, shares):
        self.arrays = arrays
        self.starts = [sum(shares[:k]) for k in range(len(shares))]
        self.shares = shares

    def natural(self, index, core):
        span = slice(self.starts[index], self.starts[index] + self.shares[index])
        pieces = [array[:, span] for array in self.arrays]
        if len(pieces) == 2:
            pieces = [jnp.stack(in_order(*pieces, core), axis=1)]
        return flat_rows(pieces[0].reshape(-1, *pieces[0].shape[-2:]))

    def operands(self, index, core, columns, column_map, parts=1, part_map=lambda *_: 0):
        share, start = self.shares[index], self.starts[index]
        if share % 8 or start % share:
            array = self.natural(index, core)
            rows = array.shape[0] // parts
            spec = pl.BlockSpec((rows, columns), lambda *i: (part_map(*i), column_map(*i)))
            return [array], [spec]
        place = start // share
        specs = [
            pl.BlockSpec(
                (array.shape[0] // parts, share, columns),
                lambda *i: (part_map(*i), place, column_map(*i)),
            )
            for array in self.arrays
        ]
        return list(self.arrays), specs


def up_operands_of(weights, steps):
    share = weights.shares[0]
    width = weights.arrays[0].shape[-1]
    if share % 8:
        array = jnp.concatenate([weights.natural(k, None) for k in range(steps)], axis=1)
        return [array], [pl.BlockSpec((array.shape[0], width), lambda s, *_: (0, s))]
    array = weights.arrays[0]
    return [array], [pl.BlockSpec((array.shape[0], share, width), lambda s, *_: (0, s, 0))]


def in_order(mine, other, core):
    return jnp.where(core == 0, mine, other), jnp.where(core == 0, other, mine)


def read_weight(refs, core):
    if len(refs) == 1:
        return flat_rows(refs[0][...])
    return flat_rows(jnp.stack(in_order(refs[0][...], refs[1][...], core), axis=1))


def pack_kernel(*refs, layout):
    *sources, out_ref = refs
    for source, (column, row, rows, columns) in zip(sources, layout):
        for k in range(column):
            out_ref[row[k] : row[k] + rows, :] = source[:, k * columns : (k + 1) * columns]


def pack_rows(pieces):
    width = pieces[0][0].shape[1] // len(pieces[0][1])
    total = max(row + m.shape[0] for m, rows in pieces for row in rows)
    if any(row % 8 for _, rows in pieces for row in rows):
        placed = sorted(
            (row, m[:, k * width : (k + 1) * width])
            for m, rows in pieces
            for k, row in enumerate(rows)
        )
        return jnp.concatenate([block for _, block in placed], axis=0)
    matrices = [m for m, _ in pieces]
    layout = [(len(rows), tuple(rows), m.shape[0], width) for m, rows in pieces]
    return pl.pallas_call(
        functools.partial(pack_kernel, layout=layout),
        grid=(1,),
        in_specs=[whole(m) for m in matrices],
        out_specs=pl.BlockSpec((total, width), lambda i: (0, 0)),
        out_shape=jax.ShapeDtypeStruct((total, width), matrices[0].dtype),
        name="pack_rows",
    )(*matrices)


def pack_later_kernel(flags_ref, targets_ref, *refs, layout, label_place):
    *sources, out_ref = refs
    pack_kernel(*sources, out_ref, layout=layout)
    count = flags_ref.shape[1]
    flags = jnp.broadcast_to(flags_ref[...], (8, count))
    row = lax.broadcasted_iota(jnp.int32, (count, count), 0)
    column = lax.broadcasted_iota(jnp.int32, (count, count), 1)
    until = to_low(jnp.where(row <= column, 1.0, 0.0))
    rank = matmul(to_low(flags.astype(jnp.float32)), until)[:1] - 1.0
    slot = lax.broadcasted_iota(jnp.int32, (MAXM, count), 0).astype(jnp.float32)
    picker = to_low(jnp.where((slot == rank) & (flags_ref[...] > 0), 1.0, 0.0))
    shifted = targets_ref[...] + 1
    high = lax.shift_right_logical(shifted, 8)
    level = lax.broadcasted_iota(jnp.int32, (8, count), 0)
    halves = jnp.where(level == 0, high, jnp.where(level == 1, shifted - high * 256, 0))
    labels = matmul_nt(to_low(halves.astype(jnp.float32)), picker)
    empty = jnp.zeros((8, out_ref.shape[1] - MAXM), jnp.float32)
    out_ref[label_place : label_place + 8, :] = to_low(jnp.concatenate([labels, empty], axis=1))


def pack_later(pieces, mask_flags, targets):
    width = pieces[0][0].shape[1] // len(pieces[0][1])
    label_place = max(row + m.shape[0] for m, rows in pieces for row in rows)
    if any(row % 8 for _, rows in pieces for row in rows) or label_place % 8:
        rank = jnp.cumsum(mask_flags) - 1
        picker = (jnp.arange(MAXM)[:, None] == rank[None, :]) & (mask_flags > 0)[None, :]
        shifted = jnp.sum(jnp.where(picker, targets[None, :] + 1, 0), axis=1)
        labels = jnp.stack([shifted // 256, shifted % 256]).astype(jnp.bfloat16)
        labels = jnp.pad(labels, ((0, 6), (0, width - MAXM)))
        return pack_rows([*pieces, (labels, [label_place])])
    matrices = [m for m, _ in pieces]
    layout = [(len(rows), tuple(rows), m.shape[0], width) for m, rows in pieces]
    operands = [mask_flags[None], targets[None], *matrices]
    return pl.pallas_call(
        functools.partial(pack_later_kernel, layout=layout, label_place=label_place),
        grid=(1,),
        in_specs=[whole(operand) for operand in operands],
        out_specs=pl.BlockSpec((label_place + 8, width), lambda i: (0, 0)),
        out_shape=jax.ShapeDtypeStruct((label_place + 8, width), matrices[0].dtype),
        name="pack_later",
    )(*operands)


def place_kernel(index, line_ref, out_ref, *, plan):
    rows, width = out_ref.shape
    device = index[0]
    line = jnp.broadcast_to(line_ref[...], (8, width))
    lane = lax.broadcasted_iota(jnp.int32, (rows, width), 1)
    level = lax.broadcasted_iota(jnp.int32, (rows, width), 0)
    out = jnp.zeros((rows, width), jnp.float32)
    for first_row, start, share in plan:
        spot = device * share
        row, place = first_row + spot // width, spot % width
        moved = pltpu.roll(line, lax.rem(place - start + width, width), 1)
        here = (level == row) & (lane >= place) & (lane < place + share)
        out = jnp.where(here, jnp.broadcast_to(moved[:1], (rows, width)), out)
    out_ref[...] = out.astype(out_ref.dtype)


def place_shares(device, vectors, first_rows, rows, width):
    plan = []
    line = 0.0
    start = 0
    for vector, first_row in zip(vectors, first_rows):
        end = start + vector.shape[0]
        plan.append((first_row, start, vector.shape[0]))
        line = line + jnp.pad(to_full(vector), (start, width - end))
        start = end
    line = line[None, :]
    return pl.pallas_call(
        functools.partial(place_kernel, plan=plan),
        grid_spec=pltpu.PrefetchScalarGridSpec(
            num_scalar_prefetch=1,
            grid=(1,),
            in_specs=[whole(line)],
            out_specs=pl.BlockSpec((rows, width), lambda i, d: (0, 0)),
        ),
        out_shape=jax.ShapeDtypeStruct((rows, width), jnp.bfloat16),
        name="place_shares",
    )(device.reshape(1), line)


def double(value, stride, axis):
    chips = lax.axis_size("dp")
    bit = (lax.axis_index("dp") // stride) % 2
    arrived = lax.ppermute(value, "dp", [(chip, chip ^ stride) for chip in range(chips)])
    low, high = in_order(value, arrived, bit)
    return jnp.stack([low, high], axis=axis)


def gather_pair(value, split):
    chips = lax.axis_size("dp")
    stride = 4
    value = value[None]
    while stride < chips:
        value = double(value, stride, 0)
        value = value.reshape(-1, *value.shape[2:])
        stride *= 2
    upper, lower = value[:, :split], value[:, split:]
    upper, lower = double(upper, 1, 1), double(lower, 2, 1)
    upper, lower = double(upper, 2, 1), double(lower, 1, 2)
    upper, lower = (part.reshape(chips, *part.shape[-2:]) for part in (upper, lower))
    swap = [(0, 1), (1, 0)]
    return (upper, lax.ppermute(upper, "fsdp", swap)), (lower, lax.ppermute(lower, "fsdp", swap))


def attention_kernel(core, *refs, sizes):
    ends = [0]
    for size in sizes:
        ends.append(ends[-1] + size)
    weights = [refs[ends[k] : ends[k + 1]] for k in range(len(sizes))]
    (tokens_ref, bias_ref, vector_ref, down_ref, across_ref) = refs[ends[-1] : ends[-1] + 5]
    (q_ref, k_ref, v_ref, context_ref, total_ref, summed_ref, hidden_ref) = refs[ends[-1] + 5 : -2]
    mask_ref, all_ref = refs[-2:]
    step = pl.program_id(0)

    @pl.when(step == 0)
    def _():
        mask_ref[...] = jnp.where(down_ref[...] == across_ref[...], 0.0, NEGATIVE)

    tokens = tokens_ref[...]
    queries = to_low(matmul(tokens, read_weight(weights[0], core[0])) + bias_ref[0:1, :])
    keys = to_low(matmul(tokens, read_weight(weights[1], core[0])))
    values = to_low(matmul(tokens, read_weight(weights[2], core[0])) + bias_ref[1:2, :])
    q_ref[...], k_ref[...], v_ref[...] = queries, keys, values
    heads = queries.shape[1] // HEAD_DIM
    pair_width = 2 * HEAD_DIM
    lane = lax.broadcasted_iota(jnp.int32, (1, pair_width), 1)
    for pair in range(heads // 2):
        span = slice(pair_width * pair, pair_width * (pair + 1))
        scaled = to_full(queries[:, span]) * HEAD_DIM ** (-0.5)
        sides = []
        for side in range(2):
            mine = to_low(jnp.where((lane < HEAD_DIM) == (side == 0), scaled, 0.0))
            scores = matmul_nt(keys[:, span], mine) + mask_ref[...]
            peak = jnp.max(scores, axis=0, keepdims=True)
            exponent = jnp.exp(scores - peak)
            total = jnp.sum(exponent, axis=0, keepdims=True)
            total_ref[pl.ds(step * heads + 2 * pair + side, 1), :] = peak + jnp.log(total)
            softmax_low = to_low(exponent * (1.0 / total))
            mixed = matmul_tn(values[:, span], softmax_low)
            sides.append(mixed[HEAD_DIM * side : HEAD_DIM * (side + 1)])
        context = to_low(jnp.concatenate(sides, axis=0).T)
        context_ref[:, span] = context
        all_ref[step * (heads // 2) + pair] = context

    @pl.when(step == pl.num_programs(0) - 1)
    def _():
        pairs = all_ref.shape[0]
        context = jnp.concatenate([all_ref[k] for k in range(pairs)], axis=1)
        product = matmul(context, read_weight(weights[3], core[0]))
        summed = to_full(tokens_ref[...]) + product + vector_ref[2:3, :]
        summed_ref[...] = summed
        hidden_ref[...] = to_low(layer_norm(summed, vector_ref[3:4, :], vector_ref[4:5, :]))


def attention_forward(core, tokens, segments, weights, vectors):
    rows, width = tokens.shape
    columns = 256
    arrays, specs, sizes = [], [], []
    for k, (group, index) in enumerate(weights):
        size, place = (columns, lambda s, c: s) if k < 3 else (width, lambda s, c: 0)
        some, their = group.operands(index, core, size, place)
        arrays, specs, sizes = arrays + some, specs + their, sizes + [len(some)]
    down, across = segments[:, None], segments[None, :]
    block = pl.BlockSpec((rows, columns), lambda s, c: (0, s))
    head_rows = 16
    return pl.pallas_call(
        functools.partial(attention_kernel, sizes=sizes),
        grid_spec=pltpu.PrefetchScalarGridSpec(
            num_scalar_prefetch=1,
            grid=(width // columns,),
            in_specs=[
                *specs,
                whole(tokens),
                pl.BlockSpec((8, columns), lambda s, c: (0, s)),
                whole(vectors),
                whole(down),
                whole(across),
            ],
            out_specs=[
                block,
                block,
                block,
                block,
                pl.BlockSpec((head_rows, rows), lambda s, c: (0, 0)),
                whole(tokens),
                whole(tokens),
            ],
            scratch_shapes=[
                pltpu.VMEM((rows, rows), jnp.float32),
                pltpu.VMEM((width // (2 * HEAD_DIM), rows, 2 * HEAD_DIM), jnp.bfloat16),
            ],
        ),
        out_shape=[
            *[jax.ShapeDtypeStruct((rows, width), jnp.bfloat16)] * 4,
            jax.ShapeDtypeStruct((head_rows, rows), jnp.float32),
            jax.ShapeDtypeStruct((rows, width), jnp.float32),
            jax.ShapeDtypeStruct((rows, width), jnp.bfloat16),
        ],
        compiler_params=pltpu.CompilerParams(dimension_semantics=("arbitrary",)),
        name="attention_forward",
    )(core.reshape(1), *arrays, tokens, vectors, vectors, down, across)


def ffn_kernel(*refs, sizes):
    up_refs, down_refs = refs[: sizes[0]], refs[sizes[0] : sum(sizes)]
    hidden_ref, bias_ref, vector_ref = refs[sum(sizes) : sum(sizes) + 3]
    active_ref, slope_ref, summed_ref, output_ref, total_ref = refs[sum(sizes) + 3 :]
    step = pl.program_id(0)
    up, down = read_weight(up_refs, None), read_weight(down_refs, None)
    pre_act = matmul(hidden_ref[...], up) + bias_ref[pl.ds(step, 1), :]
    active, slope = gelu_parts(pre_act)
    active = to_low(active)
    active_ref[...] = active
    slope_ref[...] = slope
    part = matmul(active, down)

    @pl.when(step == 0)
    def _():
        total_ref[...] = part

    @pl.when(step > 0)
    def _():
        total_ref[...] += part

    @pl.when(step == pl.num_programs(0) - 1)
    def _():
        summed = to_full(hidden_ref[...]) + total_ref[...] + vector_ref[5:6, :]
        summed_ref[...] = summed
        output_ref[...] = to_low(layer_norm(summed, vector_ref[6:7, :], vector_ref[7:8, :]))


def ffn_forward(hidden, weights, up_bias, vectors):
    rows, width = hidden.shape
    steps = len(weights.shares) - 2
    first, first_specs = up_operands_of(weights, steps)
    second, second_specs = weights.operands(steps, None, width, lambda s: 0, steps, lambda s: s)
    block = pl.BlockSpec((rows, width), lambda s: (0, s))
    return pl.pallas_call(
        functools.partial(ffn_kernel, sizes=[len(first), len(second)]),
        grid=(steps,),
        in_specs=[*first_specs, *second_specs, whole(hidden), whole(up_bias), whole(vectors)],
        out_specs=[block, block, whole(hidden), whole(hidden)],
        out_shape=[
            jax.ShapeDtypeStruct((rows, steps * width), jnp.bfloat16),
            jax.ShapeDtypeStruct((rows, steps * width), jnp.float32),
            jax.ShapeDtypeStruct((rows, width), jnp.float32),
            jax.ShapeDtypeStruct((rows, width), jnp.bfloat16),
        ],
        scratch_shapes=[pltpu.VMEM((rows, width), jnp.float32)],
        compiler_params=pltpu.CompilerParams(dimension_semantics=("arbitrary",)),
        name="ffn_forward",
    )(*first, *second, hidden, up_bias, vectors)


def head_kernel(*refs, size):
    weight_refs = refs[:size]
    picker_ref, output_ref, vector_ref, own_ref, dense_ref, normed_ref = refs[size:]
    own = to_low(matmul(picker_ref[...], output_ref[...]))
    own_ref[...] = own
    dense = matmul(own, read_weight(weight_refs, None)) + vector_ref[4:5, :]
    dense_ref[...] = dense
    active = gelu_parts(dense)[0]
    normed_ref[...] = to_low(layer_norm(active, vector_ref[5:6, :], vector_ref[6:7, :]))


def head_forward(picker, output, group, index, vectors):
    slots, width = picker.shape[0], output.shape[1]
    arrays, specs = group.operands(index, None, width, lambda s: 0)
    operands = [picker, output, vectors]
    out_shape = [
        jax.ShapeDtypeStruct((slots, width), kind)
        for kind in (jnp.bfloat16, jnp.float32, jnp.bfloat16)
    ]
    return pl.pallas_call(
        functools.partial(head_kernel, size=len(arrays)),
        grid=(1,),
        in_specs=[*specs, *[whole(operand) for operand in operands]],
        out_specs=[whole(shape) for shape in out_shape],
        out_shape=out_shape,
        name="head_forward",
    )(*arrays, *operands)


def norm_backward(summed, gain_row, grad):
    center = summed - jnp.mean(summed, axis=-1, keepdims=True)
    scale = lax.rsqrt(jnp.mean(center * center, axis=-1, keepdims=True) + EPSILON)
    unit = center * scale
    inner = grad * gain_row
    mean = jnp.mean(inner, axis=-1, keepdims=True)
    along = jnp.mean(inner * unit, axis=-1, keepdims=True)
    gain_grad = jnp.sum(grad * unit, axis=0, keepdims=True)
    shift_grad = jnp.sum(grad, axis=0, keepdims=True)
    return scale * (inner - mean - unit * along), gain_grad, shift_grad


def feed_back_kernel(place, *refs, sizes, share, down_share):
    up_refs, down_refs = refs[: sizes[0]], refs[sizes[0] : sizes[0] + sizes[1]]
    head_refs = refs[sizes[0] + sizes[1] : sum(sizes)]
    (cotangent_ref, picker_ref, summed_ref, vector_ref, own_ref, dense_ref) = refs[
        sum(sizes) : sum(sizes) + 6
    ]
    hidden_ref, active_ref, slope_ref, total_ref, sums_ref, *outs = refs[sum(sizes) + 6 : -2]
    low_ref, turned_ref = refs[-2:]
    step = pl.program_id(0)
    width = vector_ref.shape[1]

    @pl.when(step == 0)
    def _():
        picked_grad = to_low(matmul_nt(dense_ref[...], read_weight(head_refs, None)))
        grad = to_full(cotangent_ref[...]) + matmul_tn(picker_ref[...], picked_grad)
        summed_grad, gain_grad, shift_grad = norm_backward(
            summed_ref[...], vector_ref[6:7, :], grad
        )
        total_ref[...] = summed_grad
        low = to_low(summed_grad)
        low_ref[...] = low
        turned_ref[...] = hidden_ref[...].T
        sums_ref[...] = jnp.zeros_like(sums_ref)
        sums_ref[0:1, :] = jnp.sum(to_full(low), axis=0, keepdims=True)
        sums_ref[1:2, :] = gain_grad
        sums_ref[2:3, :] = shift_grad
        dense_grad = to_low(matmul_tn(own_ref[...], dense_ref[...]))
        if down_share:
            store_blocks(outs, dense_grad, place, share, slice(2 * down_share, None))
        else:
            outs[2][...] = dense_grad

    low = low_ref[...]
    up, down = read_weight(up_refs, None), read_weight(down_refs, None)
    down_grad = to_low(matmul_tn(active_ref[...], low))
    pre_grad = to_low(matmul_nt(low, down) * slope_ref[...])
    total_ref[...] += matmul_nt(pre_grad, up)
    sums_ref[pl.ds(3 + step, 1), :] = jnp.sum(to_full(pre_grad), axis=0, keepdims=True)
    up_grad = to_low(matmul(turned_ref[...], pre_grad))
    if down_share:
        chips = width // (2 * down_share)
        rows = slice(down_share, 2 * down_share)
        store_blocks(outs, down_grad, place, down_share, rows, step * chips)
        rows = pl.ds(pl.multiple_of(step * share, share), share)
        store_blocks(outs, up_grad, place, share, rows)
    else:
        outs[0][...] = up_grad
        outs[1][...] = down_grad


def feed_backward(place, count, cotangent, picker, summed, vectors, own, dense, hidden, active, slope, weights):
    rows, width = cotangent.shape
    steps = active.shape[1] // width
    share, down_share, chips = width // count, active.shape[1] // count, count // 2
    aligned = share % 8 == 0
    first, first_specs = up_operands_of(weights, steps)
    second, second_specs = weights.operands(steps, None, width, lambda s, c: 0, steps, lambda s, c: s)
    third, third_specs = weights.operands(steps + 1, None, width, lambda s, c: 0)
    operands = [cotangent, picker, summed, vectors, own, dense, hidden]
    block = pl.BlockSpec((rows, width), lambda s, c: (0, s))
    low = jnp.bfloat16
    if aligned:
        shape = jax.ShapeDtypeStruct((chips, 2 * down_share + share, width // 2), low)
        out_shape, out_specs = [shape] * 4, [whole(shape)] * 4
    else:
        out_shape = [
            jax.ShapeDtypeStruct((width, steps * width), low),
            jax.ShapeDtypeStruct((steps * width, width), low),
            jax.ShapeDtypeStruct((width, width), low),
        ]
        out_specs = [
            pl.BlockSpec((width, width), lambda s, c: (0, s)),
            pl.BlockSpec((width, width), lambda s, c: (s, 0)),
            whole(out_shape[2]),
        ]
    common = [
        jax.ShapeDtypeStruct((rows, width), jnp.float32),
        jax.ShapeDtypeStruct((8, width), jnp.float32),
    ]
    kernel = functools.partial(
        feed_back_kernel,
        sizes=[len(first), len(second), len(third)],
        share=share,
        down_share=down_share if aligned else 0,
    )
    hidden_grad, sums, *outs = pl.pallas_call(
        kernel,
        grid_spec=pltpu.PrefetchScalarGridSpec(
            num_scalar_prefetch=1,
            grid=(steps,),
            in_specs=[
                *first_specs,
                *second_specs,
                *third_specs,
                *[whole(operand) for operand in operands],
                block,
                block,
            ],
            out_specs=[*[whole(shape) for shape in common], *out_specs],
            scratch_shapes=[pltpu.VMEM((rows, width), low), pltpu.VMEM((width, rows), low)],
        ),
        out_shape=[*common, *out_shape],
        compiler_params=pltpu.CompilerParams(dimension_semantics=("arbitrary",)),
        name="feed_backward",
    )(place, *first, *second, *third, *operands, active, slope)
    if not aligned:
        away, kept = arranged([*column_blocks(outs[0], width), *outs[1:]], place)
    else:
        away, kept = outs[:2], outs[2:]
    return hidden_grad, sums, away, kept


def out_back_kernel(core, *refs, size):
    weight_refs = refs[:size]
    grad_ref, summed_ref, vector_ref, total_ref, low_ref, back_ref, sums_ref = refs[size:]
    width = vector_ref.shape[1]
    summed_grad, gain_grad, shift_grad = norm_backward(
        summed_ref[...], vector_ref[3:4, :], grad_ref[...]
    )
    total_ref[...] = summed_grad
    low = to_low(summed_grad)
    low_ref[...] = low
    bias_grad = jnp.sum(to_full(low), axis=0, keepdims=True)
    zero = jnp.zeros((5, width), jnp.float32)
    sums_ref[...] = jnp.concatenate([bias_grad, gain_grad, shift_grad, zero], axis=0)
    back_ref[...] = to_low(matmul_nt(low, read_weight(weight_refs, core[0])))


def out_backward(core, hidden_grad, summed, vectors, group, index):
    rows, width = hidden_grad.shape
    arrays, specs = group.operands(index, core, width, lambda s, c: 0)
    operands = [hidden_grad, summed, vectors]
    out_shape = [
        jax.ShapeDtypeStruct((rows, width), jnp.float32),
        jax.ShapeDtypeStruct((rows, width), jnp.bfloat16),
        jax.ShapeDtypeStruct((rows, width), jnp.bfloat16),
        jax.ShapeDtypeStruct((8, width), jnp.float32),
    ]
    return pl.pallas_call(
        functools.partial(out_back_kernel, size=len(arrays)),
        grid_spec=pltpu.PrefetchScalarGridSpec(
            num_scalar_prefetch=1,
            grid=(1,),
            in_specs=[*specs, *[whole(operand) for operand in operands]],
            out_specs=[whole(shape) for shape in out_shape],
        ),
        out_shape=out_shape,
        name="out_backward",
    )(core.reshape(1), *arrays, *operands)


def attention_back_kernel(*refs, first_head):
    (grad_ref, q_ref, k_ref, v_ref, total_ref, down_ref, across_ref) = refs[:7]
    dq_ref, dk_ref, dv_ref, sums_ref, mask_ref = refs[7:]
    step = pl.program_id(0)

    @pl.when(step == 0)
    def _():
        mask_ref[...] = jnp.where(down_ref[...] == across_ref[...], 0.0, NEGATIVE)

    pair_width = 2 * HEAD_DIM
    scale = HEAD_DIM ** (-0.5)
    lane = lax.broadcasted_iota(jnp.int32, (1, pair_width), 1)
    columns = q_ref.shape[1]
    heads = columns // HEAD_DIM
    for pair in range(heads // 2):
        span = slice(pair_width * pair, pair_width * (pair + 1))
        queries, keys, values = q_ref[:, span], k_ref[:, span], v_ref[:, span]
        grads = grad_ref[:, span]
        scaled = to_full(queries) * scale
        sides = []
        for side in range(2):
            here = (lane < HEAD_DIM) == (side == 0)
            mine = to_low(jnp.where(here, scaled, 0.0))
            my_grads = jnp.where(here, grads, jnp.zeros_like(grads))
            head = first_head + step * heads + 2 * pair + side
            scores = matmul_nt(keys, mine) + mask_ref[...]
            softmax = jnp.exp(scores - total_ref[pl.ds(head, 1), :])
            softmax_grad = matmul_nt(values, my_grads)
            inner = jnp.sum(softmax * softmax_grad, axis=0, keepdims=True)
            score_grad = to_low(softmax * (softmax_grad - inner))
            query_grad = matmul_tn(keys, score_grad)[HEAD_DIM * side : HEAD_DIM * (side + 1)]
            sides.append((query_grad, matmul(score_grad, mine), matmul(to_low(softmax), my_grads)))
        query_grad = to_low(jnp.concatenate([sides[0][0], sides[1][0]], axis=0).T * scale)
        value_grad = to_low(sides[0][2] + sides[1][2])
        dq_ref[:, span] = query_grad
        dk_ref[:, span] = to_low(sides[0][1] + sides[1][1])
        dv_ref[:, span] = value_grad
        sums_ref[0:1, span] = jnp.sum(to_full(query_grad), axis=0, keepdims=True)
        sums_ref[1:2, span] = jnp.sum(to_full(value_grad), axis=0, keepdims=True)


def attention_backward(context_grad, queries, keys, values, score_total, segments, start, columns):
    rows = context_grad.shape[0]
    size = 2 * HEAD_DIM
    down, across = segments[:, None], segments[None, :]
    block = pl.BlockSpec((rows, size), lambda s: (0, start // size + s))
    out_block = pl.BlockSpec((rows, size), lambda s: (0, s))
    return pl.pallas_call(
        functools.partial(attention_back_kernel, first_head=start // HEAD_DIM),
        grid=(columns // size,),
        in_specs=[*[block] * 4, whole(score_total), whole(down), whole(across)],
        out_specs=[*[out_block] * 3, pl.BlockSpec((8, size), lambda s: (0, s))],
        out_shape=[
            *[jax.ShapeDtypeStruct((rows, columns), jnp.bfloat16)] * 3,
            jax.ShapeDtypeStruct((8, columns), jnp.float32),
        ],
        scratch_shapes=[pltpu.VMEM((rows, rows), jnp.float32)],
        compiler_params=pltpu.CompilerParams(dimension_semantics=("arbitrary",)),
        name="attention_backward",
    )(context_grad, queries, keys, values, score_total, down, across)


def joined_sums(bias_sums, out_sums, feed_sums, head_sums, steps):
    return jnp.concatenate(
        [
            jnp.concatenate([part[:2] for part in bias_sums], axis=1),
            out_sums[:3],
            feed_sums[: 3 + steps],
            head_sums[: 8 - steps],
        ],
        axis=0,
    )


def last_grads_kernel(place, *refs, parts, share, steps):
    tokens_ref, context_ref, branch_ref, out_sums_ref, feed_sums_ref, head_sums_ref, *rest = refs
    mixed_refs, rest = rest[: 3 * parts], rest[3 * parts :]
    bias_refs, outs = rest[:parts], rest[parts:]
    turned = tokens_ref[...].T
    for which in range(3):
        for part in range(parts):
            mixed = mixed_refs[3 * part + which][...]
            columns = mixed.shape[1]
            grad = to_low(matmul(turned, mixed))
            if share:
                rows = slice(share * which, share * (which + 1))
                store_blocks(outs, grad, place, share, rows, column=columns * part)
            else:
                outs[which][:, columns * part : columns * (part + 1)] = grad
    grad = to_low(matmul_tn(context_ref[...], branch_ref[...]))
    if share:
        store_blocks(outs, grad, place, share, slice(3 * share, 4 * share))
        small = to_low(
            joined_sums(
                [ref[...] for ref in bias_refs],
                out_sums_ref[...],
                feed_sums_ref[...],
                head_sums_ref[...],
                steps,
            )
        )
        half = small.shape[1] // 2
        for index, out_ref in enumerate(outs):
            part = small[:, half * (index % 2) : half * (index % 2 + 1)]
            out_ref[:, 4 * share :, :] = jnp.broadcast_to(
                part[None], (out_ref.shape[0], *part.shape)
            )
    else:
        outs[3][...] = grad


def last_grads(place, count, tokens, context, branch_grad, sums, steps, mixed):
    width = tokens.shape[1]
    share, chips = width // count, count // 2
    aligned = share % 8 == 0
    parts = len(mixed)
    biases = [part[3] for part in mixed]
    mixed = [part[:3] for part in mixed]
    operands = [tokens, context, branch_grad, *sums, *[m for part in mixed for m in part], *biases]
    small = joined_sums(biases, *sums, steps)
    if aligned:
        rows = 4 * share + small.shape[0]
        out_shape = [jax.ShapeDtypeStruct((chips, rows, width // 2), jnp.bfloat16)] * 4
    else:
        out_shape = [jax.ShapeDtypeStruct((width, width), jnp.bfloat16)] * 4
    outs = pl.pallas_call(
        functools.partial(
            last_grads_kernel, parts=parts, share=share if aligned else 0, steps=steps
        ),
        grid_spec=pltpu.PrefetchScalarGridSpec(
            num_scalar_prefetch=1,
            grid=(1,),
            in_specs=[whole(operand) for operand in operands],
            out_specs=[whole(shape) for shape in out_shape],
        ),
        out_shape=out_shape,
        name="last_grads",
    )(place, *operands)
    if not aligned:
        both = jnp.broadcast_to(to_low(small)[None], (count, *small.shape))
        return arranged([*outs, both.reshape(-1, width)], place)
    return outs[:2], outs[2:]


def tokens_back_kernel(core, *refs, sizes, parts):
    ends = [sum(sizes[:k]) for k in range(4)]
    weights = [refs[ends[k] : ends[k + 1]] for k in range(3)]
    summed_ref, *mixed_refs, out_ref = refs[ends[3] :]
    total = summed_ref[...]
    for which in range(3):
        weight = read_weight(weights[which], core[0])
        for part in range(parts):
            mixed = mixed_refs[3 * part + which][...]
            columns = mixed.shape[1]
            total += matmul_nt(mixed, weight[:, columns * part : columns * (part + 1)])
    out_ref[...] = total


def tokens_backward(core, summed_grad, mixed, weights):
    width = summed_grad.shape[1]
    arrays, specs, sizes = [], [], []
    for group, index in weights:
        some, their = group.operands(index, core, width, lambda s, c: 0)
        arrays, specs, sizes = arrays + some, specs + their, sizes + [len(some)]
    operands = [summed_grad, *[matrix for part in mixed for matrix in part]]
    return pl.pallas_call(
        functools.partial(tokens_back_kernel, sizes=sizes, parts=len(mixed)),
        grid_spec=pltpu.PrefetchScalarGridSpec(
            num_scalar_prefetch=1,
            grid=(1,),
            in_specs=[*specs, *[whole(operand) for operand in operands]],
            out_specs=whole(summed_grad),
        ),
        out_shape=jax.ShapeDtypeStruct(summed_grad.shape, jnp.float32),
        name="tokens_backward",
    )(core.reshape(1), *arrays, *operands)


def take_kernel(index, whole_ref, *out_refs, plan):
    width = whole_ref.shape[1]
    for out_ref, (first_row, share) in zip(out_refs, plan):
        spot = index[0] * share
        row, place = first_row + spot // width, spot % width
        line = jnp.broadcast_to(whole_ref[pl.ds(row, 1), :], (8, width))
        moved = pltpu.roll(line, lax.rem(width - place, width), 1)
        out_ref[...] = moved[:1, :share]


def take_shares(device, values, first_rows, shares):
    shapes = [jax.ShapeDtypeStruct((1, share), jnp.float32) for share in shares]
    lines = pl.pallas_call(
        functools.partial(take_kernel, plan=list(zip(first_rows, shares))),
        grid_spec=pltpu.PrefetchScalarGridSpec(
            num_scalar_prefetch=1,
            grid=(1,),
            in_specs=[whole(values)],
            out_specs=[whole(shape) for shape in shapes],
        ),
        out_shape=shapes,
        name="take_shares",
    )(device.reshape(1), values)
    return [line[0] for line in lines]


def take(value, axis, index):
    return lax.dynamic_index_in_dim(value, index, axis, keepdims=False)


def add_low(first, second):
    return to_low(to_full(first) + to_full(second))


def halve(value, axis, stride):
    chips = lax.axis_size("dp")
    bit = (lax.axis_index("dp") // stride) % 2
    pairs = [(chip, chip ^ stride) for chip in range(chips)]
    arrived = lax.ppermute(take(value, axis, 1 - bit), "dp", pairs)
    return add_low(take(value, axis, bit), arrived)


def core_swap(away):
    return lax.ppermute(away, "fsdp", [(0, 1), (1, 0)])


def along(sent, stride):
    chips = lax.axis_size("dp")
    return lax.ppermute(sent, "dp", [(chip, chip ^ stride) for chip in range(chips)])


def total_of(addends):
    total = to_full(addends[0])
    for addend in addends[1:]:
        total = total + to_full(addend)
    return total


def my_place():
    chip = lax.axis_index("dp")
    return jnp.stack([lax.axis_index("fsdp"), chip % 2, (chip // 2) % 2, chip // 4])


def chip_at(index, place, levels, first_axis):
    outer, level = index // levels, index % levels
    bits = (outer // 2, outer % 2) if first_axis == 0 else (outer % 2, outer // 2)
    return ((place[3] ^ level) * 2 + (place[2] ^ bits[1])) * 2 + (place[1] ^ bits[0])


def index_of(chip, place, levels, first_axis):
    bits = ((chip % 2) ^ place[1], ((chip // 2) % 2) ^ place[2])
    outer = 2 * bits[first_axis] + bits[1 - first_axis]
    return outer * levels + ((chip // 4) ^ place[3])


class ChipSum:
    def __init__(self, away, kept):
        self.sides = [[part] for part in kept]
        self.strides = [[1, 2], [2, 1]]
        self.arrived = [core_swap(part) for part in away]

    def add(self, arrived):
        for side, part in zip(self.sides, arrived):
            side.append(part)

    def sends(self):
        sent = [to_low(total_of([a[a.shape[0] // 2 :] for a in side])) for side in self.sides]
        self.sides = [[a[: a.shape[0] // 2] for a in side] for side in self.sides]
        return sent

    def start(self, sent):
        self.arrived = [along(part, strides.pop(0)) for part, strides in zip(sent, self.strides)]

    def level_block(self, level):
        return jnp.concatenate(
            [total_of([a[level] for a in side]) for side in self.sides], axis=-1
        )

    def level_sends(self):
        while self.sides[0][0].shape[0] > 4:
            stride = 4 * (self.sides[0][0].shape[0] // 2)
            sent = self.sends()
            self.add([along(part, stride) for part in sent])
        levels = self.sides[0][0].shape[0]
        return [to_low(self.level_block(level)) for level in range(1, levels)]

    def start_levels(self, sent):
        self.arrived = [along(part, 4 * (level + 1)) for level, part in enumerate(sent)]

    def result(self, arrived):
        return total_of([self.level_block(0), *arrived])


def arranged(matrices, place):
    chips = lax.axis_size("dp")
    value = jnp.concatenate(
        [matrix.reshape(chips, 2, -1, matrix.shape[-1]) for matrix in matrices], axis=2
    )
    half = value.shape[-1] // 2
    sides = []
    for core in (1 - place[0], place[0]):
        mine = take(value, 1, core)
        sides.append(
            [
                jnp.take(
                    mine[..., axis * half : (axis + 1) * half],
                    chip_at(jnp.arange(chips), place, chips // 4, axis),
                    axis=0,
                )
                for axis in range(2)
            ]
        )
    return sides


def store_blocks(outs, value, place, share, rows, first_chip=0, column=0):
    columns = value.shape[-1]
    split = value.reshape(-1, 2, share, columns)
    kept, away = in_order(split[:, 0], split[:, 1], place[0])
    levels = outs[0].shape[0] // 4
    width = outs[0].shape[-1]
    for chip in range(split.shape[0]):
        for which, half in enumerate((away, kept)):
            for axis in range(2):
                low, high = max(column, axis * width), min(column + columns, (axis + 1) * width)
                if low >= high:
                    continue
                spot = index_of(first_chip + chip, place, levels, axis)
                outs[2 * which + axis][
                    pl.ds(spot, 1), rows, low - axis * width : high - axis * width
                ] = half[chip : chip + 1, :, low - column : high - column]


def tie(value, *others):
    return lax.optimization_barrier((value, *others))


def window_base(start, total, window):
    return pl.multiple_of(jnp.minimum((start // 16) * 16, total - window), 16)


def compact_kernel(place, places, counts, indices, mine_ref, other_ref, *refs, window, levels):
    step = pl.program_id(0)
    *before, out_ref = refs

    @pl.when(step == 0)
    def _():
        out_ref[...] = before[0][...] if before else jnp.zeros_like(out_ref)

    _, batch, slots, half = mine_ref.shape
    total = out_ref.shape[0]
    for which, ref in enumerate((mine_ref, other_ref)):
        core = place[0] if which == 0 else 1 - place[0]
        for axis in range(2):
            for lane in range(batch):
                index = indices[step * batch + lane]
                source = 2 * chip_at(index, place, levels, axis) + core
                start = places[source]
                base = window_base(start, total, window)
                row = lax.broadcasted_iota(jnp.int32, (window, slots), 0) + (base - start)
                column = lax.broadcasted_iota(jnp.int32, (window, slots), 1)
                chosen = jnp.where((row == column) & (column < counts[source]), 1.0, 0.0)
                moved = matmul(to_low(chosen), ref[axis, lane])
                out_ref[pl.ds(base, window), half * axis : half * (axis + 1)] += to_low(moved)


def compact(place, places, counts, mine, other, indices, total, before=()):
    _, blocks, slots, half = mine.shape
    levels = lax.axis_size("dp") // 4
    batch = blocks // 2 if blocks <= 16 else 2
    block = pl.BlockSpec((2, batch, slots, half), lambda i, *_: (0, i, 0, 0))
    return pl.pallas_call(
        functools.partial(compact_kernel, window=slots + 16, levels=levels),
        grid_spec=pltpu.PrefetchScalarGridSpec(
            num_scalar_prefetch=4,
            grid=(blocks // batch,),
            in_specs=[block, block, *[whole(rows) for rows in before]],
            out_specs=pl.BlockSpec((total, 2 * half), lambda i, *_: (0, 0)),
        ),
        out_shape=jax.ShapeDtypeStruct((total, 2 * half), jnp.bfloat16),
        compiler_params=pltpu.CompilerParams(dimension_semantics=("arbitrary",)),
        name="compact_rows",
    )(place, places, counts, jnp.array(indices, jnp.int32), mine, other, *before)


def compact_labels_kernel(places, counts, lines_ref, out_ref):
    out_ref[...] = jnp.zeros_like(out_ref)
    sources, slots = lines_ref.shape
    total = out_ref.shape[1]
    wide = 2 * slots
    lane = lax.broadcasted_iota(jnp.int32, (8, wide), 1)

    def place_one(source, carry):
        start = places[source]
        base = pl.multiple_of(jnp.minimum(start // slots * slots, total - wide), slots)
        shift = start - base
        line = jnp.broadcast_to(to_full(lines_ref[pl.ds(source, 1), :]), (8, slots))
        line = jnp.concatenate([line, jnp.zeros_like(line)], axis=1)
        moved = pltpu.roll(line, lax.rem(shift, wide), 1)
        here = (lane >= shift) & (lane < shift + counts[source])
        span = pl.ds(base, wide)
        out_ref[:, span] = jnp.where(here, moved, out_ref[:, span])
        return carry

    lax.fori_loop(0, sources, place_one, 0)


def compact_labels(places, counts, lines, total):
    out = pl.pallas_call(
        compact_labels_kernel,
        grid_spec=pltpu.PrefetchScalarGridSpec(
            num_scalar_prefetch=2,
            grid=(1,),
            in_specs=[whole(lines)],
            out_specs=pl.BlockSpec((8, total), lambda *_: (0, 0)),
        ),
        out_shape=jax.ShapeDtypeStruct((8, total), jnp.float32),
        name="compact_labels",
    )(places, counts, lines)
    return out[0].astype(jnp.int32)


def block_order():
    levels = lax.axis_size("dp") // 4
    near = [*range(levels), *range(2 * levels, 3 * levels), levels, 3 * levels]
    return near, [k for k in range(4 * levels) if k not in near]


def gather_blocks(value, beside, given):
    chips = lax.axis_size("dp")
    levels = chips // 4
    half = value.shape[-1] // 2
    if levels <= 4:
        others = jnp.stack([along(value, 4 * level) for level in range(1, levels)])
    else:
        others = value[None]
        while others.shape[0] < levels:
            others = jnp.concatenate([others, along(others, 4 * others.shape[0])])
        others = others[1:]
    own = [value[:, :half], value[:, half:]]
    strides = [(1, 2), (2, 1)]
    near = [along(part, first) for part, (first, _) in zip(own, strides)]
    far_sent = [jnp.stack([part, got]) for part, got in zip(own, near)]
    others = tie(others, *far_sent)[0]
    far = [along(sent, second) for sent, (_, second) in zip(far_sent, strides)]
    rest = [others[..., :half], others[..., half:]]
    near_rest = [along(part, first) for part, (first, _) in zip(rest, strides)]
    given, *near_rest = tie(given, *near_rest)
    far_rest = [
        along(jnp.concatenate([part, got]), second)
        for part, got, (_, second) in zip(rest, near_rest, strides)
    ]
    early = jnp.stack(
        [
            jnp.concatenate([own[k][None], rest[k], near[k][None], near_rest[k], far[k]])
            for k in range(2)
        ]
    )
    results = beside(early, core_swap(early), given)
    tied = tie(*far_rest, *results)
    late = jnp.stack(tied[:2])
    return late, core_swap(late), tied[2:]


def spread_kernel(place, places, counts, rows_ref, *out_refs, window):
    step = pl.program_id(0)
    total = rows_ref.shape[0]
    batch, slots, half = out_refs[0].shape
    levels = pl.num_programs(0) * batch // 4
    for which in range(2):
        core = 1 - place[0] if which == 0 else place[0]
        for axis in range(2):
            for lane in range(batch):
                chip = chip_at(step * batch + lane, place, levels, axis)
                source = 2 * chip + core
                start = places[source]
                base = window_base(start, total, window)
                row = lax.broadcasted_iota(jnp.int32, (slots, window), 0)
                column = lax.broadcasted_iota(jnp.int32, (slots, window), 1) + (base - start)
                chosen = jnp.where((row == column) & (row < counts[source]), 1.0, 0.0)
                moved = matmul(
                    to_low(chosen), rows_ref[pl.ds(base, window), half * axis : half * (axis + 1)]
                )
                out_refs[2 * which + axis][lane] = to_low(moved)


def spread(place, places, counts, rows, slots):
    chips = places.shape[0] // 2
    total, width = rows.shape
    batch = 8
    block = pl.BlockSpec((batch, slots, width // 2), lambda i, *_: (i, 0, 0))
    shape = jax.ShapeDtypeStruct((chips, slots, width // 2), jnp.bfloat16)
    outs = pl.pallas_call(
        functools.partial(spread_kernel, window=slots + 16),
        grid_spec=pltpu.PrefetchScalarGridSpec(
            num_scalar_prefetch=3,
            grid=(chips // batch,),
            in_specs=[
                pl.BlockSpec((total, width), lambda i, *_: (0, 0), pipeline_mode=pl.Buffered(1))
            ],
            out_specs=[block] * 4,
        ),
        out_shape=[shape] * 4,
        compiler_params=pltpu.CompilerParams(dimension_semantics=("arbitrary",)),
        name="spread_rows",
    )(place, places, counts, rows)
    return outs[:2], outs[2:]


def per_device(
    tokens,
    segments,
    mask_flags,
    targets,
    cotangent,
    qkv_weight,
    attn_bias,
    out_weight,
    out_bias,
    attn_gain,
    attn_shift,
    up_weight,
    up_bias,
    down_weight,
    down_bias,
    ffn_gain,
    ffn_shift,
    dense_weight,
    dense_bias,
    head_gain,
    head_shift,
    decoder,
    vocab_bias,
):
    count = lax.axis_size(AXES)
    width = tokens.shape[1]
    core = lax.axis_index("fsdp")
    device = lax.axis_index(AXES)
    here = my_place()
    blocks = qkv_weight.shape[1] // width
    steps = up_weight.shape[1] // width
    share, up_share, down_share = out_weight.shape[0], up_weight.shape[0], down_weight.shape[0]
    label_place = up_share * steps + down_share + share
    later_packed = pack_later(
        [
            (up_weight, [up_share * k for k in range(steps)]),
            (down_weight, [up_share * steps]),
            (dense_weight, [up_share * steps + down_share]),
        ],
        mask_flags,
        targets,
    )
    later_gathered = lax.all_gather(later_packed, AXES, axis=0)
    later = Weights([later_gathered], [*[up_share] * steps, down_share, share])
    small = (
        attn_bias,
        out_bias,
        attn_gain,
        attn_shift,
        down_bias,
        ffn_gain,
        ffn_shift,
        up_bias,
        dense_bias,
        head_gain,
        head_shift,
    )
    small_rows = (0, 2, 3, 4, 5, 6, 7, 8, 12, 13, 14)
    placed = place_shares(device, small, small_rows, 16, width)
    half = 2 * share + 8
    first_packed = pack_rows(
        [
            (qkv_weight, [0, share, half]),
            (placed[:8], [2 * share]),
            (out_weight, [half + share]),
            (placed[8:], [half + 2 * share]),
        ]
    )
    upper, lower = gather_pair(first_packed, half)
    first_group, second_group = (Weights(list(pair), [share, share, 8]) for pair in (upper, lower))
    vectors, more_vectors = (
        sum(jnp.sum(to_full(array[:, 2 * share :]), axis=0) for array in pair)
        for pair in (upper, lower)
    )
    queries, keys_low, values_low, context, score_total, summed1, hidden = attention_forward(
        core,
        tokens,
        segments,
        [(first_group, 0), (first_group, 1), (second_group, 0), (second_group, 1)],
        vectors,
    )
    active, slope, summed2, output = ffn_forward(hidden, later, more_vectors[:4], vectors)
    head_gain_full, head_shift_full = more_vectors[5], more_vectors[6]
    mask_rank = jnp.cumsum(mask_flags) - 1
    slot_place = jnp.where(mask_flags > 0, mask_rank, -1)
    picker_low = (jnp.arange(MAXM)[:, None] == slot_place[None, :]).astype(jnp.bfloat16)
    own_rows, dense, normed_low = head_forward(picker_low, output, later, steps + 1, more_vectors)
    _, tail_back = jax.vjp(head_tail, dense, head_gain_full, head_shift_full)
    chips = count // 2
    group = MASK_DEV * chips
    total = 2 * group
    gathered_late, normed_low = tie(later_gathered, normed_low)
    label_parts = gathered_late[:, label_place : label_place + 2, :MAXM].astype(jnp.int32)
    label_lines = label_parts[:, 0] * 256 + label_parts[:, 1] - 1
    counts = jnp.sum((label_lines >= 0).astype(jnp.int32), axis=1)
    by_core = counts.reshape(chips, 2)
    earlier = jnp.arange(chips)[:, None] < jnp.arange(chips)[None, :]
    places = jnp.sum(jnp.where(earlier[:, :, None], by_core[:, None, :], 0), axis=0)
    places = (places + jnp.arange(2)[None, :] * group).reshape(count)
    all_labels = compact_labels(places, counts, label_lines, total)
    slice_index = lax.axis_index(AXES)
    vocab_rows = decoder.shape[0]
    local_label = all_labels - slice_index * vocab_rows
    label_hit = jnp.arange(vocab_rows)[None, :] == local_label[:, None]

    early_order, late_order = block_order()

    def beside_last(mine, other, chosen):
        hit = jnp.arange(vocab_rows)[None, :] == chosen[:, None]
        pulled = to_low(matmul(hit.astype(jnp.bfloat16), decoder))
        return compact(here, places, counts, mine, other, early_order, total), pulled

    mine, other, (early_rows, label_pull) = gather_blocks(normed_low, beside_last, local_label)
    late = (here, places, counts, mine, other, late_order, total)
    small_total = total <= 4096
    all_rows = compact(*late, (early_rows,)) if small_total else early_rows + compact(*late)
    logits = matmul_nt(all_rows, decoder) + to_full(vocab_bias)
    row_peak = jnp.max(logits, axis=1)
    exp_sums = jnp.sum(jnp.exp(logits - row_peak[:, None]), axis=1)
    label_sum = jnp.sum(jnp.where(label_hit, logits, 0.0))
    local_total = (row_peak + jnp.log(exp_sums)).reshape(-1, 128)
    lines = local_total.shape[0]
    merged = jnp.concatenate(
        [local_total, jnp.pad(label_sum[None, None], ((0, 7), (0, 127)))], axis=0
    )
    is_total = jnp.arange(lines + 8)[:, None] < lines
    middle = total // 2
    pulls = []
    rounds = [[1], [2, 4, 6]]
    rounds += [[8, 16, 24]] if count == 32 else [[8 << k] for k in range((count // 8).bit_length() - 1)]
    for distances in rounds:
        arrived = [
            lax.ppermute(merged, AXES, [(place, place ^ far) for place in range(count)])
            for far in distances
        ]
        if len(pulls) < 2:
            rows = slice(middle * len(pulls), middle * (len(pulls) + 1))
            pull = matmul(to_low(jnp.exp(logits[rows] - row_peak[rows, None])), decoder)
            *arrived, pull = tie(*arrived, pull)
            pulls.append(pull)
        every = [merged, *arrived]
        peak = functools.reduce(jnp.maximum, every)
        both = peak + jnp.log(sum(jnp.exp(part - peak) for part in every))
        merged = jnp.where(is_total, both, sum(every))
    log_total = merged[:lines].reshape(total)
    mean_loss = (jnp.sum(log_total) - merged[lines, 0]) / total
    scale = jnp.exp(row_peak - log_total)[:, None]
    rows_part = jnp.concatenate(
        [
            to_low(pull * scale[rows] - to_full(label_pull[rows]))
            for pull, rows in zip(pulls, (slice(0, middle), slice(middle, total)))
        ]
    )
    rows_sum = ChipSum(*spread(here, places, counts, rows_part, MAXM))
    rows_sum.add(rows_sum.arrived)
    rows_sum.start(rows_sum.sends())
    logit_grad = to_low(jnp.exp(logits - log_total[:, None]) - label_hit.astype(jnp.float32))
    vocab_bias_grad = jnp.sum(to_full(logit_grad), axis=0)
    logit_grad, vocab_bias_grad, *arrived = tie(logit_grad, vocab_bias_grad, *rows_sum.arrived)
    rows_sum.add(arrived)
    rows_sum.start(rows_sum.sends())
    decoder_grad = matmul_tn(logit_grad, all_rows)
    decoder_grad, *arrived = tie(decoder_grad, *rows_sum.arrived)
    rows_sum.add(arrived)
    rows_sum.start_levels(rows_sum.level_sends())
    normed_grad = rows_sum.result(rows_sum.arrived)
    dense_grad, head_gain_grad, head_shift_grad = tail_back(normed_grad)
    dense_grad_low = to_low(dense_grad)
    dense_bias_grad = jnp.sum(to_full(dense_grad_low), axis=0)
    hidden_grad, feed_sums, *feed_grads = feed_backward(
        here,
        count,
        cotangent,
        picker_low,
        summed2,
        vectors,
        own_rows,
        dense_grad_low,
        hidden,
        active,
        slope,
        later,
    )
    first = ChipSum(*feed_grads)
    summed1_grad, branch1_grad, context_grad, out_sums = out_backward(
        core, hidden_grad, summed1, vectors, second_group, 1
    )
    context_grad, *arrived = tie(context_grad, *first.arrived)
    first.add(arrived)
    context_grad, *sent = tie(context_grad, *first.sends())
    first.start(sent)
    saved = (queries, keys_low, values_low, score_total, segments)
    middle = width // 2
    mixed = [list(attention_backward(context_grad, *saved, 0, middle))]
    mixed[0][0], context_grad = tie(mixed[0][0], context_grad)
    mixed.append(list(attention_backward(context_grad, *saved, middle, width - middle)))
    head_sums = jnp.stack(
        [dense_bias_grad, head_gain_grad, head_shift_grad, *[jnp.zeros((width,))] * 5]
    )
    away, kept = last_grads(
        here, count, tokens, context, branch1_grad, (out_sums, feed_sums, head_sums), steps, mixed
    )
    mixed = [part[:3] for part in mixed]
    second = ChipSum(away, kept)
    mixed[0][0], _, *arrived = tie(mixed[0][0], away[0], *first.arrived)
    first.add(arrived)
    mixed[0][0], *sent = tie(mixed[0][0], *first.sends())
    first.start(sent)
    mixed[0][0], *arrived = tie(mixed[0][0], *second.arrived)
    second.add(arrived)
    mixed[0][0], *sent = tie(mixed[0][0], *second.sends())
    second.start(sent)
    tokens_grad = tokens_backward(
        core, summed1_grad, mixed, [(first_group, 0), (first_group, 1), (second_group, 0)]
    )
    first.add(first.arrived)
    first.start_levels(first.level_sends())
    second.add(second.arrived)
    second.start(second.sends())
    second.add(second.arrived)
    sent = second.level_sends()
    first.arrived[0] = tie(first.arrived[0], *sent)[0]
    second.start_levels(sent)
    first, second = first.result(first.arrived), second.result(second.arrived)
    up_pieces = [first[share * k : share * (k + 1)] for k in range(steps)]
    down_piece = first[up_share * steps : up_share * steps + down_share]
    dense_piece = first[up_share * steps + down_share :]
    qkv_pieces = [second[share * k : share * (k + 1)] for k in range(blocks)]
    out_piece = second[share * blocks : share * (blocks + 1)]
    small_pieces = take_shares(
        device, second[share * (blocks + 1) :], small_rows, [vector.shape[0] for vector in small]
    )
    return (
        output,
        mean_loss,
        tokens_grad,
        jnp.concatenate(qkv_pieces, axis=1),
        small_pieces[0],
        out_piece,
        *small_pieces[1:4],
        jnp.concatenate(up_pieces, axis=1),
        small_pieces[7],
        down_piece,
        *small_pieces[4:7],
        dense_piece,
        *small_pieces[8:],
        decoder_grad,
        vocab_bias_grad,
    )


def solution(mesh):
    matrix_spec = P(AXES, None)
    vector_spec = P(AXES)
    m, v = matrix_spec, vector_spec
    return jax.shard_map(
        per_device,
        mesh=mesh,
        in_specs=(m, v, v, v, m, m, v, m, v, v, v, m, v, m, v, v, v, m, v, v, v, m, v),
        out_specs=(m, P(), m, m, v, m, v, v, v, m, v, m, v, v, v, m, v, v, v, m, v),
        check_vma=False,
    )
```
